256 devices in a mesh: comp: 2 (over x_hi), lat: 4 (over y), lon: 32 (over z, x_lo, core).
Axes of the slice: x: 4 (x_hi: 2, x_lo: 2; x = x_hi * 2 + x_lo), y: 4, z: 8, core: 2. Of those that a mesh axis runs over, the one named last changes fastest.
Arguments:
- state: bfloat16 [2, 80, 8, 8192], P('comp', None, 'lat', 'lon'), may hold values from -6 to 6
- direction: bfloat16 [2, 80, 8, 8192], P('comp', None, 'lat', 'lon'), may hold values from -6 to 6
- air_first: bfloat16 [9, 512, 80], replicated, may hold values from -0.21875 to 0.21875
- air_bias: float32 [512], replicated, may hold values from -4 to 4
- air_second: bfloat16 [9, 80, 512], replicated, may hold values from -0.09375 to 0.09375
- air_flux: bfloat16 [2, 80], replicated, may hold values from -1.25 to 1.25
- aloft_reaction_to_seawarmth: float32 [80], replicated, may hold values from -4 to 4
- sea_first: bfloat16 [9, 256, 40], replicated, may hold values from -0.3125 to 0.3125
- sea_bias: float32 [256], replicated, may hold values from -4 to 4
- sea_second: bfloat16 [9, 40, 256], replicated, may hold values from -0.125 to 0.125
- sea_forcing: bfloat16 [40, 2], replicated, may hold values from -4 to 4
- regrid_index: int32 [2, 8, 8, 8192], P('comp', None, 'lat', 'lon'), may hold values from 0 to 2047, as said below
- regrid_weight: int32 [2, 8, 8, 8192], P('comp', None, 'lat', 'lon'), may hold values from 1 to 255
- land_mask: int32 [2, 8, 8192], P(None, 'lat', 'lon'), may hold values 0 or 1
Outputs:
- image: bfloat16 [2, 80, 8, 8192], P('comp', None, 'lat', 'lon')
- product: bfloat16 [2, 80, 8, 8192], P('comp', None, 'lat', 'lon')
The draws below stay inside these ranges and needn't reach their ends.
Inputs may be any that keep to these rules, and one draw needn't show every extreme that they name: `regrid_index`: in block 0, entries number cells of the fine window of the tile that holds the cell (below 2048); in block 1 they number cells of its coarse window (below 1024); the sources of a cell lie near it.
All inputs are finite; a program needn't handle non-finite values. No bound on the sum of `land_mask` on one device may be relied on, other than what follows from the above.
Results may differ from the reference program's by a relative error of at most 0.0064.
Values may be sent and summed in bfloat16 or wider, within the bound.
No kernel may reach another device: no remote copies, remote signals or barrier semaphores. Data moves between devices by JAX's collectives and lax.ppermute only.
A program may use at most 64 MiB of HBM per device.

```python
import jax
import jax.numpy as jnp
from jax import lax

CH_ATM = 80
HID_ATM = 512
CH_OCN = 40
HID_OCN = 256
FLUX = 2
SLOTS = 8
ROWS_DEV = 2
COLS_DEV = 256
NLAT = 8
NLON = 8192
N_LAT = 4
N_LON = 32


def draw_regrid_index(key, part):
    rows = ROWS_DEV
    columns = COLS_DEV
    first_key, second_key = jax.random.split(jax.random.fold_in(key, 17))
    local_row = (lax.iota(jnp.int32, NLAT) % rows)[:, None]
    local_col = (lax.iota(jnp.int32, NLON) % columns)[None, :]
    air_offset = jax.random.randint(first_key, (NLAT, NLON), 1, columns - 1)
    air_offset = jnp.where(local_col == 0, 1, jnp.where(local_col == columns - 1, columns - 2, air_offset))
    sea_offset = jax.random.randint(second_key, (NLAT, NLON), 1, columns + 1)
    sea_offset = jnp.where(local_col == 0, 1, jnp.where(local_col == columns - 1, columns, sea_offset))
    slot = lax.iota(jnp.int32, 8)[:, None, None]
    air_row = 2 * local_row + slot // 4
    air_col = local_col + air_offset - 1 + slot % 4
    aloft_lookup_position = air_row * 2 * columns + air_col
    fine_row = slot // 4 * rows + local_row
    sea_row = jnp.minimum(fine_row // 2 + slot % 4 // 2, rows - 1)
    sea_col = local_col + sea_offset - 1 + slot % 2
    sea_index = sea_row * 2 * columns + sea_col
    return jnp.stack([aloft_lookup_position, sea_index]).astype(jnp.int32)


def plant(entries, stream_key, low, high):
    longest = entries.shape.index(max(entries.shape))
    spots = []
    for shift in (0, 1):
        where = [jax.random.randint(jax.random.fold_in(stream_key, axis), (), 0, length) for axis, length in enumerate(entries.shape)]
        where[longest] = (where[longest] + shift) % entries.shape[longest]
        spots.append(tuple(where))
    return entries.at[spots[0]].set(low).at[spots[1]].set(high)


def block_levels(rng, dims, cuts, low, top_value):
    gain, own = 1.0, jax.random.fold_in(rng, 6)
    for axis_at, blocks in cuts:
        draws = jnp.exp(jax.random.uniform(jax.random.fold_in(own, axis_at), (blocks,), jnp.float32, low / len(cuts), top_value / len(cuts)))
        gain = gain * jnp.repeat(draws, dims[axis_at] // blocks).reshape([-1 if axis == axis_at else 1 for axis in range(len(dims))])
    return gain


def bell_draw(stream_key, dims, scale, reach, cuts=(), kind=jnp.bfloat16):
    array = scale * jax.random.normal(stream_key, dims, jnp.float32)
    if cuts:
        array = array * block_levels(stream_key, dims, cuts, -0.22, 0.18)
    return jnp.clip(array, -reach, reach).astype(kind)


def setup_inputs(seed: int = 0) -> dict:
    splits = jax.random.split(jax.random.key(seed), 15)
    return {
        "state": bell_draw(splits[0], (2, CH_ATM, NLAT, NLON), 1.0, 6.0, ((0, 2), (2, 4), (3, 32))),
        "direction": bell_draw(splits[1], (2, CH_ATM, NLAT, NLON), 1.0, 6.0, ((0, 2), (2, 4), (3, 32))),
        "air_first": bell_draw(splits[2], (9, HID_ATM, CH_ATM), (9 * CH_ATM) ** -0.5, 0.21875),
        "air_bias": bell_draw(splits[3], (HID_ATM,), 1.0, 4.0, (), jnp.float32),
        "air_second": bell_draw(splits[4], (9, CH_ATM, HID_ATM), (9 * HID_ATM) ** -0.5, 0.09375),
        "air_flux": bell_draw(splits[5], (FLUX, CH_ATM), (CH_ATM // 4) ** -0.5, 1.25),
        "aloft_reaction_to_seawarmth": bell_draw(splits[6], (CH_ATM,), 1.0, 4.0, (), jnp.float32),
        "sea_first": bell_draw(splits[7], (9, HID_OCN, CH_OCN), (9 * CH_OCN) ** -0.5, 0.3125),
        "sea_bias": bell_draw(splits[8], (HID_OCN,), 1.0, 4.0, (), jnp.float32),
        "sea_second": bell_draw(splits[9], (9, CH_OCN, HID_OCN), (9 * HID_OCN) ** -0.5, 0.125),
        "sea_forcing": bell_draw(splits[10], (CH_OCN, FLUX), FLUX ** -0.5, 4.0),
        "regrid_index": draw_regrid_index(jax.random.fold_in(splits[14], 71), 0),
        "regrid_weight": plant(jax.random.randint(splits[12], (2, SLOTS, NLAT, NLON), 1, 256), jax.random.fold_in(splits[12], 1), 1, 255).astype(jnp.int32),
        "land_mask": plant((jax.random.randint(splits[13], (2, NLAT, NLON), 0, 4) < 3).astype(jnp.int32), jax.random.fold_in(splits[13], 1), 0, 1),
    }


HIGH = lax.Precision.HIGHEST


def pad_grid(field):
    field = jnp.pad(field, ((0, 0), (1, 1), (0, 0)))
    return jnp.concatenate([field[:, :, -1:], field, field[:, :, :1]], axis=2)


def conv_taps(weight, field):
    padded = pad_grid(field.astype(jnp.float32))
    height = field.shape[1]
    length = field.shape[2]
    summed = jnp.zeros((weight.shape[1], height, length), jnp.float32)
    for tap in range(9):
        down_off, across_off = divmod(tap, 3)
        part = padded[:, down_off:down_off + height, across_off:across_off + length]
        summed = summed + jnp.einsum("oc,chw->ohw", weight[tap].astype(jnp.float32), part)
    return summed


def conv_back(weight, field):
    padded = pad_grid(field.astype(jnp.float32))
    height = field.shape[1]
    length = field.shape[2]
    summed = jnp.zeros((weight.shape[2], height, length), jnp.float32)
    for tap in range(9):
        down_off, across_off = divmod(tap, 3)
        part = padded[:, 2 - down_off:2 - down_off + height, 2 - across_off:2 - across_off + length]
        summed = summed + jnp.einsum("oc,ohw->chw", weight[tap].astype(jnp.float32), part)
    return summed


def fine_from_packed(packed):
    half = packed.shape[0] // 2
    split = packed.reshape(2, half, N_LAT, ROWS_DEV, NLON).transpose(1, 2, 0, 3, 4)
    return split.reshape(half, 2 * NLAT, NLON)


def packed_from_fine(fine):
    half = fine.shape[0]
    split = fine.reshape(half, N_LAT, 2, ROWS_DEV, NLON).transpose(2, 0, 1, 3, 4)
    return split.reshape(2 * half, NLAT, NLON)


def tiles(field):
    depth = field.shape[1] // N_LAT
    return field.reshape(field.shape[0], N_LAT, depth, N_LON, COLS_DEV).transpose(0, 1, 3, 2, 4)


def untiles(blocks):
    return blocks.transpose(0, 1, 3, 2, 4).reshape(blocks.shape[0], N_LAT * blocks.shape[3], NLON)


def windows(field):
    blocks = tiles(field)
    joined = jnp.concatenate([blocks, jnp.roll(blocks, -1, axis=2)], axis=4)
    return joined.reshape(field.shape[0], N_LAT, N_LON, -1)


def table_view(table):
    return tiles(table).transpose(1, 2, 0, 3, 4)


def outgoing_marine_flux(fine, index, weight):
    window = windows(fine[None])[0]
    taken = jnp.take_along_axis(window, index.reshape(N_LAT, N_LON, -1), axis=2).reshape(index.shape)
    result = jnp.sum(weight * taken, axis=2) / jnp.sum(weight, axis=2)
    return untiles(result[None])[0]


def to_sea(coarse, index, weight):
    count = coarse.shape[0]
    window = windows(coarse)
    flat_index = jnp.broadcast_to(index.reshape(N_LAT, N_LON, -1)[None], (count, N_LAT, N_LON, index[0, 0].size))
    taken = jnp.take_along_axis(window, flat_index, axis=3)
    taken = taken.reshape(count, N_LAT, N_LON, 2, 4, ROWS_DEV, COLS_DEV)
    grouped = weight.reshape(N_LAT, N_LON, 2, 4, ROWS_DEV, COLS_DEV)
    result = jnp.sum(grouped * taken, axis=4) / jnp.sum(grouped, axis=3)
    result = result.transpose(0, 1, 3, 4, 2, 5)
    return result.reshape(count, 2 * NLAT, NLON)


def arriving_aloft_flux(topmost_marine_level, index, weight):
    values = tiles(topmost_marine_level[None])[0]
    share = weight / jnp.sum(weight, axis=2, keepdims=True) * values[:, :, None]
    size = 4 * ROWS_DEV * COLS_DEV
    offsets = (jnp.arange(N_LAT * N_LON, dtype=jnp.int32) * size).reshape(N_LAT, N_LON, 1, 1, 1)
    flat_index = (index + offsets).reshape(-1).astype(jnp.int32)
    summed = jnp.zeros((N_LAT * N_LON * size,), jnp.float32).at[flat_index].add(share.reshape(-1))
    summed = summed.reshape(N_LAT, N_LON, 2 * ROWS_DEV, 2 * COLS_DEV)
    joined = summed[..., :COLS_DEV] + jnp.roll(summed[..., COLS_DEV:], 1, axis=1)
    return untiles(joined[None])[0]


def from_sea(pulled, index, weight):
    count = pulled.shape[0]
    values = pulled.reshape(count, N_LAT, 2, ROWS_DEV, N_LON, COLS_DEV).transpose(0, 1, 4, 2, 3, 5)
    grouped = weight.reshape(N_LAT, N_LON, 2, 4, ROWS_DEV, COLS_DEV)
    share = (grouped / jnp.sum(grouped, axis=3, keepdims=True))[None] * values[:, :, :, :, None]
    size = 2 * ROWS_DEV * COLS_DEV
    offsets = (jnp.arange(N_LAT * N_LON, dtype=jnp.int32) * size).reshape(N_LAT, N_LON, 1, 1, 1)
    flat_index = (index + offsets).reshape(-1).astype(jnp.int32)
    summed = jnp.zeros((count, N_LAT * N_LON * size), jnp.float32).at[:, flat_index].add(share.reshape(count, -1))
    summed = summed.reshape(count, N_LAT, N_LON, ROWS_DEV, 2 * COLS_DEV)
    joined = summed[..., :COLS_DEV] + jnp.roll(summed[..., COLS_DEV:], 1, axis=2)
    return untiles(joined)


def reference(state, direction, air_first, air_bias, air_second, air_flux, aloft_reaction_to_seawarmth, sea_first, sea_bias, sea_second, sea_forcing, regrid_index, regrid_weight, land_mask):
    aloft_lookup_position = table_view(regrid_index[0])
    aloft_regrid_coefficient = table_view(regrid_weight[0]).astype(jnp.float32)
    sea_index = table_view(regrid_index[1])
    sea_weight = table_view(regrid_weight[1]).astype(jnp.float32)
    sea_state = fine_from_packed(state[1])
    marine_probe_vector = fine_from_packed(direction[1])
    mask = land_mask.reshape(2, N_LAT, ROWS_DEV, NLON).transpose(1, 0, 2, 3).reshape(2 * NLAT, NLON).astype(jnp.float32)

    air_slope = 1.0 - jnp.tanh(conv_taps(air_first, state[0]) + air_bias[:, None, None]) ** 2
    air_hidden = (air_slope * conv_taps(air_first, direction[0])).astype(jnp.bfloat16)
    aloft_perturbation = conv_taps(air_second, air_hidden)
    flux = jnp.einsum("fc,chw->fhw", air_flux.astype(jnp.float32), aloft_perturbation, precision=HIGH)

    sea_slope = 1.0 - jnp.tanh(conv_taps(sea_first, sea_state) + sea_bias[:, None, None]) ** 2
    sea_hidden = (sea_slope * conv_taps(sea_first, marine_probe_vector)).astype(jnp.bfloat16)
    sea_increment = conv_taps(sea_second, sea_hidden)

    seawarmth_lifted = outgoing_marine_flux(marine_probe_vector[0].astype(jnp.float32), aloft_lookup_position, aloft_regrid_coefficient)
    aloft_picture_values = (aloft_perturbation + aloft_reaction_to_seawarmth[:, None, None] * seawarmth_lifted).astype(jnp.bfloat16)
    forcing = to_sea(flux, sea_index, sea_weight)
    added = jnp.einsum("cf,fhw->chw", sea_forcing.astype(jnp.float32), forcing, precision=HIGH)
    sea_image = (mask * (sea_increment + added)).astype(jnp.bfloat16)
    image = jnp.stack([aloft_picture_values, packed_from_fine(sea_image)])

    topmost_marine_level = jnp.einsum("c,chw->hw", aloft_reaction_to_seawarmth, aloft_picture_values.astype(jnp.float32), precision=HIGH)
    pulled = jnp.einsum("cf,chw->fhw", sea_forcing.astype(jnp.float32), sea_image.astype(jnp.float32), precision=HIGH)
    flux_back = from_sea(pulled, sea_index, sea_weight)
    seawarmth_adjoint = arriving_aloft_flux(topmost_marine_level, aloft_lookup_position, aloft_regrid_coefficient)

    pushed = jnp.einsum("fc,fhw->chw", air_flux.astype(jnp.float32), flux_back, precision=HIGH)
    air_cot = (aloft_picture_values.astype(jnp.float32) + pushed).astype(jnp.bfloat16)
    air_back = (air_slope * conv_back(air_second, air_cot)).astype(jnp.bfloat16)
    air_product = conv_back(air_first, air_back).astype(jnp.bfloat16)
    sea_back = (sea_slope * conv_back(sea_second, sea_image)).astype(jnp.bfloat16)
    marine_sensitivity = conv_back(sea_first, sea_back)
    marine_sensitivity = marine_sensitivity.at[0].add(seawarmth_adjoint)
    product = jnp.stack([air_product, packed_from_fine(marine_sensitivity.astype(jnp.bfloat16))])
    return image, product
```

```python
import functools

import jax
import jax.numpy as jnp
from jax import lax
from jax.experimental import pallas as pl
from jax.experimental.pallas import tpu as pltpu
from jax.sharding import PartitionSpec as P

F32 = jnp.float32
BF16 = jnp.bfloat16
ROWS = 2
COLS = 256
PITCH = COLS + 128
CELLS = ROWS * COLS
SLOTS = 8


def lane_iota(shape):
    return lax.broadcasted_iota(jnp.int32, shape, 1)


def split_parts(values):
    high = values.astype(BF16)
    low = (values - high.astype(F32)).astype(BF16)
    return jnp.concatenate([high, low], axis=0)


def dot(left, right):
    return lax.dot_general(left, right, (((1,), (0,)), ((), ())), preferred_element_type=F32)


def sources(own, above, below):
    return [(ref, r) for ref in (above, own, below) for r in range(ROWS)]


def prepare_kernel(
    flags, first_a, second_a, first_o, second_o, index, weight, fwd1, fwd2, bwd1, bwd2, hot, share
):
    def weights(first, second, channels):
        padded = -(-3 * channels // 16) * 16
        hidden = first.shape[2]
        fill = jnp.zeros((padded - 3 * channels, hidden), F32)

        def to_hidden(source, flip, target):
            pieces = []
            for a in range(3):
                for e in range(3):
                    tap = 3 * a + e
                    pieces.append(source[8 - tap if flip else tap].astype(F32))
                if padded > 3 * channels:
                    pieces.append(fill)
            stacked = jnp.concatenate(pieces, axis=0)
            target[:hidden, : 3 * padded] = stacked.T.astype(BF16)

        def from_hidden(source, flip, target):
            for a in range(3):
                pieces = []
                for e in range(3):
                    tap = 3 * a + e
                    pieces.append(source[8 - tap if flip else tap].astype(F32))
                stacked = jnp.concatenate(pieces, axis=0)
                target[: 3 * channels, a * hidden : (a + 1) * hidden] = stacked.astype(BF16)

        to_hidden(first, False, fwd1)
        from_hidden(second, False, fwd2)
        to_hidden(second, True, bwd1)
        from_hidden(first, True, bwd2)

    table = weight[...].astype(F32)

    @pl.when(flags[0] == 0)
    def _():
        weights(first_a, second_a, first_a.shape[1])
        share[...] = table / jnp.sum(table, axis=0, keepdims=True)

    @pl.when(flags[0] != 0)
    def _():
        weights(first_o, second_o, first_o.shape[1])
        upper = jnp.sum(table[:4], axis=0, keepdims=True)
        lower = jnp.sum(table[4:], axis=0, keepdims=True)
        place = lax.broadcasted_iota(jnp.int32, table.shape, 0)
        share[...] = table / jnp.where(place < 4, upper, lower)

    lanes = lax.broadcasted_iota(jnp.int32, (128, CELLS), 0)
    for slot in range(SLOTS):
        low = index[slot : slot + 1, :] & 127
        hot[:, slot * CELLS : (slot + 1) * CELLS] = jnp.where(lanes == low, 1.0, 0.0).astype(BF16)


def edge_kernel(own, above, below, to_left, to_right):
    channels = own.shape[0]
    lanes = lane_iota((channels, 128))
    left = jnp.zeros((channels, 128), F32)
    right = jnp.zeros((channels, 128), F32)
    for place, (ref, r) in enumerate(sources(own, above, below)):
        initial = ref[:, r * COLS : r * COLS + 128].astype(F32)
        last = ref[:, r * COLS + 128 : (r + 1) * COLS].astype(F32)
        here = (lanes >> 1) == place
        if place:
            initial = pltpu.roll(initial, 2 * place, 1)
        left = jnp.where(here, initial, left)
        right = jnp.where(here, pltpu.roll(last, 2 * place + 2, 1), right)
    to_left[...] = left.astype(BF16)
    to_right[...] = right.astype(BF16)


def shifted_rows(main, place, from_left, from_right, fill):
    lanes = lane_iota(from_left.shape)
    after = pltpu.roll(from_right, (128 - 2 * place) % 128, 1) if place else from_right
    before = pltpu.roll(from_left, 126 - 2 * place, 1)
    edge = jnp.where(lanes < 2, after, jnp.where(lanes >= 126, before, 0.0))
    full = jnp.concatenate([main, edge], axis=1)
    pieces = [pltpu.roll(full, 1, 1), full, pltpu.roll(full, PITCH - 1, 1)]
    if fill:
        pieces.append(jnp.zeros((fill, PITCH), F32))
    return jnp.concatenate(pieces, axis=0).astype(BF16)


def air_rows(own, above, below, from_left, from_right, fields, store):
    for field in range(fields):
        part = slice(field * 80, (field + 1) * 80)
        left = from_left[part, :].astype(F32)
        right = from_right[part, :].astype(F32)
        for place, (ref, r) in enumerate(sources(own, above, below)):
            main = ref[part, r * COLS : (r + 1) * COLS].astype(F32)
            store(field, place, shifted_rows(main, place, left, right, 0))


def sea_rows(own, above, below, from_left, from_right, fields, store):
    for field in range(fields):
        part = slice(field * 80, (field + 1) * 80)
        left = from_left[part, :].astype(F32)
        right = from_right[part, :].astype(F32)
        for place, (ref, r) in enumerate(sources(own, above, below)):
            main = ref[part, r * COLS : (r + 1) * COLS].astype(F32)
            for half in range(2):
                fine = 2 * (2 * (place // 2) + half - 1) + r
                if 0 <= fine < 8:
                    cut = slice(half * 40, half * 40 + 40)
                    rows = shifted_rows(main[cut], place, left[cut], right[cut], 8)
                    store(field, fine, rows)


def row_span(place):
    return pl.ds(pl.multiple_of(place * PITCH, 128), PITCH)


def tap_stack(ref, first_row, depth, place):
    pieces = [ref[first_row : first_row + depth, row_span(place + a)] for a in range(3)]
    return jnp.concatenate(pieces, axis=0)


def joined_taps(product, channels):
    total = pltpu.roll(product[:channels], 1, 1) + product[channels : 2 * channels]
    total = total + pltpu.roll(product[2 * channels : 3 * channels], PITCH - 1, 1)
    return total[:, :COLS]


def pole_scale(flags, place, count):
    outside = ((flags[1] == 0) & (place == 0)) | ((flags[1] == flags[2] - 1) & (place == count - 1))
    return jnp.where(outside, 0.0, 1.0).astype(F32)


def tangent_kernel(
    flags, own, above, below, from_left, from_right, fwd1, fwd2, bias, flux_weight,
    y, slope, payload, stack, hidden,
):
    def run(channels, width, depth, count, slope_slice):
        padded = depth // 3

        def one_row(place, unused):
            scale = pole_scale(flags, place, count)
            base = dot(fwd1[:width, :depth], tap_stack(stack, 0, padded, place))
            tangent = dot(fwd1[:width, :depth], tap_stack(stack, padded, padded, place))
            steep = 1.0 - jnp.tanh(base + bias[:width, :]) ** 2
            hidden[:width, row_span(place)] = (steep * tangent * scale).astype(BF16)
            slope_slice(place, steep.astype(BF16))
            return unused

        lax.fori_loop(0, count, one_row, 0)

    def second(channels, width, place):
        taps = tap_stack(hidden, 0, width, place)
        return joined_taps(dot(fwd2[: 3 * channels, : 3 * width], taps), channels)

    @pl.when(flags[0] == 0)
    def _():
        def store(field, place, rows):
            stack[field * 240 : field * 240 + 240, place * PITCH : (place + 1) * PITCH] = rows

        air_rows(own, above, below, from_left, from_right, 2, store)

        def keep(place, rows):
            slope[:, row_span(place)] = rows

        run(80, 512, 720, 4, keep)
        for r in range(ROWS):
            result = second(80, 512, r)
            y[:, r * COLS : (r + 1) * COLS] = result
            for f in range(2):
                flux = jnp.sum(flux_weight[:, f : f + 1] * result, axis=0, keepdims=True)
                for part in range(2):
                    line = f * 4 + r * 2 + part
                    payload[line : line + 1, :] = flux[:, part * 128 : (part + 1) * 128]

    @pl.when(flags[0] != 0)
    def _():
        def store(field, place, rows):
            stack[field * 128 : field * 128 + 128, place * PITCH : (place + 1) * PITCH] = rows

        sea_rows(own, above, below, from_left, from_right, 2, store)

        def keep(place, rows):
            @pl.when(place < 4)
            def _():
                slope[:256, row_span(place)] = rows

            @pl.when(place >= 4)
            def _():
                slope[256:, row_span(place - 4)] = rows

        run(40, 256, 384, 6, keep)
        for fine in range(2 * ROWS):
            y[:40, fine * COLS : (fine + 1) * COLS] = second(40, 256, fine)
            half, r = divmod(fine, 2)
            line = own[80 + 40 * half : 88 + 40 * half, r * COLS : (r + 1) * COLS].astype(F32)
            for part in range(2):
                place = fine * 2 + part
                payload[place : place + 1, :] = line[:1, part * 128 : (part + 1) * 128]


def couple_kernel(
    flags, y, near, far, hot, index, share, mask, aloft, forcing_weight, image, back_near, back_far
):
    window = jnp.concatenate([near[...], far[...]], axis=0)
    parts = dot(split_parts(window), hot[...])
    gathered = parts[:16] + parts[16:]
    lines = lax.broadcasted_iota(jnp.int32, (16, CELLS), 0)

    def span(slot):
        return slice(slot * CELLS, (slot + 1) * CELLS)

    def line_of(slot):
        place = index[slot : slot + 1, :]
        return ((place >> 8) & 1) * 8 + (place >> 9) * 2 + ((place >> 7) & 1)

    def scatter(pieces):
        spread = split_parts(jnp.concatenate(pieces, axis=1))
        total = lax.dot_general(
            spread, hot[...], (((1,), (1,)), ((), ())), preferred_element_type=F32
        )
        total = total[:16] + total[16:]
        back_near[...] = total[:8]
        back_far[...] = total[8:]

    def pick(slot, offset):
        chosen = jnp.where(lines == line_of(slot) + offset, gathered[:, span(slot)], 0.0)
        return share[slot : slot + 1, :] * jnp.sum(chosen, axis=0, keepdims=True)

    @pl.when(flags[0] == 0)
    def _():
        lifted = pick(0, 0)
        for slot in range(1, SLOTS):
            lifted = lifted + pick(slot, 0)
        rounded = (y[:, :CELLS] + aloft[...] * lifted).astype(BF16)
        image[...] = rounded
        surface = jnp.sum(aloft[...] * rounded.astype(F32), axis=0, keepdims=True)
        pieces = []
        for slot in range(SLOTS):
            value = share[slot : slot + 1, :] * surface
            pieces.append(jnp.where(lines == line_of(slot), value, 0.0))
        scatter(pieces)

    @pl.when(flags[0] != 0)
    def _():
        halves = []
        pulled = []
        for half in range(2):
            forcing = []
            for f in range(2):
                total = pick(4 * half, 4 * f)
                for k in range(1, 4):
                    total = total + pick(4 * half + k, 4 * f)
                forcing.append(total)
            added = forcing_weight[:, :1] * forcing[0] + forcing_weight[:, 1:] * forcing[1]
            fine = mask[half : half + 1, :] * (y[:40, span(half)] + added)
            rounded = fine.astype(BF16).astype(F32)
            halves.append(rounded)
            pulled.append(
                [jnp.sum(forcing_weight[:, f : f + 1] * rounded, axis=0, keepdims=True) for f in range(2)]
            )
        image[...] = jnp.concatenate(halves, axis=0).astype(BF16)
        pieces = []
        for slot in range(SLOTS):
            line = line_of(slot)
            part = share[slot : slot + 1, :]
            first = jnp.where(lines == line, part * pulled[slot // 4][0], 0.0)
            other = jnp.where(lines == line + 4, part * pulled[slot // 4][1], 0.0)
            pieces.append(first + other)
        scatter(pieces)


def cotangent_kernel(flags, image, near, far, flux_weight, cotangent):
    @pl.when(flags[0] == 0)
    def _():
        arrived = near[...] + far[...]
        total = image[...].astype(F32)
        for f in range(2):
            row = jnp.concatenate([arrived[f * 4 + q : f * 4 + q + 1, :] for q in range(4)], axis=1)
            total = total + flux_weight[:, f : f + 1] * row
        cotangent[...] = total.astype(BF16)

    @pl.when(flags[0] != 0)
    def _():
        cotangent[...] = image[...]


def adjoint_kernel(
    flags, own, above, below, from_left, from_right, bwd1, bwd2, slope, near, far,
    product, stack, hidden,
):
    def run(width, depth, count, slope_slice):
        padded = depth // 3

        def one_row(place, unused):
            scale = pole_scale(flags, place, count)
            back = dot(bwd1[:width, :depth], tap_stack(stack, 0, padded, place))
            back = back * slope_slice(place).astype(F32) * scale
            hidden[:width, row_span(place)] = back.astype(BF16)
            return unused

        lax.fori_loop(0, count, one_row, 0)

    def second(channels, width, place):
        taps = tap_stack(hidden, 0, width, place)
        return joined_taps(dot(bwd2[: 3 * channels, : 3 * width], taps), channels)

    @pl.when(flags[0] == 0)
    def _():
        def store(field, place, rows):
            stack[:240, place * PITCH : (place + 1) * PITCH] = rows

        air_rows(own, above, below, from_left, from_right, 1, store)
        run(512, 720, 4, lambda place: slope[:, row_span(place)])
        for r in range(ROWS):
            product[:, r * COLS : (r + 1) * COLS] = second(80, 512, r).astype(BF16)

    @pl.when(flags[0] != 0)
    def _():
        def store(field, place, rows):
            stack[:128, place * PITCH : (place + 1) * PITCH] = rows

        sea_rows(own, above, below, from_left, from_right, 1, store)

        def slope_slice(place):
            upper = slope[:256, row_span(jnp.minimum(place, 3))]
            lower = slope[256:, row_span(jnp.maximum(place - 4, 0))]
            return jnp.where(place < 4, upper, lower)

        run(256, 384, 6, slope_slice)
        arrived = near[...] + far[...]
        channel = lax.broadcasted_iota(jnp.int32, (40, COLS), 0)
        for r in range(ROWS):
            halves = []
            for half in range(2):
                fine = 2 * half + r
                row = jnp.concatenate(
                    [arrived[2 * fine + q : 2 * fine + q + 1, :] for q in range(2)], axis=1
                )
                halves.append(second(40, 256, fine) + jnp.where(channel == 0, row, 0.0))
            rows = jnp.concatenate(halves, axis=0)
            product[:, r * COLS : (r + 1) * COLS] = rows.astype(BF16)


def call(kernel, name, out_shape, inputs, scratch=()):
    smem = pl.BlockSpec(memory_space=pltpu.SMEM)
    vmem = pl.BlockSpec(memory_space=pltpu.VMEM)
    flagged = inputs[0].ndim == 1
    specs = [smem if flagged and i == 0 else vmem for i in range(len(inputs))]
    out_specs = tuple(vmem for _ in out_shape)
    return pl.pallas_call(
        kernel,
        name=name,
        out_shape=tuple(jax.ShapeDtypeStruct(shape, dtype) for shape, dtype in out_shape),
        in_specs=specs,
        out_specs=out_specs,
        scratch_shapes=[pltpu.VMEM(shape, dtype) for shape, dtype in scratch],
        compiler_params=pltpu.CompilerParams(vmem_limit_bytes=48 << 20),
    )(*inputs)


def lat_pair(block):
    count = lax.axis_size("lat")
    above = lax.ppermute(block, "lat", [(i, i + 1) for i in range(count - 1)])
    below = lax.ppermute(block, "lat", [(i + 1, i) for i in range(count - 1)])
    return above, below


def lon_pair(to_left, to_right):
    count = lax.axis_size("lon")
    from_left = lax.ppermute(to_right, "lon", [(i, (i + 1) % count) for i in range(count)])
    from_right = lax.ppermute(to_left, "lon", [((i + 1) % count, i) for i in range(count)])
    return from_left, from_right


def across(near, far, shift):
    count = lax.axis_size("lon")
    same = lax.ppermute(near, "comp", [(0, 1), (1, 0)])
    route = []
    for part in range(2):
        for i in range(count):
            route.append((part * count + i, (1 - part) * count + (i + shift) % count))
    return same, lax.ppermute(far, ("comp", "lon"), route)


def shards(
    state,
    direction,
    air_first,
    air_bias,
    air_second,
    air_flux,
    aloft_reaction_to_seawarmth,
    sea_first,
    sea_bias,
    sea_second,
    sea_forcing,
    regrid_index,
    regrid_weight,
    land_mask,
):
    comp = lax.axis_index("comp")
    flags = jnp.stack([comp, lax.axis_index("lat"), jnp.int32(lax.axis_size("lat"))]).astype(jnp.int32)
    own = jnp.concatenate([state[0].reshape(80, CELLS), direction[0].reshape(80, CELLS)], axis=0)
    index = regrid_index[0].reshape(SLOTS, CELLS)
    weight = regrid_weight[0].reshape(SLOTS, CELLS)
    mask = land_mask.reshape(2, CELLS).astype(F32)
    bias = jnp.where(comp == 0, air_bias, jnp.concatenate([sea_bias, sea_bias])).reshape(512, 1)
    flux_weight = air_flux.astype(F32).T
    forcing_weight = sea_forcing.astype(F32)
    aloft = aloft_reaction_to_seawarmth.reshape(80, 1)

    above, below = lat_pair(own)
    fwd1, fwd2, bwd1, bwd2, hot, share = call(
        prepare_kernel,
        "prepare",
        [
            ((512, 720), BF16), ((240, 1536), BF16), ((512, 720), BF16), ((240, 1536), BF16),
            ((128, SLOTS * CELLS), BF16), ((SLOTS, CELLS), F32),
        ],
        [
            flags, air_first.transpose(0, 2, 1), air_second, sea_first.transpose(0, 2, 1),
            sea_second, index, weight,
        ],
    )
    to_left, to_right = call(
        edge_kernel, "edges", [((160, 128), BF16)] * 2, [own, above, below]
    )
    from_left, from_right = lon_pair(to_left, to_right)
    y, slope, payload = call(
        tangent_kernel,
        "tangent",
        [((80, 2 * CELLS), F32), ((512, 4 * PITCH), BF16), ((8, 128), F32)],
        [flags, own, above, below, from_left, from_right, fwd1, fwd2, bias, flux_weight],
        [((480, 8 * PITCH), BF16), ((512, 6 * PITCH), BF16)],
    )
    near, far = across(payload, payload, -1)
    image, back_near, back_far = call(
        couple_kernel,
        "couple",
        [((80, CELLS), BF16), ((8, 128), F32), ((8, 128), F32)],
        [flags, y, near, far, hot, index, share, mask, aloft, forcing_weight],
    )
    back_near, back_far = across(back_near, back_far, 1)
    (cotangent,) = call(
        cotangent_kernel, "cotangent", [((80, CELLS), BF16)],
        [flags, image, back_near, back_far, flux_weight],
    )
    above, below = lat_pair(cotangent)
    to_left, to_right = call(
        edge_kernel, "edges_back", [((80, 128), BF16)] * 2, [cotangent, above, below]
    )
    from_left, from_right = lon_pair(to_left, to_right)
    (product,) = call(
        adjoint_kernel,
        "adjoint",
        [((80, CELLS), BF16)],
        [
            flags, cotangent, above, below, from_left, from_right, bwd1, bwd2, slope,
            back_near, back_far,
        ],
        [((240, 8 * PITCH), BF16), ((512, 6 * PITCH), BF16)],
    )
    return image.reshape(1, 80, ROWS, COLS), product.reshape(1, 80, ROWS, COLS)


def solution(mesh):
    return jax.shard_map(
        shards,
        mesh=mesh,
        in_specs=(
            P("comp", None, "lat", "lon"),
            P("comp", None, "lat", "lon"),
            P(),
            P(),
            P(),
            P(),
            P(),
            P(),
            P(),
            P(),
            P(),
            P("comp", None, "lat", "lon"),
            P("comp", None, "lat", "lon"),
            P(None, "lat", "lon"),
        ),
        out_specs=(P("comp", None, "lat", "lon"), P("comp", None, "lat", "lon")),
        check_vma=False,
    )
```

```python
import functools

import jax
import jax.numpy as jnp
from jax import lax
from jax.experimental import pallas as pl
from jax.experimental.pallas import tpu as pltpu
from jax.sharding import PartitionSpec as P

F32 = jnp.float32
BF16 = jnp.bfloat16
ROWS = 2
COLS = 256
PITCH = COLS + 128
CELLS = ROWS * COLS
SLOTS = 8


def lane_iota(shape):
    return lax.broadcasted_iota(jnp.int32, shape, 1)


def split_parts(values):
    high = values.astype(BF16)
    low = (values - high.astype(F32)).astype(BF16)
    return jnp.concatenate([high, low], axis=0)


def dot(left, right):
    return lax.dot_general(left, right, (((1,), (0,)), ((), ())), preferred_element_type=F32)


def sources(flags, own, above, below):
    upper = jnp.where(flags[1] == 0, 0.0, 1.0).astype(F32)
    lower = jnp.where(flags[1] == flags[2] - 1, 0.0, 1.0).astype(F32)
    chosen = []
    for ref, scale in ((above, upper), (own, None), (below, lower)):
        for r in range(ROWS):

            def read(part, start, stop, ref=ref, scale=scale, r=r):
                rows = ref[part, r * COLS + start : r * COLS + stop].astype(F32)
                return rows if scale is None else rows * scale

            chosen.append((read, r))
    return chosen


def pack_kernel(state, direction, packed):
    for field, ref in enumerate((state, direction)):
        block = ref[0].astype(F32)
        for r in range(ROWS):
            packed[field * 80 : field * 80 + 80, r * COLS : (r + 1) * COLS] = block[:, r, :].astype(BF16)


def prepare_kernel(
    flags, first_a, second_a, first_o, second_o, index, weight, land, bias_a, bias_o, flux, aloft,
    forcing, fwd1, fwd2, bwd1, bwd2, hot, share, line, mask, columns,
):
    def flat(rows):
        return jnp.concatenate([rows[r : r + 1] for r in range(ROWS)], axis=1)

    def weights(first, second, channels):
        padded = -(-3 * channels // 16) * 16
        hidden = first.shape[2]
        fill = jnp.zeros((padded - 3 * channels, hidden), F32)

        def to_hidden(source, flip, target):
            pieces = []
            for a in range(3):
                for e in range(3):
                    tap = 3 * a + e
                    pieces.append(source[8 - tap if flip else tap].astype(F32))
                if padded > 3 * channels:
                    pieces.append(fill)
            stacked = jnp.concatenate(pieces, axis=0)
            target[:hidden, : 3 * padded] = stacked.T.astype(BF16)

        def from_hidden(source, flip, target):
            for a in range(3):
                pieces = []
                for e in range(3):
                    tap = 3 * a + e
                    pieces.append(source[8 - tap if flip else tap].astype(F32))
                stacked = jnp.concatenate(pieces, axis=0)
                target[: 3 * channels, a * hidden : (a + 1) * hidden] = stacked.astype(BF16)

        to_hidden(first, False, fwd1)
        from_hidden(second, False, fwd2)
        to_hidden(second, True, bwd1)
        from_hidden(first, True, bwd2)

    table = jnp.concatenate([flat(weight[0, s]) for s in range(SLOTS)], axis=0).astype(F32)
    place = jnp.concatenate([flat(index[0, s]) for s in range(SLOTS)], axis=0)
    line[...] = ((place >> 8) & 1) * 8 + (place >> 9) * 2 + ((place >> 7) & 1)
    mask[...] = jnp.concatenate([flat(land[s]) for s in range(2)], axis=0).astype(F32)
    pad = jnp.zeros((1, 512 - 80), F32)
    bias = jnp.where(flags[0] == 0, bias_a[...], jnp.concatenate([bias_o[...]] * 2, axis=1))
    rows = [bias] + [jnp.concatenate([flux[f : f + 1, :].astype(F32), pad], axis=1) for f in range(2)]
    rows.append(jnp.concatenate([aloft[...], pad], axis=1))
    pad = jnp.zeros((1, 512 - 40), F32)
    rows += [jnp.concatenate([forcing[f : f + 1, :].astype(F32), pad], axis=1) for f in range(2)]
    rows.append(jnp.zeros((2, 512), F32))
    columns[...] = jnp.concatenate(rows, axis=0).T

    @pl.when(flags[0] == 0)
    def _():
        weights(first_a, second_a, first_a.shape[1])
        share[...] = table / jnp.sum(table, axis=0, keepdims=True)

    @pl.when(flags[0] != 0)
    def _():
        weights(first_o, second_o, first_o.shape[1])
        upper = jnp.sum(table[:4], axis=0, keepdims=True)
        lower = jnp.sum(table[4:], axis=0, keepdims=True)
        slot = lax.broadcasted_iota(jnp.int32, table.shape, 0)
        share[...] = table / jnp.where(slot < 4, upper, lower)

    lanes = lax.broadcasted_iota(jnp.int32, (128, CELLS), 0)
    for slot in range(SLOTS):
        low = place[slot : slot + 1, :] & 127
        hot[:, slot * CELLS : (slot + 1) * CELLS] = jnp.where(lanes == low, 1.0, 0.0).astype(BF16)


def edge_kernel(flags, own, above, below, after, to_left, to_right):
    channels = own.shape[0]
    lanes = lane_iota((channels, 128))
    left = jnp.zeros((channels, 128), F32)
    right = jnp.zeros((channels, 128), F32)
    for place, (read, r) in enumerate(sources(flags, own, above, below)):
        initial = read(slice(0, channels), 0, 128)
        last = read(slice(0, channels), 128, COLS)
        here = (lanes >> 1) == place
        if place:
            initial = pltpu.roll(initial, 2 * place, 1)
        left = jnp.where(here, initial, left)
        right = jnp.where(here, pltpu.roll(last, 2 * place + 2, 1), right)
    to_left[...] = left.astype(BF16)
    to_right[...] = right.astype(BF16)


def shifted_rows(main, place, from_left, from_right, fill):
    lanes = lane_iota(from_left.shape)
    after = pltpu.roll(from_right, (128 - 2 * place) % 128, 1) if place else from_right
    before = pltpu.roll(from_left, 126 - 2 * place, 1)
    edge = jnp.where(lanes < 2, after, jnp.where(lanes >= 126, before, 0.0))
    full = jnp.concatenate([main, edge], axis=1)
    pieces = [pltpu.roll(full, 1, 1), full, pltpu.roll(full, PITCH - 1, 1)]
    if fill:
        pieces.append(jnp.zeros((fill, PITCH), F32))
    return jnp.concatenate(pieces, axis=0).astype(BF16)


def air_rows(flags, own, above, below, from_left, from_right, fields, store):
    for field in range(fields):
        part = slice(field * 80, (field + 1) * 80)
        left = from_left[part, :].astype(F32)
        right = from_right[part, :].astype(F32)
        for place, (read, r) in enumerate(sources(flags, own, above, below)):
            main = read(part, 0, COLS)
            store(field, place, shifted_rows(main, place, left, right, 0))


def sea_rows(flags, own, above, below, from_left, from_right, fields, store):
    for field in range(fields):
        part = slice(field * 80, (field + 1) * 80)
        left = from_left[part, :].astype(F32)
        right = from_right[part, :].astype(F32)
        for place, (read, r) in enumerate(sources(flags, own, above, below)):
            main = read(part, 0, COLS)
            for half in range(2):
                fine = 2 * (2 * (place // 2) + half - 1) + r
                if 0 <= fine < 8:
                    cut = slice(half * 40, half * 40 + 40)
                    rows = shifted_rows(main[cut], place, left[cut], right[cut], 8)
                    store(field, fine, rows)


def row_span(place):
    return pl.ds(pl.multiple_of(place * PITCH, 128), PITCH)


def tap_stack(ref, first_row, depth, place):
    pieces = [ref[first_row : first_row + depth, row_span(place + a)] for a in range(3)]
    return jnp.concatenate(pieces, axis=0)


def joined_taps(product, channels):
    total = pltpu.roll(product[:channels], 1, 1) + product[channels : 2 * channels]
    total = total + pltpu.roll(product[2 * channels : 3 * channels], PITCH - 1, 1)
    return total[:, :COLS]


def pole_scale(flags, place, count):
    outside = ((flags[1] == 0) & (place == 0)) | ((flags[1] == flags[2] - 1) & (place == count - 1))
    return jnp.where(outside, 0.0, 1.0).astype(F32)


def tangent_kernel(
    flags, own, above, below, from_left, from_right, fwd1, fwd2, columns,
    y, slope, payload, stack, hidden,
):
    def run(channels, width, depth, count, slope_slice):
        padded = depth // 3

        def one_row(place, unused):
            scale = pole_scale(flags, place, count)
            base = dot(fwd1[:width, :depth], tap_stack(stack, 0, padded, place))
            tangent = dot(fwd1[:width, :depth], tap_stack(stack, padded, padded, place))
            steep = 1.0 - jnp.tanh(base + columns[:width, 0:1]) ** 2
            hidden[:width, row_span(place)] = (steep * tangent * scale).astype(BF16)
            slope_slice(place, steep.astype(BF16))
            return unused

        lax.fori_loop(0, count, one_row, 0)

    def second(channels, width, place):
        taps = tap_stack(hidden, 0, width, place)
        return joined_taps(dot(fwd2[: 3 * channels, : 3 * width], taps), channels)

    @pl.when(flags[0] == 0)
    def _():
        def store(field, place, rows):
            stack[field * 240 : field * 240 + 240, place * PITCH : (place + 1) * PITCH] = rows

        air_rows(flags, own, above, below, from_left, from_right, 2, store)

        def keep(place, rows):
            slope[:, row_span(place)] = rows

        run(80, 512, 720, 4, keep)
        for r in range(ROWS):
            result = second(80, 512, r)
            y[:, r * COLS : (r + 1) * COLS] = result
            for f in range(2):
                flux = jnp.sum(columns[:80, 1 + f : 2 + f] * result, axis=0, keepdims=True)
                for part in range(2):
                    line = f * 4 + r * 2 + part
                    payload[line : line + 1, :] = flux[:, part * 128 : (part + 1) * 128]

    @pl.when(flags[0] != 0)
    def _():
        def store(field, place, rows):
            stack[field * 128 : field * 128 + 128, place * PITCH : (place + 1) * PITCH] = rows

        sea_rows(flags, own, above, below, from_left, from_right, 2, store)

        def keep(place, rows):
            @pl.when(place < 4)
            def _():
                slope[:256, row_span(place)] = rows

            @pl.when(place >= 4)
            def _():
                slope[256:, row_span(place - 4)] = rows

        run(40, 256, 384, 6, keep)
        for fine in range(2 * ROWS):
            y[:40, fine * COLS : (fine + 1) * COLS] = second(40, 256, fine)
            half, r = divmod(fine, 2)
            line = own[80 + 40 * half : 88 + 40 * half, r * COLS : (r + 1) * COLS].astype(F32)
            for part in range(2):
                place = fine * 2 + part
                payload[place : place + 1, :] = line[:1, part * 128 : (part + 1) * 128]


def couple_kernel(
    flags, y, near, far, hot, line, share, mask, columns, image, back_near, back_far
):
    window = jnp.concatenate([near[...], far[...]], axis=0)
    parts = dot(split_parts(window), hot[...])
    gathered = parts[:16] + parts[16:]
    lines = lax.broadcasted_iota(jnp.int32, (16, CELLS), 0)

    def span(slot):
        return slice(slot * CELLS, (slot + 1) * CELLS)

    def line_of(slot):
        return line[slot : slot + 1, :]

    def scatter(pieces):
        spread = split_parts(jnp.concatenate(pieces, axis=1))
        total = lax.dot_general(
            spread, hot[...], (((1,), (1,)), ((), ())), preferred_element_type=F32
        )
        total = total[:16] + total[16:]
        back_near[...] = total[:8]
        back_far[...] = total[8:]

    def pick(slot, offset):
        chosen = jnp.where(lines == line_of(slot) + offset, gathered[:, span(slot)], 0.0)
        return share[slot : slot + 1, :] * jnp.sum(chosen, axis=0, keepdims=True)

    @pl.when(flags[0] == 0)
    def _():
        aloft = columns[:80, 3:4]
        lifted = pick(0, 0)
        for slot in range(1, SLOTS):
            lifted = lifted + pick(slot, 0)
        rounded = (y[:, :CELLS] + aloft * lifted).astype(BF16)
        image[...] = rounded
        surface = jnp.sum(aloft * rounded.astype(F32), axis=0, keepdims=True)
        pieces = []
        for slot in range(SLOTS):
            value = share[slot : slot + 1, :] * surface
            pieces.append(jnp.where(lines == line_of(slot), value, 0.0))
        scatter(pieces)

    @pl.when(flags[0] != 0)
    def _():
        forcing_weight = columns[:40, 4:6]
        halves = []
        pulled = []
        for half in range(2):
            forcing = []
            for f in range(2):
                total = pick(4 * half, 4 * f)
                for k in range(1, 4):
                    total = total + pick(4 * half + k, 4 * f)
                forcing.append(total)
            added = forcing_weight[:, :1] * forcing[0] + forcing_weight[:, 1:] * forcing[1]
            fine = mask[half : half + 1, :] * (y[:40, span(half)] + added)
            rounded = fine.astype(BF16).astype(F32)
            halves.append(rounded)
            pulled.append(
                [jnp.sum(forcing_weight[:, f : f + 1] * rounded, axis=0, keepdims=True) for f in range(2)]
            )
        image[...] = jnp.concatenate(halves, axis=0).astype(BF16)
        pieces = []
        for slot in range(SLOTS):
            lead = line_of(slot)
            part = share[slot : slot + 1, :]
            first = jnp.where(lines == lead, part * pulled[slot // 4][0], 0.0)
            other = jnp.where(lines == lead + 4, part * pulled[slot // 4][1], 0.0)
            pieces.append(first + other)
        scatter(pieces)


def cotangent_kernel(flags, image, near, far, columns, cotangent):
    @pl.when(flags[0] == 0)
    def _():
        arrived = near[...] + far[...]
        total = image[...].astype(F32)
        for f in range(2):
            row = jnp.concatenate([arrived[f * 4 + q : f * 4 + q + 1, :] for q in range(4)], axis=1)
            total = total + columns[:80, 1 + f : 2 + f] * row
        cotangent[...] = total.astype(BF16)

    @pl.when(flags[0] != 0)
    def _():
        cotangent[...] = image[...]


def spread_rows(target, rows):
    target[0] = jnp.stack(rows, axis=1).astype(BF16)


def adjoint_kernel(
    flags, own, above, below, from_left, from_right, bwd1, bwd2, slope, near, far,
    product, stack, hidden,
):
    def run(width, depth, count, slope_slice):
        padded = depth // 3

        def one_row(place, unused):
            scale = pole_scale(flags, place, count)
            back = dot(bwd1[:width, :depth], tap_stack(stack, 0, padded, place))
            back = back * slope_slice(place).astype(F32) * scale
            hidden[:width, row_span(place)] = back.astype(BF16)
            return unused

        lax.fori_loop(0, count, one_row, 0)

    def second(channels, width, place):
        taps = tap_stack(hidden, 0, width, place)
        return joined_taps(dot(bwd2[: 3 * channels, : 3 * width], taps), channels)

    @pl.when(flags[0] == 0)
    def _():
        def store(field, place, rows):
            stack[:240, place * PITCH : (place + 1) * PITCH] = rows

        air_rows(flags, own, above, below, from_left, from_right, 1, store)
        run(512, 720, 4, lambda place: slope[:, row_span(place)])
        rows = []
        for r in range(ROWS):
            rows.append(second(80, 512, r))
        spread_rows(product, rows)

    @pl.when(flags[0] != 0)
    def _():
        def store(field, place, rows):
            stack[:128, place * PITCH : (place + 1) * PITCH] = rows

        sea_rows(flags, own, above, below, from_left, from_right, 1, store)

        def slope_slice(place):
            upper = slope[:256, row_span(jnp.minimum(place, 3))]
            lower = slope[256:, row_span(jnp.maximum(place - 4, 0))]
            return jnp.where(place < 4, upper, lower)

        run(256, 384, 6, slope_slice)
        arrived = near[...] + far[...]
        channel = lax.broadcasted_iota(jnp.int32, (40, COLS), 0)
        rows = []
        for r in range(ROWS):
            halves = []
            for half in range(2):
                fine = 2 * half + r
                row = jnp.concatenate(
                    [arrived[2 * fine + q : 2 * fine + q + 1, :] for q in range(2)], axis=1
                )
                halves.append(second(40, 256, fine) + jnp.where(channel == 0, row, 0.0))
            rows.append(jnp.concatenate(halves, axis=0))
        spread_rows(product, rows)


def call(kernel, name, out_shape, inputs, scratch=(), limit=8):
    smem = pl.BlockSpec(memory_space=pltpu.SMEM)
    vmem = pl.BlockSpec(memory_space=pltpu.VMEM)
    flagged = inputs[0].ndim == 1
    specs = [smem if flagged and i == 0 else vmem for i in range(len(inputs))]
    out_specs = tuple(vmem for _ in out_shape)
    return pl.pallas_call(
        kernel,
        name=name,
        out_shape=tuple(jax.ShapeDtypeStruct(shape, dtype) for shape, dtype in out_shape),
        in_specs=specs,
        out_specs=out_specs,
        scratch_shapes=[pltpu.VMEM(shape, dtype) for shape, dtype in scratch],
        compiler_params=pltpu.CompilerParams(vmem_limit_bytes=limit << 20),
    )(*inputs)


def lat_pair(block):
    count = lax.axis_size("lat")
    above = lax.ppermute(block, "lat", [(i, (i + 1) % count) for i in range(count)])
    below = lax.ppermute(block, "lat", [((i + 1) % count, i) for i in range(count)])
    return above, below


def lon_pair(to_left, to_right):
    count = lax.axis_size("lon")
    from_left = lax.ppermute(to_right, "lon", [(i, (i + 1) % count) for i in range(count)])
    from_right = lax.ppermute(to_left, "lon", [((i + 1) % count, i) for i in range(count)])
    return from_left, from_right


def across(near, far, shift):
    count = lax.axis_size("lon")
    same = lax.ppermute(near, "comp", [(0, 1), (1, 0)])
    route = []
    for part in range(2):
        for i in range(count):
            route.append((part * count + i, (1 - part) * count + (i + shift) % count))
    return same, lax.ppermute(far, ("comp", "lon"), route)


def shards(
    state,
    direction,
    air_first,
    air_bias,
    air_second,
    air_flux,
    aloft_reaction_to_seawarmth,
    sea_first,
    sea_bias,
    sea_second,
    sea_forcing,
    regrid_index,
    regrid_weight,
    land_mask,
):
    comp = lax.axis_index("comp")
    flags = jnp.stack([comp, lax.axis_index("lat"), jnp.int32(lax.axis_size("lat"))]).astype(jnp.int32)
    (own,) = call(pack_kernel, "pack", [((160, CELLS), BF16)], [state, direction])
    above, below = lat_pair(own)
    fwd1, fwd2, bwd1, bwd2, hot, share, line, mask, columns = call(
        prepare_kernel,
        "prepare",
        [
            ((512, 720), BF16), ((240, 1536), BF16), ((512, 720), BF16), ((240, 1536), BF16),
            ((128, SLOTS * CELLS), BF16), ((SLOTS, CELLS), F32), ((SLOTS, CELLS), jnp.int32),
            ((2, CELLS), F32), ((512, 8), F32),
        ],
        [
            flags, air_first.transpose(0, 2, 1), air_second, sea_first.transpose(0, 2, 1),
            sea_second, regrid_index, regrid_weight, land_mask, air_bias.reshape(1, 512),
            sea_bias.reshape(1, 256), air_flux, aloft_reaction_to_seawarmth.reshape(1, 80),
            sea_forcing.T,
        ],
        limit=16,
    )
    to_left, to_right = call(
        edge_kernel, "edges", [((160, 128), BF16)] * 2, [flags, own, above, below, columns]
    )
    from_left, from_right = lon_pair(to_left, to_right)
    y, slope, payload = call(
        tangent_kernel,
        "tangent",
        [((80, 2 * CELLS), F32), ((512, 4 * PITCH), BF16), ((8, 128), F32)],
        [flags, own, above, below, from_left, from_right, fwd1, fwd2, columns],
        [((480, 8 * PITCH), BF16), ((512, 6 * PITCH), BF16)],
        limit=20,
    )
    near, far = across(payload, payload, -1)
    image, back_near, back_far = call(
        couple_kernel,
        "couple",
        [((80, CELLS), BF16), ((8, 128), F32), ((8, 128), F32)],
        [flags, y, near, far, hot, line, share, mask, columns],
    )
    back_near, back_far = across(back_near, back_far, 1)
    (cotangent,) = call(
        cotangent_kernel, "cotangent", [((80, CELLS), BF16)],
        [flags, image, back_near, back_far, columns],
    )
    above, below = lat_pair(cotangent)
    to_left, to_right = call(
        edge_kernel, "edges_back", [((80, 128), BF16)] * 2,
        [flags, cotangent, above, below, columns],
    )
    from_left, from_right = lon_pair(to_left, to_right)
    (product,) = call(
        adjoint_kernel,
        "adjoint",
        [((1, 80, ROWS, COLS), BF16)],
        [
            flags, cotangent, above, below, from_left, from_right, bwd1, bwd2, slope,
            back_near, back_far,
        ],
        [((240, 8 * PITCH), BF16), ((512, 6 * PITCH), BF16)],
        limit=16,
    )
    return image.reshape(1, 80, ROWS, COLS), product


def solution(mesh):
    return jax.shard_map(
        shards,
        mesh=mesh,
        in_specs=(
            P("comp", None, "lat", "lon"),
            P("comp", None, "lat", "lon"),
            P(),
            P(),
            P(),
            P(),
            P(),
            P(),
            P(),
            P(),
            P(),
            P("comp", None, "lat", "lon"),
            P("comp", None, "lat", "lon"),
            P(None, "lat", "lon"),
        ),
        out_specs=(P("comp", None, "lat", "lon"), P("comp", None, "lat", "lon")),
        check_vma=False,
    )
```

```python
import functools

import jax
import jax.numpy as jnp
from jax import lax
from jax.experimental import pallas as pl
from jax.experimental.pallas import tpu as pltpu
from jax.sharding import PartitionSpec as P

F32 = jnp.float32
BF16 = jnp.bfloat16
ROWS = 2
COLS = 256
PITCH = COLS + 128
CELLS = ROWS * COLS
SLOTS = 8


def is_air():
    return lax.axis_index("comp") == 0


def is_sea():
    return lax.axis_index("comp") != 0


def at_top():
    return lax.axis_index("lat") == 0


def at_bottom():
    return lax.axis_index("lat") == lax.axis_size("lat") - 1


def lane_iota(shape):
    return lax.broadcasted_iota(jnp.int32, shape, 1)


def split_parts(values):
    high = values.astype(BF16)
    low = (values - high.astype(F32)).astype(BF16)
    return jnp.concatenate([high, low], axis=0)


def dot(left, right):
    return lax.dot_general(left, right, (((1,), (0,)), ((), ())), preferred_element_type=F32)


def sources(own, above, below):
    upper = jnp.where(at_top(), 0.0, 1.0).astype(F32)
    lower = jnp.where(at_bottom(), 0.0, 1.0).astype(F32)
    chosen = []
    for ref, scale in ((above, upper), (own, None), (below, lower)):
        for r in range(ROWS):

            def read(part, start, stop, ref=ref, scale=scale, r=r):
                rows = ref[part, r * COLS + start : r * COLS + stop].astype(F32)
                return rows if scale is None else rows * scale

            chosen.append((read, r))
    return chosen


def pack_kernel(state, direction, packed, rows, sems):
    copies = []
    for field, ref in enumerate((state, direction)):
        copies.append(pltpu.make_async_copy(ref.at[0], rows.at[field], sems.at[field]))
        copies[-1].start()
    for field, copy in enumerate(copies):
        copy.wait()
        block = rows[field].astype(F32)
        for r in range(ROWS):
            packed[field * 80 : field * 80 + 80, r * COLS : (r + 1) * COLS] = block[:, r, :].astype(BF16)


def prepare_kernel(*refs):
    sources = refs[:12]
    fwd1, fwd2, bwd1, bwd2, hot, share, line, mask, columns = refs[12:21]
    held = refs[21:33]
    sems = refs[33]
    copies = [
        pltpu.make_async_copy(source, target, sems.at[i])
        for i, (source, target) in enumerate(zip(sources, held))
    ]
    first_a, second_a, first_o, second_o, index, weight, land, bias_a, bias_o, flux, aloft, forcing = held
    for copy in copies[4:]:
        copy.start()

    @pl.when(is_air())
    def _():
        for copy in copies[:2]:
            copy.start()

    @pl.when(is_sea())
    def _():
        for copy in copies[2:4]:
            copy.start()

    for copy in copies[4:]:
        copy.wait()

    def flat(rows):
        return jnp.concatenate([rows[r : r + 1] for r in range(ROWS)], axis=1)

    def weights(first, second, channels):
        padded = -(-3 * channels // 16) * 16
        hidden = first.shape[2]
        fill = jnp.zeros((padded - 3 * channels, hidden), F32)

        def to_hidden(source, flip, target):
            pieces = []
            for a in range(3):
                for e in range(3):
                    tap = 3 * a + e
                    pieces.append(source[8 - tap if flip else tap].astype(F32))
                if padded > 3 * channels:
                    pieces.append(fill)
            stacked = jnp.concatenate(pieces, axis=0)
            target[:hidden, : 3 * padded] = stacked.T.astype(BF16)

        def from_hidden(source, flip, target):
            for a in range(3):
                pieces = []
                for e in range(3):
                    tap = 3 * a + e
                    pieces.append(source[8 - tap if flip else tap].astype(F32))
                stacked = jnp.concatenate(pieces, axis=0)
                target[: 3 * channels, a * hidden : (a + 1) * hidden] = stacked.astype(BF16)

        to_hidden(first, False, fwd1)
        from_hidden(second, False, fwd2)
        to_hidden(second, True, bwd1)
        from_hidden(first, True, bwd2)

    table = jnp.concatenate([flat(weight[0, s]) for s in range(SLOTS)], axis=0).astype(F32)
    place = jnp.concatenate([flat(index[0, s]) for s in range(SLOTS)], axis=0)
    line[...] = ((place >> 8) & 1) * 8 + (place >> 9) * 2 + ((place >> 7) & 1)
    mask[...] = jnp.concatenate([flat(land[s]) for s in range(2)], axis=0).astype(F32)
    pad = jnp.zeros((1, 512 - 80), F32)
    bias = jnp.where(is_air(), bias_a[...], jnp.concatenate([bias_o[...]] * 2, axis=1))
    rows = [bias] + [jnp.concatenate([flux[f : f + 1, :].astype(F32), pad], axis=1) for f in range(2)]
    rows.append(jnp.concatenate([aloft[...], pad], axis=1))
    pad = jnp.zeros((1, 512 - 40), F32)
    rows += [jnp.concatenate([forcing[f : f + 1, :].astype(F32), pad], axis=1) for f in range(2)]
    rows.append(jnp.zeros((2, 512), F32))
    columns[...] = jnp.concatenate(rows, axis=0).T

    @pl.when(is_air())
    def _():
        for copy in copies[:2]:
            copy.wait()
        weights(first_a, second_a, first_a.shape[1])
        share[...] = table / jnp.sum(table, axis=0, keepdims=True)

    @pl.when(is_sea())
    def _():
        for copy in copies[2:4]:
            copy.wait()
        weights(first_o, second_o, first_o.shape[1])
        upper = jnp.sum(table[:4], axis=0, keepdims=True)
        lower = jnp.sum(table[4:], axis=0, keepdims=True)
        slot = lax.broadcasted_iota(jnp.int32, table.shape, 0)
        share[...] = table / jnp.where(slot < 4, upper, lower)

    lanes = lax.broadcasted_iota(jnp.int32, (128, CELLS), 0)
    for slot in range(SLOTS):
        low = place[slot : slot + 1, :] & 127
        hot[:, slot * CELLS : (slot + 1) * CELLS] = jnp.where(lanes == low, 1.0, 0.0).astype(BF16)


def edge_kernel(own, above, below, after, to_left, to_right):
    channels = own.shape[0]
    lanes = lane_iota((channels, 128))
    left = jnp.zeros((channels, 128), F32)
    right = jnp.zeros((channels, 128), F32)
    for place, (read, r) in enumerate(sources(own, above, below)):
        initial = read(slice(0, channels), 0, 128)
        last = read(slice(0, channels), 128, COLS)
        here = (lanes >> 1) == place
        if place:
            initial = pltpu.roll(initial, 2 * place, 1)
        left = jnp.where(here, initial, left)
        right = jnp.where(here, pltpu.roll(last, 2 * place + 2, 1), right)
    to_left[...] = left.astype(BF16)
    to_right[...] = right.astype(BF16)


def shifted_rows(main, place, from_left, from_right, fill):
    lanes = lane_iota(from_left.shape)
    after = pltpu.roll(from_right, (128 - 2 * place) % 128, 1) if place else from_right
    before = pltpu.roll(from_left, 126 - 2 * place, 1)
    edge = jnp.where(lanes < 2, after, jnp.where(lanes >= 126, before, 0.0))
    full = jnp.concatenate([main, edge], axis=1)
    pieces = [pltpu.roll(full, 1, 1), full, pltpu.roll(full, PITCH - 1, 1)]
    if fill:
        pieces.append(jnp.zeros((fill, PITCH), F32))
    return jnp.concatenate(pieces, axis=0).astype(BF16)


def air_rows(own, above, below, from_left, from_right, fields, store):
    for field in range(fields):
        part = slice(field * 80, (field + 1) * 80)
        left = from_left[part, :].astype(F32)
        right = from_right[part, :].astype(F32)
        for place, (read, r) in enumerate(sources(own, above, below)):
            main = read(part, 0, COLS)
            store(field, place, shifted_rows(main, place, left, right, 0))


def sea_rows(own, above, below, from_left, from_right, fields, store):
    for field in range(fields):
        part = slice(field * 80, (field + 1) * 80)
        left = from_left[part, :].astype(F32)
        right = from_right[part, :].astype(F32)
        for place, (read, r) in enumerate(sources(own, above, below)):
            main = read(part, 0, COLS)
            for half in range(2):
                fine = 2 * (2 * (place // 2) + half - 1) + r
                if 0 <= fine < 8:
                    cut = slice(half * 40, half * 40 + 40)
                    rows = shifted_rows(main[cut], place, left[cut], right[cut], 8)
                    store(field, fine, rows)


def row_span(place):
    return pl.ds(pl.multiple_of(place * PITCH, 128), PITCH)


def tap_stack(ref, first_row, depth, place):
    pieces = [ref[first_row : first_row + depth, row_span(place + a)] for a in range(3)]
    return jnp.concatenate(pieces, axis=0)


def joined_taps(product, channels):
    total = pltpu.roll(product[:channels], 1, 1) + product[channels : 2 * channels]
    total = total + pltpu.roll(product[2 * channels : 3 * channels], PITCH - 1, 1)
    return total[:, :COLS]


def pole_scale(place, count):
    outside = (at_top() & (place == 0)) | (at_bottom() & (place == count - 1))
    return jnp.where(outside, 0.0, 1.0).astype(F32)


def tangent_kernel(
    own, above, below, from_left, from_right, fwd1, fwd2, columns,
    y, slope, payload, stack, hidden,
):
    def run(channels, width, depth, count, slope_slice):
        padded = depth // 3

        def one_row(place, unused):
            scale = pole_scale(place, count)
            base = dot(fwd1[:width, :depth], tap_stack(stack, 0, padded, place))
            tangent = dot(fwd1[:width, :depth], tap_stack(stack, padded, padded, place))
            steep = 1.0 - jnp.tanh(base + columns[:width, 0:1]) ** 2
            hidden[:width, row_span(place)] = (steep * tangent * scale).astype(BF16)
            slope_slice(place, steep.astype(BF16))
            return unused

        lax.fori_loop(0, count, one_row, 0)

    def second(channels, width, place):
        taps = tap_stack(hidden, 0, width, place)
        return joined_taps(dot(fwd2[: 3 * channels, : 3 * width], taps), channels)

    @pl.when(is_air())
    def _():
        def store(field, place, rows):
            stack[field * 240 : field * 240 + 240, place * PITCH : (place + 1) * PITCH] = rows

        air_rows(own, above, below, from_left, from_right, 2, store)

        def keep(place, rows):
            slope[:, row_span(place)] = rows

        run(80, 512, 720, 4, keep)
        for r in range(ROWS):
            result = second(80, 512, r)
            y[:, r * COLS : (r + 1) * COLS] = result
            for f in range(2):
                flux = jnp.sum(columns[:80, 1 + f : 2 + f] * result, axis=0, keepdims=True)
                for part in range(2):
                    line = f * 4 + r * 2 + part
                    payload[line : line + 1, :] = flux[:, part * 128 : (part + 1) * 128]

    @pl.when(is_sea())
    def _():
        def store(field, place, rows):
            stack[field * 128 : field * 128 + 128, place * PITCH : (place + 1) * PITCH] = rows

        sea_rows(own, above, below, from_left, from_right, 2, store)

        def keep(place, rows):
            @pl.when(place < 4)
            def _():
                slope[:256, row_span(place)] = rows

            @pl.when(place >= 4)
            def _():
                slope[256:, row_span(place - 4)] = rows

        run(40, 256, 384, 6, keep)
        for fine in range(2 * ROWS):
            y[:40, fine * COLS : (fine + 1) * COLS] = second(40, 256, fine)
            half, r = divmod(fine, 2)
            line = own[80 + 40 * half : 88 + 40 * half, r * COLS : (r + 1) * COLS].astype(F32)
            for part in range(2):
                place = fine * 2 + part
                payload[place : place + 1, :] = line[:1, part * 128 : (part + 1) * 128]


def couple_kernel(
    y, near, far, hot, line, share, mask, columns, image, back_near, back_far
):
    window = jnp.concatenate([near[...], far[...]], axis=0)
    parts = dot(split_parts(window), hot[...])
    gathered = parts[:16] + parts[16:]
    lines = lax.broadcasted_iota(jnp.int32, (16, CELLS), 0)

    def span(slot):
        return slice(slot * CELLS, (slot + 1) * CELLS)

    def line_of(slot):
        return line[slot : slot + 1, :]

    def scatter(pieces):
        spread = split_parts(jnp.concatenate(pieces, axis=1))
        total = lax.dot_general(
            spread, hot[...], (((1,), (1,)), ((), ())), preferred_element_type=F32
        )
        total = total[:16] + total[16:]
        back_near[...] = total[:8]
        back_far[...] = total[8:]

    def pick(slot, offset):
        chosen = jnp.where(lines == line_of(slot) + offset, gathered[:, span(slot)], 0.0)
        return share[slot : slot + 1, :] * jnp.sum(chosen, axis=0, keepdims=True)

    @pl.when(is_air())
    def _():
        aloft = columns[:80, 3:4]
        lifted = pick(0, 0)
        for slot in range(1, SLOTS):
            lifted = lifted + pick(slot, 0)
        rounded = (y[:, :CELLS] + aloft * lifted).astype(BF16)
        image[...] = rounded
        surface = jnp.sum(aloft * rounded.astype(F32), axis=0, keepdims=True)
        pieces = []
        for slot in range(SLOTS):
            value = share[slot : slot + 1, :] * surface
            pieces.append(jnp.where(lines == line_of(slot), value, 0.0))
        scatter(pieces)

    @pl.when(is_sea())
    def _():
        forcing_weight = columns[:40, 4:6]
        halves = []
        pulled = []
        for half in range(2):
            forcing = []
            for f in range(2):
                total = pick(4 * half, 4 * f)
                for k in range(1, 4):
                    total = total + pick(4 * half + k, 4 * f)
                forcing.append(total)
            added = forcing_weight[:, :1] * forcing[0] + forcing_weight[:, 1:] * forcing[1]
            fine = mask[half : half + 1, :] * (y[:40, span(half)] + added)
            rounded = fine.astype(BF16).astype(F32)
            halves.append(rounded)
            pulled.append(
                [jnp.sum(forcing_weight[:, f : f + 1] * rounded, axis=0, keepdims=True) for f in range(2)]
            )
        image[...] = jnp.concatenate(halves, axis=0).astype(BF16)
        pieces = []
        for slot in range(SLOTS):
            lead = line_of(slot)
            part = share[slot : slot + 1, :]
            first = jnp.where(lines == lead, part * pulled[slot // 4][0], 0.0)
            other = jnp.where(lines == lead + 4, part * pulled[slot // 4][1], 0.0)
            pieces.append(first + other)
        scatter(pieces)


def cotangent_kernel(image, near, far, columns, cotangent):
    @pl.when(is_air())
    def _():
        arrived = near[...] + far[...]
        total = image[...].astype(F32)
        for f in range(2):
            row = jnp.concatenate([arrived[f * 4 + q : f * 4 + q + 1, :] for q in range(4)], axis=1)
            total = total + columns[:80, 1 + f : 2 + f] * row
        cotangent[...] = total.astype(BF16)

    @pl.when(is_sea())
    def _():
        cotangent[...] = image[...]


def spread_rows(target, rows):
    target[0] = jnp.stack(rows, axis=1).astype(BF16)


def adjoint_kernel(
    own, above, below, from_left, from_right, bwd1, bwd2, slope, near, far,
    product, stack, hidden,
):
    def run(width, depth, count, slope_slice):
        padded = depth // 3

        def one_row(place, unused):
            scale = pole_scale(place, count)
            back = dot(bwd1[:width, :depth], tap_stack(stack, 0, padded, place))
            back = back * slope_slice(place).astype(F32) * scale
            hidden[:width, row_span(place)] = back.astype(BF16)
            return unused

        lax.fori_loop(0, count, one_row, 0)

    def second(channels, width, place):
        taps = tap_stack(hidden, 0, width, place)
        return joined_taps(dot(bwd2[: 3 * channels, : 3 * width], taps), channels)

    @pl.when(is_air())
    def _():
        def store(field, place, rows):
            stack[:240, place * PITCH : (place + 1) * PITCH] = rows

        air_rows(own, above, below, from_left, from_right, 1, store)
        run(512, 720, 4, lambda place: slope[:, row_span(place)])
        rows = []
        for r in range(ROWS):
            rows.append(second(80, 512, r))
        spread_rows(product, rows)

    @pl.when(is_sea())
    def _():
        def store(field, place, rows):
            stack[:128, place * PITCH : (place + 1) * PITCH] = rows

        sea_rows(own, above, below, from_left, from_right, 1, store)

        def slope_slice(place):
            upper = slope[:256, row_span(jnp.minimum(place, 3))]
            lower = slope[256:, row_span(jnp.maximum(place - 4, 0))]
            return jnp.where(place < 4, upper, lower)

        run(256, 384, 6, slope_slice)
        arrived = near[...] + far[...]
        channel = lax.broadcasted_iota(jnp.int32, (40, COLS), 0)
        rows = []
        for r in range(ROWS):
            halves = []
            for half in range(2):
                fine = 2 * half + r
                row = jnp.concatenate(
                    [arrived[2 * fine + q : 2 * fine + q + 1, :] for q in range(2)], axis=1
                )
                halves.append(second(40, 256, fine) + jnp.where(channel == 0, row, 0.0))
            rows.append(jnp.concatenate(halves, axis=0))
        spread_rows(product, rows)


def call(kernel, name, out_shape, inputs, scratch=(), limit=8, loads=False):
    vmem = pl.BlockSpec(memory_space=pltpu.VMEM)
    source = vmem
    if loads:
        source = pl.BlockSpec(memory_space=pltpu.HBM)
        inputs = [pltpu.with_memory_space_constraint(array, pltpu.HBM) for array in inputs]
    return pl.pallas_call(
        kernel,
        name=name,
        out_shape=tuple(jax.ShapeDtypeStruct(shape, dtype) for shape, dtype in out_shape),
        in_specs=[source] * len(inputs),
        out_specs=tuple(vmem for _ in out_shape),
        scratch_shapes=list(scratch),
        compiler_params=pltpu.CompilerParams(vmem_limit_bytes=limit << 20),
    )(*inputs)


def lat_pair(block):
    count = lax.axis_size("lat")
    above = lax.ppermute(block, "lat", [(i, (i + 1) % count) for i in range(count)])
    below = lax.ppermute(block, "lat", [((i + 1) % count, i) for i in range(count)])
    return above, below


def lon_pair(to_left, to_right):
    count = lax.axis_size("lon")
    from_left = lax.ppermute(to_right, "lon", [(i, (i + 1) % count) for i in range(count)])
    from_right = lax.ppermute(to_left, "lon", [((i + 1) % count, i) for i in range(count)])
    return from_left, from_right


def across(near, far, shift):
    count = lax.axis_size("lon")
    same = lax.ppermute(near, "comp", [(0, 1), (1, 0)])
    route = []
    for part in range(2):
        for i in range(count):
            route.append((part * count + i, (1 - part) * count + (i + shift) % count))
    return same, lax.ppermute(far, ("comp", "lon"), route)


def shards(
    state,
    direction,
    air_first,
    air_bias,
    air_second,
    air_flux,
    aloft_reaction_to_seawarmth,
    sea_first,
    sea_bias,
    sea_second,
    sea_forcing,
    regrid_index,
    regrid_weight,
    land_mask,
):
    (own,) = call(
        pack_kernel,
        "pack",
        [((160, CELLS), BF16)],
        [state, direction],
        [pltpu.VMEM((2, 80, ROWS, COLS), BF16), pltpu.SemaphoreType.DMA((2,))],
        loads=True,
    )
    above, below = lat_pair(own)
    raw = [
        air_first.transpose(0, 2, 1),
        air_second,
        sea_first.transpose(0, 2, 1),
        sea_second,
        regrid_index,
        regrid_weight,
        land_mask,
        air_bias.reshape(1, 512),
        sea_bias.reshape(1, 256),
        air_flux,
        aloft_reaction_to_seawarmth.reshape(1, 80),
        sea_forcing.T,
    ]
    fwd1, fwd2, bwd1, bwd2, hot, share, line, mask, columns = call(
        prepare_kernel,
        "prepare",
        [
            ((512, 720), BF16), ((240, 1536), BF16), ((512, 720), BF16), ((240, 1536), BF16),
            ((128, SLOTS * CELLS), BF16), ((SLOTS, CELLS), F32), ((SLOTS, CELLS), jnp.int32),
            ((2, CELLS), F32), ((512, 8), F32),
        ],
        raw,
        [pltpu.VMEM(array.shape, array.dtype) for array in raw] + [pltpu.SemaphoreType.DMA((12,))],
        limit=20,
        loads=True,
    )
    to_left, to_right = call(
        edge_kernel, "edges", [((160, 128), BF16)] * 2, [own, above, below, columns]
    )
    from_left, from_right = lon_pair(to_left, to_right)
    y, slope, payload = call(
        tangent_kernel,
        "tangent",
        [((80, 2 * CELLS), F32), ((512, 4 * PITCH), BF16), ((8, 128), F32)],
        [own, above, below, from_left, from_right, fwd1, fwd2, columns],
        [pltpu.VMEM((480, 8 * PITCH), BF16), pltpu.VMEM((512, 6 * PITCH), BF16)],
        limit=20,
    )
    near, far = across(payload, payload, -1)
    image, back_near, back_far = call(
        couple_kernel,
        "couple",
        [((80, CELLS), BF16), ((8, 128), F32), ((8, 128), F32)],
        [y, near, far, hot, line, share, mask, columns],
    )
    back_near, back_far = across(back_near, back_far, 1)
    (cotangent,) = call(
        cotangent_kernel, "cotangent", [((80, CELLS), BF16)],
        [image, back_near, back_far, columns],
    )
    above, below = lat_pair(cotangent)
    to_left, to_right = call(
        edge_kernel, "edges_back", [((80, 128), BF16)] * 2,
        [cotangent, above, below, columns],
    )
    from_left, from_right = lon_pair(to_left, to_right)
    (product,) = call(
        adjoint_kernel,
        "adjoint",
        [((1, 80, ROWS, COLS), BF16)],
        [
            cotangent, above, below, from_left, from_right, bwd1, bwd2, slope,
            back_near, back_far,
        ],
        [pltpu.VMEM((240, 8 * PITCH), BF16), pltpu.VMEM((512, 6 * PITCH), BF16)],
        limit=16,
    )
    return image.reshape(1, 80, ROWS, COLS), product


def solution(mesh):
    return jax.shard_map(
        shards,
        mesh=mesh,
        in_specs=(
            P("comp", None, "lat", "lon"),
            P("comp", None, "lat", "lon"),
            P(),
            P(),
            P(),
            P(),
            P(),
            P(),
            P(),
            P(),
            P(),
            P("comp", None, "lat", "lon"),
            P("comp", None, "lat", "lon"),
            P(None, "lat", "lon"),
        ),
        out_specs=(P("comp", None, "lat", "lon"), P("comp", None, "lat", "lon")),
        check_vma=False,
    )
```

```python
import functools

import jax
import jax.numpy as jnp
from jax import lax
from jax.experimental import pallas as pl
from jax.experimental.pallas import tpu as pltpu
from jax.sharding import PartitionSpec as P

F32 = jnp.float32
BF16 = jnp.bfloat16
ROWS = 2
COLS = 256
CELLS = ROWS * COLS
SLOTS = 8


def is_air():
    return lax.axis_index("comp") == 0


def is_sea():
    return lax.axis_index("comp") != 0


def at_top():
    return lax.axis_index("lat") == 0


def at_bottom():
    return lax.axis_index("lat") == lax.axis_size("lat") - 1


def lane_iota(shape):
    return lax.broadcasted_iota(jnp.int32, shape, 1)


def split_parts(values):
    high = values.astype(BF16)
    low = (values - high.astype(F32)).astype(BF16)
    return jnp.concatenate([high, low], axis=0)


def dot(left, right):
    return lax.dot_general(left, right, (((1,), (0,)), ((), ())), preferred_element_type=F32)


def sources(own, above, below):
    upper = jnp.where(at_top(), 0.0, 1.0).astype(F32)
    lower = jnp.where(at_bottom(), 0.0, 1.0).astype(F32)
    chosen = []
    for ref, scale in ((above, upper), (own, None), (below, lower)):
        for r in range(ROWS):

            def read(part, start, stop, ref=ref, scale=scale, r=r):
                rows = ref[part, r * COLS + start : r * COLS + stop].astype(F32)
                return rows if scale is None else rows * scale

            chosen.append((read, r))
    return chosen


def pack_kernel(state, direction, packed, rows, sems):
    copies = []
    for field, ref in enumerate((state, direction)):
        copies.append(pltpu.make_async_copy(ref.at[0], rows.at[field], sems.at[field]))
        copies[-1].start()
    for field, copy in enumerate(copies):
        copy.wait()
        block = rows[field].astype(F32)
        for r in range(ROWS):
            packed[field * 80 : field * 80 + 80, r * COLS : (r + 1) * COLS] = block[:, r, :].astype(BF16)


def prepare_kernel(*refs):
    sources = refs[:12]
    fwd1, fwd2, bwd1, bwd2, hot, share, line, mask, columns = refs[12:21]
    held = refs[21:33]
    sems = refs[33]
    copies = [
        pltpu.make_async_copy(source, target, sems.at[i])
        for i, (source, target) in enumerate(zip(sources, held))
    ]
    first_a, second_a, first_o, second_o, index, weight, land, bias_a, bias_o, flux, aloft, forcing = held
    for copy in copies[4:]:
        copy.start()

    @pl.when(is_air())
    def _():
        for copy in copies[:2]:
            copy.start()

    @pl.when(is_sea())
    def _():
        for copy in copies[2:4]:
            copy.start()

    for copy in copies[4:]:
        copy.wait()

    def flat(rows):
        return jnp.concatenate([rows[r : r + 1] for r in range(ROWS)], axis=1)

    def weights(first, second, channels):
        padded = -(-3 * channels // 16) * 16
        hidden = first.shape[2]
        fill = jnp.zeros((padded - 3 * channels, hidden), F32)

        def to_hidden(source, flip, target):
            pieces = []
            for a in range(3):
                for e in range(3):
                    tap = 3 * a + e
                    pieces.append(source[8 - tap if flip else tap].astype(F32))
                if padded > 3 * channels:
                    pieces.append(fill)
            stacked = jnp.concatenate(pieces, axis=0)
            target[:hidden, : 3 * padded] = stacked.T.astype(BF16)

        def from_hidden(source, flip, target):
            for a in range(3):
                pieces = []
                for e in range(3):
                    tap = 3 * a + e
                    pieces.append(source[8 - tap if flip else tap].astype(F32))
                stacked = jnp.concatenate(pieces, axis=0)
                target[: 3 * channels, a * hidden : (a + 1) * hidden] = stacked.astype(BF16)

        to_hidden(first, False, fwd1)
        from_hidden(second, False, fwd2)
        to_hidden(second, True, bwd1)
        from_hidden(first, True, bwd2)

    table = jnp.concatenate([flat(weight[0, s]) for s in range(SLOTS)], axis=0).astype(F32)
    place = jnp.concatenate([flat(index[0, s]) for s in range(SLOTS)], axis=0)
    line[...] = ((place >> 8) & 1) * 8 + (place >> 9) * 2 + ((place >> 7) & 1)
    mask[...] = jnp.concatenate([flat(land[s]) for s in range(2)], axis=0).astype(F32)
    pad = jnp.zeros((1, 512 - 80), F32)
    bias = jnp.where(is_air(), bias_a[...], jnp.concatenate([bias_o[...]] * 2, axis=1))
    rows = [bias] + [jnp.concatenate([flux[f : f + 1, :].astype(F32), pad], axis=1) for f in range(2)]
    rows.append(jnp.concatenate([aloft[...], pad], axis=1))
    pad = jnp.zeros((1, 512 - 40), F32)
    rows += [jnp.concatenate([forcing[f : f + 1, :].astype(F32), pad], axis=1) for f in range(2)]
    rows.append(jnp.zeros((2, 512), F32))
    columns[...] = jnp.concatenate(rows, axis=0).T

    @pl.when(is_air())
    def _():
        for copy in copies[:2]:
            copy.wait()
        weights(first_a, second_a, first_a.shape[1])
        share[...] = table / jnp.sum(table, axis=0, keepdims=True)

    @pl.when(is_sea())
    def _():
        for copy in copies[2:4]:
            copy.wait()
        weights(first_o, second_o, first_o.shape[1])
        upper = jnp.sum(table[:4], axis=0, keepdims=True)
        lower = jnp.sum(table[4:], axis=0, keepdims=True)
        slot = lax.broadcasted_iota(jnp.int32, table.shape, 0)
        share[...] = table / jnp.where(slot < 4, upper, lower)

    lanes = lax.broadcasted_iota(jnp.int32, (128, CELLS), 0)
    for slot in range(SLOTS):
        low = place[slot : slot + 1, :] & 127
        hot[:, slot * CELLS : (slot + 1) * CELLS] = jnp.where(lanes == low, 1.0, 0.0).astype(BF16)


def edge_kernel(own, above, below, after, to_left, to_right):
    channels = own.shape[0]
    lanes = lane_iota((channels, 128))
    left = jnp.zeros((channels, 128), F32)
    right = jnp.zeros((channels, 128), F32)
    for place, (read, r) in enumerate(sources(own, above, below)):
        initial = pltpu.roll(read(slice(0, channels), 0, 128), 4 * place + 2, 1)
        last = pltpu.roll(read(slice(0, channels), 128, COLS), 4 * place + 2, 1)
        left = jnp.where((lanes >> 1) == 2 * place + 1, initial, left)
        right = jnp.where((lanes >> 1) == 2 * place, last, right)
    to_left[...] = left.astype(BF16)
    to_right[...] = right.astype(BF16)


def shifted_rows(main, fill):
    pieces = [pltpu.roll(main, 1, 1), main, pltpu.roll(main, COLS - 1, 1)]
    if fill:
        pieces.append(jnp.zeros((fill, COLS), F32))
    return jnp.concatenate(pieces, axis=0).astype(BF16)


def air_rows(own, above, below, fields, store):
    for field in range(fields):
        part = slice(field * 80, (field + 1) * 80)
        for place, (read, r) in enumerate(sources(own, above, below)):
            store(field, place, shifted_rows(read(part, 0, COLS), 0))


def sea_rows(own, above, below, fields, store):
    for field in range(fields):
        part = slice(field * 80, (field + 1) * 80)
        for place, (read, r) in enumerate(sources(own, above, below)):
            main = read(part, 0, COLS)
            for half in range(2):
                fine = 2 * (2 * (place // 2) + half - 1) + r
                if 0 <= fine < 8:
                    store(field, fine, shifted_rows(main[half * 40 : half * 40 + 40], 8))


def kept(rows, count, first_row):
    lanes = lane_iota((1, rows * COLS))
    row = first_row + lanes // COLS
    column = lanes % COLS
    drop = (column == 0) | (column == COLS - 1)
    drop = drop | (at_top() & (row == 0)) | (at_bottom() & (row == count - 1))
    return jnp.where(drop, 0.0, 1.0).astype(F32)


def edge_kept(count):
    lanes = lane_iota((1, 128))
    row = lanes >> 2
    drop = (row >= count) | (at_top() & (row == 0)) | (at_bottom() & (row == count - 1))
    return jnp.where(drop, 0.0, 1.0).astype(F32)


def edge_sides(to_left, to_right, from_left, from_right, part):
    lanes = lane_iota((80, 128))
    head = (lanes & 3) < 2
    before = jnp.where(
        head, from_left[part, :].astype(F32), pltpu.roll(to_right[part, :].astype(F32), 2, 1)
    )
    after = jnp.where(
        head, pltpu.roll(to_left[part, :].astype(F32), 126, 1), from_right[part, :].astype(F32)
    )
    return before, after


def fine_lanes(rows):
    lanes = lane_iota((40, 128)) >> 3
    upper, lower = rows[:40], rows[40:]
    result = jnp.where(lanes == 0, lower, upper)
    result = jnp.where(lanes == 2, pltpu.roll(lower, 8, 1), result)
    return jnp.where(lanes == 3, pltpu.roll(upper, 8, 1), result)


def edge_stack(to_left, to_right, from_left, from_right, fields, fine):
    merged = None
    for field in range(fields):
        part = slice(field * 80, (field + 1) * 80)
        sides = edge_sides(to_left, to_right, from_left, from_right, part)
        if fine:
            sides = [fine_lanes(side) for side in sides]
        if merged is None:
            merged = sides
        else:
            low = lane_iota(sides[0].shape) < 64
            merged = [jnp.where(low, m, pltpu.roll(s, 64, 1)) for m, s in zip(merged, sides)]
    before, after = merged
    even = (lane_iota(before.shape) & 1) == 0
    middle = jnp.where(even, pltpu.roll(before, 127, 1), pltpu.roll(after, 1, 1))
    pieces = []
    for a in range(3):
        for rows in (before, middle, after):
            pieces.append(pltpu.roll(rows, 128 - 4 * a, 1) if a else rows)
        if fine:
            pieces.append(jnp.zeros((8, 128), F32))
    return jnp.concatenate(pieces, axis=0).astype(BF16)


def second_rows(weights, main, edge, channels, width, count):
    shifted = [edge] + [pltpu.roll(edge, 128 - 4 * a, 1) for a in (1, 2)]
    taps = jnp.concatenate(shifted, axis=0).astype(BF16)
    matrix = weights[: 3 * channels, : 3 * width]
    block = dot(matrix, taps)
    first, middle, last = [block[e * channels : (e + 1) * channels] for e in range(3)]
    lanes = lane_iota((channels, 128))
    left = first + jnp.where((lanes & 3) == 0, pltpu.roll(middle, 127, 1), 0.0)
    right = last + jnp.where((lanes & 3) == 3, pltpu.roll(middle, 1, 1), 0.0)
    result = []
    for pair in range(0, count, 2):
        pieces = [main[:width, (pair + a) * COLS : (pair + a + 2) * COLS] for a in range(3)]
        whole = dot(matrix, jnp.concatenate(pieces, axis=0))
        for row in (pair, pair + 1):
            cut = whole[:, (row - pair) * COLS : (row - pair + 1) * COLS]
            total = pltpu.roll(cut[:channels], 1, 1) + cut[channels : 2 * channels]
            total = total + pltpu.roll(cut[2 * channels :], COLS - 1, 1)
            head = pltpu.roll(left, 128 - 4 * row, 1) if row else left
            head = jnp.where(lanes < 2, head, 0.0)
            tail = jnp.where(lanes >= 126, pltpu.roll(right, 124 - 4 * row, 1), 0.0)
            result.append(total + jnp.concatenate([head, tail], axis=1))
    return result


def tangent_main_kernel(own, above, below, fwd1, columns, hidden, slope, stack):
    def run(width, depth, count):
        padded = depth // 3

        def one_row(place, unused):
            pieces = []
            for a in range(3):
                span = pl.ds(pl.multiple_of((place + a) * 2 * COLS, 128), 2 * COLS)
                pieces.append(stack[:padded, span])
            both = dot(fwd1[:width, :depth], jnp.concatenate(pieces, axis=0))
            steep = 1.0 - jnp.tanh(both[:, :COLS] + columns[:width, 0:1]) ** 2
            span = pl.ds(pl.multiple_of(place * COLS, 128), COLS)
            hidden[:width, span] = (steep * both[:, COLS:] * kept(1, count, place)).astype(BF16)
            slope[:width, span] = steep.astype(BF16)
            return unused

        lax.fori_loop(0, count, one_row, 0)

    def store(field, place, rows):
        start = place * 2 * COLS + field * COLS
        stack[: rows.shape[0], start : start + COLS] = rows

    @pl.when(is_air())
    def _():
        air_rows(own, above, below, 2, store)
        run(512, 720, 4)

    @pl.when(is_sea())
    def _():
        sea_rows(own, above, below, 2, store)
        run(256, 384, 6)


def tangent_edge_kernel(
    own, to_left, to_right, from_left, from_right, hidden, fwd1, fwd2, columns,
    y, slope, payload,
):
    def run(channels, width, depth, count):
        stack = edge_stack(to_left, to_right, from_left, from_right, 2, channels == 40)
        both = dot(fwd1[:width, :depth], stack)
        steep = 1.0 - jnp.tanh(both + columns[:width, 0:1]) ** 2
        slope[:width, :] = steep.astype(BF16)
        edge = steep * pltpu.roll(both, 64, 1) * edge_kept(count)
        return second_rows(fwd2, hidden, edge, channels, width, count - 2)

    @pl.when(is_air())
    def _():
        for r, result in enumerate(run(80, 512, 720, 4)):
            y[:, r * COLS : (r + 1) * COLS] = result
            for f in range(2):
                flux = jnp.sum(columns[:80, 1 + f : 2 + f] * result, axis=0, keepdims=True)
                for part in range(2):
                    line = f * 4 + r * 2 + part
                    payload[line : line + 1, :] = flux[:, part * 128 : (part + 1) * 128]

    @pl.when(is_sea())
    def _():
        for fine, result in enumerate(run(40, 256, 384, 6)):
            y[:40, fine * COLS : (fine + 1) * COLS] = result
            half, r = divmod(fine, 2)
            line = own[80 + 40 * half : 88 + 40 * half, r * COLS : (r + 1) * COLS].astype(F32)
            for part in range(2):
                place = fine * 2 + part
                payload[place : place + 1, :] = line[:1, part * 128 : (part + 1) * 128]


def couple_kernel(
    y, near, far, hot, line, share, mask, columns, image, back_near, back_far
):
    window = jnp.concatenate([near[...], far[...]], axis=0)
    parts = dot(split_parts(window), hot[...])
    gathered = parts[:16] + parts[16:]
    lines = lax.broadcasted_iota(jnp.int32, (16, CELLS), 0)

    def span(slot):
        return slice(slot * CELLS, (slot + 1) * CELLS)

    def line_of(slot):
        return line[slot : slot + 1, :]

    def scatter(pieces):
        spread = split_parts(jnp.concatenate(pieces, axis=1))
        total = lax.dot_general(
            spread, hot[...], (((1,), (1,)), ((), ())), preferred_element_type=F32
        )
        total = total[:16] + total[16:]
        back_near[...] = total[:8]
        back_far[...] = total[8:]

    def pick(slot, offset):
        chosen = jnp.where(lines == line_of(slot) + offset, gathered[:, span(slot)], 0.0)
        return share[slot : slot + 1, :] * jnp.sum(chosen, axis=0, keepdims=True)

    @pl.when(is_air())
    def _():
        aloft = columns[:80, 3:4]
        lifted = pick(0, 0)
        for slot in range(1, SLOTS):
            lifted = lifted + pick(slot, 0)
        rounded = (y[:, :CELLS] + aloft * lifted).astype(BF16)
        image[...] = rounded
        surface = jnp.sum(aloft * rounded.astype(F32), axis=0, keepdims=True)
        pieces = []
        for slot in range(SLOTS):
            value = share[slot : slot + 1, :] * surface
            pieces.append(jnp.where(lines == line_of(slot), value, 0.0))
        scatter(pieces)

    @pl.when(is_sea())
    def _():
        forcing_weight = columns[:40, 4:6]
        halves = []
        pulled = []
        for half in range(2):
            forcing = []
            for f in range(2):
                total = pick(4 * half, 4 * f)
                for k in range(1, 4):
                    total = total + pick(4 * half + k, 4 * f)
                forcing.append(total)
            added = forcing_weight[:, :1] * forcing[0] + forcing_weight[:, 1:] * forcing[1]
            fine = mask[half : half + 1, :] * (y[:40, span(half)] + added)
            rounded = fine.astype(BF16).astype(F32)
            halves.append(rounded)
            pulled.append(
                [jnp.sum(forcing_weight[:, f : f + 1] * rounded, axis=0, keepdims=True) for f in range(2)]
            )
        image[...] = jnp.concatenate(halves, axis=0).astype(BF16)
        pieces = []
        for slot in range(SLOTS):
            lead = line_of(slot)
            part = share[slot : slot + 1, :]
            first = jnp.where(lines == lead, part * pulled[slot // 4][0], 0.0)
            other = jnp.where(lines == lead + 4, part * pulled[slot // 4][1], 0.0)
            pieces.append(first + other)
        scatter(pieces)


def cotangent_kernel(image, near, far, columns, cotangent):
    @pl.when(is_air())
    def _():
        arrived = near[...] + far[...]
        total = image[...].astype(F32)
        for f in range(2):
            row = jnp.concatenate([arrived[f * 4 + q : f * 4 + q + 1, :] for q in range(4)], axis=1)
            total = total + columns[:80, 1 + f : 2 + f] * row
        cotangent[...] = total.astype(BF16)

    @pl.when(is_sea())
    def _():
        cotangent[...] = image[...]


def spread_rows(target, rows):
    target[0] = jnp.stack(rows, axis=1).astype(BF16)


def adjoint_main_kernel(own, above, below, bwd1, slope, packed, hidden, image, stack):
    wide = packed[...].astype(F32)
    spread_rows(image, [wide[:, r * COLS : (r + 1) * COLS] for r in range(ROWS)])

    def run(width, depth, count):
        padded = depth // 3

        def two_rows(pair, unused):
            pieces = []
            for a in range(3):
                span = pl.ds(pl.multiple_of((2 * pair + a) * COLS, 128), 2 * COLS)
                pieces.append(stack[:padded, span])
            back = dot(bwd1[:width, :depth], jnp.concatenate(pieces, axis=0))
            span = pl.ds(pl.multiple_of(2 * pair * COLS, 128), 2 * COLS)
            back = back * slope[:width, span].astype(F32) * kept(2, count, 2 * pair)
            hidden[:width, span] = back.astype(BF16)
            return unused

        lax.fori_loop(0, count // 2, two_rows, 0)

    def store(field, place, rows):
        stack[: rows.shape[0], place * COLS : (place + 1) * COLS] = rows

    @pl.when(is_air())
    def _():
        air_rows(own, above, below, 1, store)
        run(512, 720, 4)

    @pl.when(is_sea())
    def _():
        sea_rows(own, above, below, 1, store)
        run(256, 384, 6)


def adjoint_edge_kernel(
    to_left, to_right, from_left, from_right, hidden, slope, bwd1, bwd2, near, far, product
):
    def run(channels, width, depth, count):
        stack = edge_stack(to_left, to_right, from_left, from_right, 1, channels == 40)
        edge = dot(bwd1[:width, :depth], stack)
        edge = edge * slope[:width, :].astype(F32)
        edge = jnp.where(edge_kept(count) > 0.0, edge, 0.0)
        return second_rows(bwd2, hidden, edge, channels, width, count - 2)

    @pl.when(is_air())
    def _():
        spread_rows(product, run(80, 512, 720, 4))

    @pl.when(is_sea())
    def _():
        results = run(40, 256, 384, 6)
        arrived = near[...] + far[...]
        channel = lax.broadcasted_iota(jnp.int32, (40, COLS), 0)
        rows = []
        for r in range(ROWS):
            halves = []
            for half in range(2):
                fine = 2 * half + r
                row = jnp.concatenate(
                    [arrived[2 * fine + q : 2 * fine + q + 1, :] for q in range(2)], axis=1
                )
                halves.append(results[fine] + jnp.where(channel == 0, row, 0.0))
            rows.append(jnp.concatenate(halves, axis=0))
        spread_rows(product, rows)


def call(kernel, name, out_shape, inputs, scratch=(), limit=8, loads=False):
    vmem = pl.BlockSpec(memory_space=pltpu.VMEM)
    source = vmem
    if loads:
        source = pl.BlockSpec(memory_space=pltpu.HBM)
        inputs = [pltpu.with_memory_space_constraint(array, pltpu.HBM) for array in inputs]
    return pl.pallas_call(
        kernel,
        name=name,
        out_shape=tuple(jax.ShapeDtypeStruct(shape, dtype) for shape, dtype in out_shape),
        in_specs=[source] * len(inputs),
        out_specs=tuple(vmem for _ in out_shape),
        scratch_shapes=list(scratch),
        compiler_params=pltpu.CompilerParams(vmem_limit_bytes=limit << 20),
    )(*inputs)


def lat_pair(block):
    count = lax.axis_size("lat")
    above = lax.ppermute(block, "lat", [(i, (i + 1) % count) for i in range(count)])
    below = lax.ppermute(block, "lat", [((i + 1) % count, i) for i in range(count)])
    return above, below


def lon_pair(to_left, to_right):
    count = lax.axis_size("lon")
    from_left = lax.ppermute(to_right, "lon", [(i, (i + 1) % count) for i in range(count)])
    from_right = lax.ppermute(to_left, "lon", [((i + 1) % count, i) for i in range(count)])
    return from_left, from_right


def across(near, far, shift):
    count = lax.axis_size("lon")
    same = lax.ppermute(near, "comp", [(0, 1), (1, 0)])
    route = []
    for part in range(2):
        for i in range(count):
            route.append((part * count + i, (1 - part) * count + (i + shift) % count))
    return same, lax.ppermute(far, ("comp", "lon"), route)


def shards(
    state,
    direction,
    air_first,
    air_bias,
    air_second,
    air_flux,
    aloft_reaction_to_seawarmth,
    sea_first,
    sea_bias,
    sea_second,
    sea_forcing,
    regrid_index,
    regrid_weight,
    land_mask,
):
    (own,) = call(
        pack_kernel,
        "pack",
        [((160, CELLS), BF16)],
        [state, direction],
        [pltpu.VMEM((2, 80, ROWS, COLS), BF16), pltpu.SemaphoreType.DMA((2,))],
        loads=True,
    )
    above, below = lat_pair(own)
    raw = [
        air_first.transpose(0, 2, 1),
        air_second,
        sea_first.transpose(0, 2, 1),
        sea_second,
        regrid_index,
        regrid_weight,
        land_mask,
        air_bias.reshape(1, 512),
        sea_bias.reshape(1, 256),
        air_flux,
        aloft_reaction_to_seawarmth.reshape(1, 80),
        sea_forcing.T,
    ]
    fwd1, fwd2, bwd1, bwd2, hot, share, line, mask, columns = call(
        prepare_kernel,
        "prepare",
        [
            ((512, 720), BF16), ((240, 1536), BF16), ((512, 720), BF16), ((240, 1536), BF16),
            ((128, SLOTS * CELLS), BF16), ((SLOTS, CELLS), F32), ((SLOTS, CELLS), jnp.int32),
            ((2, CELLS), F32), ((512, 8), F32),
        ],
        raw,
        [pltpu.VMEM(array.shape, array.dtype) for array in raw] + [pltpu.SemaphoreType.DMA((12,))],
        limit=20,
        loads=True,
    )
    to_left, to_right = call(
        edge_kernel, "edges", [((160, 128), BF16)] * 2, [own, above, below, columns]
    )
    from_left, from_right = lon_pair(to_left, to_right)
    hidden, slope = call(
        tangent_main_kernel,
        "tangent_main",
        [((512, 6 * COLS), BF16), ((512, 6 * COLS), BF16)],
        [own, above, below, fwd1, columns],
        [pltpu.VMEM((240, 16 * COLS), BF16)],
        limit=16,
    )
    y, edge_slope, payload = call(
        tangent_edge_kernel,
        "tangent_edge",
        [((80, 2 * CELLS), F32), ((512, 128), BF16), ((8, 128), F32)],
        [own, to_left, to_right, from_left, from_right, hidden, fwd1, fwd2, columns],
        limit=16,
    )
    near, far = across(payload, payload, -1)
    image, back_near, back_far = call(
        couple_kernel,
        "couple",
        [((80, CELLS), BF16), ((8, 128), F32), ((8, 128), F32)],
        [y, near, far, hot, line, share, mask, columns],
    )
    back_near, back_far = across(back_near, back_far, 1)
    (cotangent,) = call(
        cotangent_kernel, "cotangent", [((80, CELLS), BF16)],
        [image, back_near, back_far, columns],
    )
    above, below = lat_pair(cotangent)
    to_left, to_right = call(
        edge_kernel, "edges_back", [((80, 128), BF16)] * 2,
        [cotangent, above, below, columns],
    )
    from_left, from_right = lon_pair(to_left, to_right)
    hidden, result = call(
        adjoint_main_kernel,
        "adjoint_main",
        [((512, 6 * COLS), BF16), ((1, 80, ROWS, COLS), BF16)],
        [cotangent, above, below, bwd1, slope, image],
        [pltpu.VMEM((240, 8 * COLS), BF16)],
        limit=16,
    )
    (product,) = call(
        adjoint_edge_kernel,
        "adjoint_edge",
        [((1, 80, ROWS, COLS), BF16)],
        [
            to_left, to_right, from_left, from_right, hidden, edge_slope, bwd1, bwd2,
            back_near, back_far,
        ],
        limit=16,
    )
    return result, product


def solution(mesh):
    return jax.shard_map(
        shards,
        mesh=mesh,
        in_specs=(
            P("comp", None, "lat", "lon"),
            P("comp", None, "lat", "lon"),
            P(),
            P(),
            P(),
            P(),
            P(),
            P(),
            P(),
            P(),
            P(),
            P("comp", None, "lat", "lon"),
            P("comp", None, "lat", "lon"),
            P(None, "lat", "lon"),
        ),
        out_specs=(P("comp", None, "lat", "lon"), P("comp", None, "lat", "lon")),
        check_vma=False,
    )
```

```python
import functools

import jax
import jax.numpy as jnp
from jax import lax
from jax.experimental import pallas as pl
from jax.experimental.pallas import tpu as pltpu
from jax.sharding import PartitionSpec as P

F32 = jnp.float32
BF16 = jnp.bfloat16
ROWS = 2
COLS = 256
CELLS = ROWS * COLS
SLOTS = 8


def is_air():
    return lax.axis_index("comp") == 0


def is_sea():
    return lax.axis_index("comp") != 0


def at_top():
    return lax.axis_index("lat") == 0


def at_bottom():
    return lax.axis_index("lat") == lax.axis_size("lat") - 1


def lane_iota(shape):
    return lax.broadcasted_iota(jnp.int32, shape, 1)


def split_parts(values):
    high = values.astype(BF16)
    low = (values - high.astype(F32)).astype(BF16)
    return jnp.concatenate([high, low], axis=0)


def dot(left, right):
    return lax.dot_general(left, right, (((1,), (0,)), ((), ())), preferred_element_type=F32)


def sources(own, above, below):
    upper = jnp.where(at_top(), 0.0, 1.0).astype(F32)
    lower = jnp.where(at_bottom(), 0.0, 1.0).astype(F32)
    chosen = []
    for ref, scale in ((above, upper), (own, None), (below, lower)):
        for r in range(ROWS):

            def read(part, start, stop, ref=ref, scale=scale, r=r):
                rows = ref[part, r * COLS + start : r * COLS + stop].astype(F32)
                return rows if scale is None else rows * scale

            chosen.append((read, r))
    return chosen


def pack_kernel(state, direction, packed, rows, sems):
    copies = []
    for field, ref in enumerate((state, direction)):
        copies.append(pltpu.make_async_copy(ref.at[0], rows.at[field], sems.at[field]))
        copies[-1].start()
    for field, copy in enumerate(copies):
        copy.wait()
        block = rows[field].astype(F32)
        for r in range(ROWS):
            packed[field * 80 : field * 80 + 80, r * COLS : (r + 1) * COLS] = block[:, r, :].astype(BF16)


def prepare_kernel(*refs):
    sources = refs[:12]
    fwd1, fwd2, bwd1, bwd2, hot, share, line, mask, columns = refs[12:21]
    held = refs[21:33]
    sems = refs[33]
    copies = [
        pltpu.make_async_copy(source, target, sems.at[i])
        for i, (source, target) in enumerate(zip(sources, held))
    ]
    first_a, second_a, first_o, second_o, index, weight, land, bias_a, bias_o, flux, aloft, forcing = held
    for copy in copies[4:]:
        copy.start()

    @pl.when(is_air())
    def _():
        for copy in copies[:2]:
            copy.start()

    @pl.when(is_sea())
    def _():
        for copy in copies[2:4]:
            copy.start()

    for copy in copies[4:]:
        copy.wait()

    def flat(rows):
        return jnp.concatenate([rows[r : r + 1] for r in range(ROWS)], axis=1)

    def weights(first, second, channels):
        padded = -(-3 * channels // 16) * 16
        hidden = first.shape[2]
        fill = jnp.zeros((padded - 3 * channels, hidden), F32)

        def to_hidden(source, flip, target):
            pieces = []
            for a in range(3):
                for e in range(3):
                    tap = 3 * a + e
                    pieces.append(source[8 - tap if flip else tap].astype(F32))
                if padded > 3 * channels:
                    pieces.append(fill)
            stacked = jnp.concatenate(pieces, axis=0)
            target[:hidden, : 3 * padded] = stacked.T.astype(BF16)

        def from_hidden(source, flip, target):
            for a in range(3):
                pieces = []
                for e in range(3):
                    tap = 3 * a + e
                    pieces.append(source[8 - tap if flip else tap].astype(F32))
                stacked = jnp.concatenate(pieces, axis=0)
                target[: 3 * channels, a * hidden : (a + 1) * hidden] = stacked.astype(BF16)

        to_hidden(first, False, fwd1)
        from_hidden(second, False, fwd2)
        to_hidden(second, True, bwd1)
        from_hidden(first, True, bwd2)

    table = jnp.concatenate([flat(weight[0, s]) for s in range(SLOTS)], axis=0).astype(F32)
    place = jnp.concatenate([flat(index[0, s]) for s in range(SLOTS)], axis=0)
    line[...] = ((place >> 8) & 1) * 8 + (place >> 9) * 2 + ((place >> 7) & 1)
    mask[...] = jnp.concatenate([flat(land[s]) for s in range(2)], axis=0).astype(F32)
    pad = jnp.zeros((1, 512 - 80), F32)
    bias = jnp.where(is_air(), bias_a[...], jnp.concatenate([bias_o[...]] * 2, axis=1))
    rows = [bias] + [jnp.concatenate([flux[f : f + 1, :].astype(F32), pad], axis=1) for f in range(2)]
    rows.append(jnp.concatenate([aloft[...], pad], axis=1))
    pad = jnp.zeros((1, 512 - 40), F32)
    rows += [jnp.concatenate([forcing[f : f + 1, :].astype(F32), pad], axis=1) for f in range(2)]
    rows.append(jnp.zeros((2, 512), F32))
    columns[...] = jnp.concatenate(rows, axis=0).T

    @pl.when(is_air())
    def _():
        for copy in copies[:2]:
            copy.wait()
        weights(first_a, second_a, first_a.shape[1])
        share[...] = table / jnp.sum(table, axis=0, keepdims=True)

    @pl.when(is_sea())
    def _():
        for copy in copies[2:4]:
            copy.wait()
        weights(first_o, second_o, first_o.shape[1])
        upper = jnp.sum(table[:4], axis=0, keepdims=True)
        lower = jnp.sum(table[4:], axis=0, keepdims=True)
        slot = lax.broadcasted_iota(jnp.int32, table.shape, 0)
        share[...] = table / jnp.where(slot < 4, upper, lower)

    lanes = lax.broadcasted_iota(jnp.int32, (128, CELLS), 0)
    for slot in range(SLOTS):
        low = place[slot : slot + 1, :] & 127
        hot[:, slot * CELLS : (slot + 1) * CELLS] = jnp.where(lanes == low, 1.0, 0.0).astype(BF16)


def edge_kernel(own, above, below, after, to_left, to_right):
    lanes = lane_iota((80, 128)) >> 1
    left = jnp.zeros((80, 128), F32)
    right = jnp.zeros((80, 128), F32)
    for field in range(own.shape[0] // 80):
        part = slice(field * 80, (field + 1) * 80)
        for place, (read, r) in enumerate(sources(own, above, below)):
            shift = 64 * field + 4 * place + 2
            initial = pltpu.roll(read(part, 0, 128), shift, 1)
            last = pltpu.roll(read(part, 128, COLS), shift, 1)
            pair = 32 * field + 2 * place
            left = jnp.where(lanes == pair + 1, initial, left)
            right = jnp.where(lanes == pair, last, right)
    to_left[...] = left.astype(BF16)
    to_right[...] = right.astype(BF16)


def shifted_rows(main, fill):
    pieces = [pltpu.roll(main, 1, 1), main, pltpu.roll(main, COLS - 1, 1)]
    if fill:
        pieces.append(jnp.zeros((fill, COLS), F32))
    return jnp.concatenate(pieces, axis=0).astype(BF16)


def air_rows(own, above, below, fields, store):
    for field in range(fields):
        part = slice(field * 80, (field + 1) * 80)
        for place, (read, r) in enumerate(sources(own, above, below)):
            store(field, place, shifted_rows(read(part, 0, COLS), 0))


def sea_rows(own, above, below, fields, store):
    for field in range(fields):
        part = slice(field * 80, (field + 1) * 80)
        for place, (read, r) in enumerate(sources(own, above, below)):
            main = read(part, 0, COLS)
            for half in range(2):
                fine = 2 * (2 * (place // 2) + half - 1) + r
                if 0 <= fine < 8:
                    store(field, fine, shifted_rows(main[half * 40 : half * 40 + 40], 8))


def kept(rows, count, first_row):
    lanes = lane_iota((1, rows * COLS))
    row = first_row + lanes // COLS
    column = lanes % COLS
    drop = (column == 0) | (column == COLS - 1)
    drop = drop | (at_top() & (row == 0)) | (at_bottom() & (row == count - 1))
    return jnp.where(drop, 0.0, 1.0).astype(F32)


def edge_kept(count):
    lanes = lane_iota((1, 128))
    row = lanes >> 2
    drop = (row >= count) | (at_top() & (row == 0)) | (at_bottom() & (row == count - 1))
    return jnp.where(drop, 0.0, 1.0).astype(F32)


def fine_lanes(rows):
    lanes = (lane_iota((40, 128)) & 63) >> 3
    upper, lower = rows[:40], rows[40:]
    result = jnp.where(lanes == 0, lower, upper)
    result = jnp.where(lanes == 2, pltpu.roll(lower, 8, 1), result)
    return jnp.where(lanes == 3, pltpu.roll(upper, 8, 1), result)


def own_sides(to_left, to_right, sides, fine):
    for i, (ref, shift) in enumerate(((to_right, 2), (to_left, 126))):
        rows = pltpu.roll(ref[...].astype(F32), shift, 1)
        if fine:
            sides[i, :40, :] = fine_lanes(rows)
        else:
            sides[i] = rows


def edge_stack(sides, from_left, from_right, fine):
    both = []
    for i, ref in enumerate((from_left, from_right)):
        rows = ref[...].astype(F32)
        both.append(fine_lanes(rows) + sides[i, :40, :] if fine else rows + sides[i])
    before, after = both
    even = (lane_iota(before.shape) & 1) == 0
    middle = jnp.where(even, pltpu.roll(before, 127, 1), pltpu.roll(after, 1, 1))
    pieces = []
    for a in range(3):
        for rows in (before, middle, after):
            pieces.append(pltpu.roll(rows, 128 - 4 * a, 1) if a else rows)
        if fine:
            pieces.append(jnp.zeros((8, 128), F32))
    return jnp.concatenate(pieces, axis=0).astype(BF16)


def halved_dot(matrix, taps):
    half = matrix.shape[0] // 16 * 8
    return jnp.concatenate([dot(matrix[:half], taps), dot(matrix[half:], taps)], axis=0)


def inner_rows(weights, main, channels, width, count):
    matrix = weights[: 3 * channels, : 3 * width]
    result = []
    for pair in range(0, count, 2):
        pieces = [main[:width, (pair + a) * COLS : (pair + a + 2) * COLS] for a in range(3)]
        whole = dot(matrix, jnp.concatenate(pieces, axis=0))
        for row in range(2):
            cut = whole[:, row * COLS : (row + 1) * COLS]
            total = pltpu.roll(cut[:channels], 1, 1) + cut[channels : 2 * channels]
            result.append(total + pltpu.roll(cut[2 * channels :], COLS - 1, 1))
    return result


def outer_rows(weights, edge, channels, width, count):
    taps = edge.astype(BF16)
    block = dot(weights[: 3 * channels, :width], taps)
    for a in (1, 2):
        part = dot(weights[: 3 * channels, a * width : (a + 1) * width], taps)
        block = block + pltpu.roll(part, 128 - 4 * a, 1)
    first, middle, last = [block[e * channels : (e + 1) * channels] for e in range(3)]
    lanes = lane_iota((channels, 128))
    left = first + jnp.where((lanes & 3) == 0, pltpu.roll(middle, 127, 1), 0.0)
    right = last + jnp.where((lanes & 3) == 3, pltpu.roll(middle, 1, 1), 0.0)
    result = []
    for row in range(count):
        head = pltpu.roll(left, 128 - 4 * row, 1) if row else left
        head = jnp.where(lanes < 2, head, 0.0)
        tail = jnp.where(lanes >= 126, pltpu.roll(right, 124 - 4 * row, 1), 0.0)
        result.append(jnp.concatenate([head, tail], axis=1))
    return result


def tangent_main_kernel(
    own, above, below, to_left, to_right, fwd1, fwd2, columns, inner, slope, sides, stack, hidden
):
    def run(channels, width, depth, count):
        padded = depth // 3
        for place in range(count):
            pieces = []
            for a in range(3):
                start = (place + a) * 2 * COLS
                pieces.append(stack[:padded, start : start + 2 * COLS])
            both = dot(fwd1[:width, :depth], jnp.concatenate(pieces, axis=0))
            steep = 1.0 - jnp.tanh(both[:, :COLS] + columns[:width, 0:1]) ** 2
            span = slice(place * COLS, (place + 1) * COLS)
            hidden[:width, span] = (steep * both[:, COLS:] * kept(1, count, place)).astype(BF16)
            slope[:width, span] = steep.astype(BF16)
        for row, result in enumerate(inner_rows(fwd2, hidden, channels, width, count - 2)):
            inner[:channels, row * COLS : (row + 1) * COLS] = result

    def store(field, place, rows):
        start = place * 2 * COLS + field * COLS
        stack[: rows.shape[0], start : start + COLS] = rows

    @pl.when(is_air())
    def _():
        own_sides(to_left, to_right, sides, False)
        air_rows(own, above, below, 2, store)
        run(80, 512, 720, 4)

    @pl.when(is_sea())
    def _():
        own_sides(to_left, to_right, sides, True)
        sea_rows(own, above, below, 2, store)
        run(40, 256, 384, 6)


def tangent_edge_kernel(
    own, sides, from_left, from_right, inner, fwd1, fwd2, columns,
    y, slope, payload,
):
    def run(channels, width, depth, count):
        stack = edge_stack(sides, from_left, from_right, channels == 40)
        both = halved_dot(fwd1[:width, :depth], stack)
        steep = 1.0 - jnp.tanh(both + columns[:width, 0:1]) ** 2
        slope[:width, :] = steep.astype(BF16)
        edge = steep * pltpu.roll(both, 64, 1) * edge_kept(count)
        rows = outer_rows(fwd2, edge, channels, width, count - 2)
        return [
            inner[:channels, i * COLS : (i + 1) * COLS] + row for i, row in enumerate(rows)
        ]

    @pl.when(is_air())
    def _():
        for r, result in enumerate(run(80, 512, 720, 4)):
            y[:, r * COLS : (r + 1) * COLS] = result
            for f in range(2):
                flux = jnp.sum(columns[:80, 1 + f : 2 + f] * result, axis=0, keepdims=True)
                for part in range(2):
                    line = f * 4 + r * 2 + part
                    payload[line : line + 1, :] = flux[:, part * 128 : (part + 1) * 128]

    @pl.when(is_sea())
    def _():
        for fine, result in enumerate(run(40, 256, 384, 6)):
            y[:40, fine * COLS : (fine + 1) * COLS] = result
            half, r = divmod(fine, 2)
            line = own[80 + 40 * half : 88 + 40 * half, r * COLS : (r + 1) * COLS].astype(F32)
            for part in range(2):
                place = fine * 2 + part
                payload[place : place + 1, :] = line[:1, part * 128 : (part + 1) * 128]


def couple_kernel(
    y, near, far, hot, line, share, mask, columns, image, back_near, back_far
):
    window = jnp.concatenate([near[...], far[...]], axis=0)
    parts = dot(split_parts(window), hot[...])
    gathered = parts[:16] + parts[16:]
    lines = lax.broadcasted_iota(jnp.int32, (16, CELLS), 0)

    def span(slot):
        return slice(slot * CELLS, (slot + 1) * CELLS)

    def line_of(slot):
        return line[slot : slot + 1, :]

    def scatter(pieces):
        spread = split_parts(jnp.concatenate(pieces, axis=1))
        total = lax.dot_general(
            spread, hot[...], (((1,), (1,)), ((), ())), preferred_element_type=F32
        )
        total = total[:16] + total[16:]
        back_near[...] = total[:8]
        back_far[...] = total[8:]

    def pick(slot, offset):
        chosen = jnp.where(lines == line_of(slot) + offset, gathered[:, span(slot)], 0.0)
        return share[slot : slot + 1, :] * jnp.sum(chosen, axis=0, keepdims=True)

    @pl.when(is_air())
    def _():
        aloft = columns[:80, 3:4]
        lifted = pick(0, 0)
        for slot in range(1, SLOTS):
            lifted = lifted + pick(slot, 0)
        rounded = (y[:, :CELLS] + aloft * lifted).astype(BF16)
        image[...] = rounded
        surface = jnp.sum(aloft * rounded.astype(F32), axis=0, keepdims=True)
        pieces = []
        for slot in range(SLOTS):
            value = share[slot : slot + 1, :] * surface
            pieces.append(jnp.where(lines == line_of(slot), value, 0.0))
        scatter(pieces)

    @pl.when(is_sea())
    def _():
        forcing_weight = columns[:40, 4:6]
        halves = []
        pulled = []
        for half in range(2):
            forcing = []
            for f in range(2):
                total = pick(4 * half, 4 * f)
                for k in range(1, 4):
                    total = total + pick(4 * half + k, 4 * f)
                forcing.append(total)
            added = forcing_weight[:, :1] * forcing[0] + forcing_weight[:, 1:] * forcing[1]
            fine = mask[half : half + 1, :] * (y[:40, span(half)] + added)
            rounded = fine.astype(BF16).astype(F32)
            halves.append(rounded)
            pulled.append(
                [jnp.sum(forcing_weight[:, f : f + 1] * rounded, axis=0, keepdims=True) for f in range(2)]
            )
        image[...] = jnp.concatenate(halves, axis=0).astype(BF16)
        pieces = []
        for slot in range(SLOTS):
            lead = line_of(slot)
            part = share[slot : slot + 1, :]
            first = jnp.where(lines == lead, part * pulled[slot // 4][0], 0.0)
            other = jnp.where(lines == lead + 4, part * pulled[slot // 4][1], 0.0)
            pieces.append(first + other)
        scatter(pieces)


def cotangent_kernel(image, near, far, columns, cotangent):
    @pl.when(is_air())
    def _():
        arrived = near[...] + far[...]
        total = image[...].astype(F32)
        for f in range(2):
            row = jnp.concatenate([arrived[f * 4 + q : f * 4 + q + 1, :] for q in range(4)], axis=1)
            total = total + columns[:80, 1 + f : 2 + f] * row
        cotangent[...] = total.astype(BF16)

    @pl.when(is_sea())
    def _():
        cotangent[...] = image[...]


def spread_rows(target, rows):
    target[0] = jnp.stack(rows, axis=1).astype(BF16)


def unpack_kernel(packed, image):
    wide = packed[...].astype(F32)
    spread_rows(image, [wide[:, r * COLS : (r + 1) * COLS] for r in range(ROWS)])


def adjoint_main_kernel(
    own, above, below, to_left, to_right, bwd1, bwd2, slope, inner, sides, stack, hidden
):
    def run(channels, width, depth, count):
        padded = depth // 3
        for pair in range(0, count, 2):
            pieces = []
            for a in range(3):
                pieces.append(stack[:padded, (pair + a) * COLS : (pair + a + 2) * COLS])
            back = dot(bwd1[:width, :depth], jnp.concatenate(pieces, axis=0))
            span = slice(pair * COLS, (pair + 2) * COLS)
            back = back * slope[:width, span].astype(F32) * kept(2, count, pair)
            hidden[:width, span] = back.astype(BF16)
        for row, result in enumerate(inner_rows(bwd2, hidden, channels, width, count - 2)):
            inner[:channels, row * COLS : (row + 1) * COLS] = result

    def store(field, place, rows):
        stack[: rows.shape[0], place * COLS : (place + 1) * COLS] = rows

    @pl.when(is_air())
    def _():
        own_sides(to_left, to_right, sides, False)
        air_rows(own, above, below, 1, store)
        run(80, 512, 720, 4)

    @pl.when(is_sea())
    def _():
        own_sides(to_left, to_right, sides, True)
        sea_rows(own, above, below, 1, store)
        run(40, 256, 384, 6)


def adjoint_edge_kernel(
    sides, from_left, from_right, inner, slope, bwd1, bwd2, near, far, product
):
    def run(channels, width, depth, count):
        stack = edge_stack(sides, from_left, from_right, channels == 40)
        edge = halved_dot(bwd1[:width, :depth], stack)
        edge = edge * slope[:width, :].astype(F32)
        edge = jnp.where(edge_kept(count) > 0.0, edge, 0.0)
        rows = outer_rows(bwd2, edge, channels, width, count - 2)
        return [
            inner[:channels, i * COLS : (i + 1) * COLS] + row for i, row in enumerate(rows)
        ]

    @pl.when(is_air())
    def _():
        spread_rows(product, run(80, 512, 720, 4))

    @pl.when(is_sea())
    def _():
        results = run(40, 256, 384, 6)
        arrived = near[...] + far[...]
        channel = lax.broadcasted_iota(jnp.int32, (40, COLS), 0)
        rows = []
        for r in range(ROWS):
            halves = []
            for half in range(2):
                fine = 2 * half + r
                row = jnp.concatenate(
                    [arrived[2 * fine + q : 2 * fine + q + 1, :] for q in range(2)], axis=1
                )
                halves.append(results[fine] + jnp.where(channel == 0, row, 0.0))
            rows.append(jnp.concatenate(halves, axis=0))
        spread_rows(product, rows)


def call(kernel, name, out_shape, inputs, scratch=(), limit=8, loads=False, idle=0):
    vmem = pl.BlockSpec(memory_space=pltpu.VMEM)
    source = vmem
    if loads:
        source = pl.BlockSpec(memory_space=pltpu.HBM)
        inputs = [pltpu.with_memory_space_constraint(array, pltpu.HBM) for array in inputs]
    for i in range(len(inputs) - idle, len(inputs)):
        inputs[i] = pltpu.with_memory_space_constraint(inputs[i], pltpu.HBM)
    return pl.pallas_call(
        kernel,
        name=name,
        out_shape=tuple(jax.ShapeDtypeStruct(shape, dtype) for shape, dtype in out_shape),
        in_specs=[source] * (len(inputs) - idle) + [pl.BlockSpec(memory_space=pltpu.HBM)] * idle,
        out_specs=tuple(vmem for _ in out_shape),
        scratch_shapes=list(scratch),
        compiler_params=pltpu.CompilerParams(vmem_limit_bytes=limit << 20),
    )(*inputs)


def lat_pair(block):
    count = lax.axis_size("lat")
    above = lax.ppermute(block, "lat", [(i, (i + 1) % count) for i in range(count)])
    below = lax.ppermute(block, "lat", [((i + 1) % count, i) for i in range(count)])
    return above, below


def lon_pair(to_left, to_right):
    count = lax.axis_size("lon")
    from_left = lax.ppermute(to_right, "lon", [(i, (i + 1) % count) for i in range(count)])
    from_right = lax.ppermute(to_left, "lon", [((i + 1) % count, i) for i in range(count)])
    return from_left, from_right


def across(near, far, shift):
    count = lax.axis_size("lon")
    same = lax.ppermute(near, "comp", [(0, 1), (1, 0)])
    route = []
    for part in range(2):
        for i in range(count):
            route.append((part * count + i, (1 - part) * count + (i + shift) % count))
    return same, lax.ppermute(far, ("comp", "lon"), route)


def shards(
    state,
    direction,
    air_first,
    air_bias,
    air_second,
    air_flux,
    aloft_reaction_to_seawarmth,
    sea_first,
    sea_bias,
    sea_second,
    sea_forcing,
    regrid_index,
    regrid_weight,
    land_mask,
):
    (own,) = call(
        pack_kernel,
        "pack",
        [((160, CELLS), BF16)],
        [state, direction],
        [pltpu.VMEM((2, 80, ROWS, COLS), BF16), pltpu.SemaphoreType.DMA((2,))],
        loads=True,
    )
    above, below = lat_pair(own)
    raw = [
        air_first.transpose(0, 2, 1),
        air_second,
        sea_first.transpose(0, 2, 1),
        sea_second,
        regrid_index,
        regrid_weight,
        land_mask,
        air_bias.reshape(1, 512),
        sea_bias.reshape(1, 256),
        air_flux,
        aloft_reaction_to_seawarmth.reshape(1, 80),
        sea_forcing.T,
    ]
    fwd1, fwd2, bwd1, bwd2, hot, share, line, mask, columns = call(
        prepare_kernel,
        "prepare",
        [
            ((512, 720), BF16), ((240, 1536), BF16), ((512, 720), BF16), ((240, 1536), BF16),
            ((128, SLOTS * CELLS), BF16), ((SLOTS, CELLS), F32), ((SLOTS, CELLS), jnp.int32),
            ((2, CELLS), F32), ((512, 8), F32),
        ],
        raw,
        [pltpu.VMEM(array.shape, array.dtype) for array in raw] + [pltpu.SemaphoreType.DMA((12,))],
        limit=20,
        loads=True,
    )
    to_left, to_right = call(
        edge_kernel, "edges", [((80, 128), BF16)] * 2, [own, above, below, columns]
    )
    from_left, from_right = lon_pair(to_left, to_right)
    inner, slope, sides = call(
        tangent_main_kernel,
        "tangent_main",
        [((80, 2 * CELLS), F32), ((512, 6 * COLS), BF16), ((2, 80, 128), F32)],
        [own, above, below, to_left, to_right, fwd1, fwd2, columns],
        [pltpu.VMEM((240, 16 * COLS), BF16), pltpu.VMEM((512, 6 * COLS), BF16)],
        limit=16,
    )
    y, edge_slope, payload = call(
        tangent_edge_kernel,
        "tangent_edge",
        [((80, 2 * CELLS), F32), ((512, 128), BF16), ((8, 128), F32)],
        [own, sides, from_left, from_right, inner, fwd1, fwd2, columns],
        limit=16,
    )
    near, far = across(payload, payload, -1)
    image, back_near, back_far = call(
        couple_kernel,
        "couple",
        [((80, CELLS), BF16), ((8, 128), F32), ((8, 128), F32)],
        [y, near, far, hot, line, share, mask, columns],
    )
    back_near, back_far = across(back_near, back_far, 1)
    (result,) = call(unpack_kernel, "unpack", [((1, 80, ROWS, COLS), BF16)], [image])
    (cotangent,) = call(
        cotangent_kernel, "cotangent", [((80, CELLS), BF16)],
        [image, back_near, back_far, columns],
    )
    above, below = lat_pair(cotangent)
    to_left, to_right = call(
        edge_kernel, "edges_back", [((80, 128), BF16)] * 2,
        [cotangent, above, below, result],
        idle=1,
    )
    from_left, from_right = lon_pair(to_left, to_right)
    inner, sides = call(
        adjoint_main_kernel,
        "adjoint_main",
        [((80, 2 * CELLS), F32), ((2, 80, 128), F32)],
        [cotangent, above, below, to_left, to_right, bwd1, bwd2, slope],
        [pltpu.VMEM((240, 8 * COLS), BF16), pltpu.VMEM((512, 6 * COLS), BF16)],
        limit=16,
    )
    (product,) = call(
        adjoint_edge_kernel,
        "adjoint_edge",
        [((1, 80, ROWS, COLS), BF16)],
        [
            sides, from_left, from_right, inner, edge_slope, bwd1, bwd2,
            back_near, back_far,
        ],
        limit=16,
    )
    return result, product


def solution(mesh):
    return jax.shard_map(
        shards,
        mesh=mesh,
        in_specs=(
            P("comp", None, "lat", "lon"),
            P("comp", None, "lat", "lon"),
            P(),
            P(),
            P(),
            P(),
            P(),
            P(),
            P(),
            P(),
            P(),
            P("comp", None, "lat", "lon"),
            P("comp", None, "lat", "lon"),
            P(None, "lat", "lon"),
        ),
        out_specs=(P("comp", None, "lat", "lon"), P("comp", None, "lat", "lon")),
        check_vma=False,
    )
```

```python
import functools

import jax
import jax.numpy as jnp
from jax import lax
from jax.experimental import pallas as pl
from jax.experimental.pallas import tpu as pltpu
from jax.sharding import PartitionSpec as P

F32 = jnp.float32
BF16 = jnp.bfloat16
ROWS = 2
COLS = 256
CELLS = ROWS * COLS
SLOTS = 8


def is_air():
    return lax.axis_index("comp") == 0


def is_sea():
    return lax.axis_index("comp") != 0


def at_top():
    return lax.axis_index("lat") == 0


def at_bottom():
    return lax.axis_index("lat") == lax.axis_size("lat") - 1


def lane_iota(shape):
    return lax.broadcasted_iota(jnp.int32, shape, 1)


def split_parts(values):
    high = values.astype(BF16)
    low = (values - high.astype(F32)).astype(BF16)
    return jnp.concatenate([high, low], axis=0)


def dot(left, right):
    return lax.dot_general(left, right, (((1,), (0,)), ((), ())), preferred_element_type=F32)


def sources(own, above, below):
    upper = jnp.where(at_top(), 0.0, 1.0).astype(F32)
    lower = jnp.where(at_bottom(), 0.0, 1.0).astype(F32)
    chosen = []
    for ref, scale in ((above, upper), (own, None), (below, lower)):
        for r in range(ROWS):

            def read(part, start, stop, ref=ref, scale=scale, r=r):
                rows = ref[part, r * COLS + start : r * COLS + stop].astype(F32)
                return rows if scale is None else rows * scale

            chosen.append((read, r))
    return chosen


def pack_kernel(state, direction, packed, rows, sems):
    copies = []
    for field, ref in enumerate((state, direction)):
        copies.append(pltpu.make_async_copy(ref.at[0], rows.at[field], sems.at[field]))
        copies[-1].start()
    line = lax.broadcasted_iota(jnp.int32, (160, 160), 0)
    place = lane_iota((160, 160))
    source = jnp.where(line < 80, 2 * line, 2 * line - 159)
    order = jnp.where(place == source, 1.0, 0.0).astype(BF16)
    for field, copy in enumerate(copies):
        copy.wait()
        block = dot(order, rows[field].reshape(160, COLS)).astype(BF16)
        for r in range(ROWS):
            packed[field * 80 : field * 80 + 80, r * COLS : (r + 1) * COLS] = block[r * 80 : (r + 1) * 80]


def prepare_kernel(*refs):
    sources = refs[:12]
    fwd1, fwd2, bwd1, bwd2, hot, picked, mask, columns = refs[12:20]
    held = refs[20:32]
    sems = refs[32]
    copies = [
        pltpu.make_async_copy(source, target, sems.at[i])
        for i, (source, target) in enumerate(zip(sources, held))
    ]
    first_a, second_a, first_o, second_o, index, weight, land, bias_a, bias_o, flux, aloft, forcing = held
    for copy in copies[4:]:
        copy.start()

    @pl.when(is_air())
    def _():
        for copy in copies[:2]:
            copy.start()

    @pl.when(is_sea())
    def _():
        for copy in copies[2:4]:
            copy.start()

    for copy in copies[4:]:
        copy.wait()

    def flat(rows):
        return jnp.concatenate([rows[r : r + 1] for r in range(ROWS)], axis=1)

    def weights(first, second, channels):
        padded = -(-3 * channels // 16) * 16
        hidden = first.shape[2]
        fill = jnp.zeros((padded - 3 * channels, hidden), F32)

        def to_hidden(source, flip, target):
            pieces = []
            for a in range(3):
                for e in range(3):
                    tap = 3 * a + e
                    pieces.append(source[8 - tap if flip else tap].astype(F32))
                if padded > 3 * channels:
                    pieces.append(fill)
            stacked = jnp.concatenate(pieces, axis=0)
            target[:hidden, : 3 * padded] = stacked.T.astype(BF16)

        def from_hidden(source, flip, target):
            for a in range(3):
                pieces = []
                for e in range(3):
                    tap = 3 * a + e
                    pieces.append(source[8 - tap if flip else tap].astype(F32))
                stacked = jnp.concatenate(pieces, axis=0)
                target[: 3 * channels, a * hidden : (a + 1) * hidden] = stacked.astype(BF16)

        to_hidden(first, False, fwd1)
        from_hidden(second, False, fwd2)
        to_hidden(second, True, bwd1)
        from_hidden(first, True, bwd2)

    table = jnp.concatenate([flat(weight[0, s]) for s in range(SLOTS)], axis=0).astype(F32)
    place = jnp.concatenate([flat(index[0, s]) for s in range(SLOTS)], axis=0)
    line = ((place >> 8) & 1) * 8 + (place >> 9) * 2 + ((place >> 7) & 1)
    rows16 = lax.broadcasted_iota(jnp.int32, (16, CELLS), 0)

    def select(share, folded):
        for slot in range(SLOTS):
            chosen = folded == line[slot : slot + 1]
            part = jnp.where(chosen, share[slot : slot + 1], 0.0)
            picked[:, slot * CELLS : (slot + 1) * CELLS] = part
    mask[...] = jnp.concatenate([flat(land[s]) for s in range(2)], axis=0).astype(F32)
    pad = jnp.zeros((1, 512 - 80), F32)
    bias = jnp.where(is_air(), bias_a[...], jnp.concatenate([bias_o[...]] * 2, axis=1))
    rows = [bias] + [jnp.concatenate([flux[f : f + 1, :].astype(F32), pad], axis=1) for f in range(2)]
    rows.append(jnp.concatenate([aloft[...], pad], axis=1))
    pad = jnp.zeros((1, 512 - 40), F32)
    rows += [jnp.concatenate([forcing[f : f + 1, :].astype(F32), pad], axis=1) for f in range(2)]
    rows.append(jnp.zeros((2, 512), F32))
    columns[...] = jnp.concatenate(rows, axis=0).T

    @pl.when(is_air())
    def _():
        for copy in copies[:2]:
            copy.wait()
        weights(first_a, second_a, first_a.shape[1])
        select(table / jnp.sum(table, axis=0, keepdims=True), rows16)

    @pl.when(is_sea())
    def _():
        for copy in copies[2:4]:
            copy.wait()
        weights(first_o, second_o, first_o.shape[1])
        upper = jnp.sum(table[:4], axis=0, keepdims=True)
        lower = jnp.sum(table[4:], axis=0, keepdims=True)
        slot = lax.broadcasted_iota(jnp.int32, table.shape, 0)
        select(table / jnp.where(slot < 4, upper, lower), rows16 & 11)

    lanes = lax.broadcasted_iota(jnp.int32, (128, CELLS), 0)
    for slot in range(SLOTS):
        low = place[slot : slot + 1, :] & 127
        hot[:, slot * CELLS : (slot + 1) * CELLS] = jnp.where(lanes == low, 1.0, 0.0).astype(BF16)


def edge_kernel(own, above, below, after, to_left, to_right):
    lanes = lane_iota((80, 128)) >> 1
    left = jnp.zeros((80, 128), F32)
    right = jnp.zeros((80, 128), F32)
    for field in range(own.shape[0] // 80):
        part = slice(field * 80, (field + 1) * 80)
        for place, (read, r) in enumerate(sources(own, above, below)):
            shift = 64 * field + 4 * place + 2
            initial = pltpu.roll(read(part, 0, 128), shift, 1)
            last = pltpu.roll(read(part, 128, COLS), shift, 1)
            pair = 32 * field + 2 * place
            left = jnp.where(lanes == pair + 1, initial, left)
            right = jnp.where(lanes == pair, last, right)
    to_left[...] = left.astype(BF16)
    to_right[...] = right.astype(BF16)


def shifted_rows(main, fill):
    pieces = [pltpu.roll(main, 1, 1), main, pltpu.roll(main, COLS - 1, 1)]
    if fill:
        pieces.append(jnp.zeros((fill, COLS), F32))
    return jnp.concatenate(pieces, axis=0).astype(BF16)


def air_rows(own, above, below, fields, store):
    for field in range(fields):
        part = slice(field * 80, (field + 1) * 80)
        for place, (read, r) in enumerate(sources(own, above, below)):
            store(field, place, shifted_rows(read(part, 0, COLS), 0))


def sea_rows(own, above, below, fields, store):
    for field in range(fields):
        part = slice(field * 80, (field + 1) * 80)
        for place, (read, r) in enumerate(sources(own, above, below)):
            main = read(part, 0, COLS)
            for half in range(2):
                fine = 2 * (2 * (place // 2) + half - 1) + r
                if 0 <= fine < 8:
                    store(field, fine, shifted_rows(main[half * 40 : half * 40 + 40], 8))


def kept(rows, count, first_row):
    lanes = lane_iota((1, rows * COLS))
    row = first_row + lanes // COLS
    column = lanes % COLS
    drop = (column == 0) | (column == COLS - 1)
    drop = drop | (at_top() & (row == 0)) | (at_bottom() & (row == count - 1))
    return jnp.where(drop, 0.0, 1.0).astype(F32)


def edge_kept(count):
    lanes = lane_iota((1, 128))
    row = lanes >> 2
    drop = (row >= count) | (at_top() & (row == 0)) | (at_bottom() & (row == count - 1))
    return jnp.where(drop, 0.0, 1.0).astype(F32)


def fine_lanes(rows):
    lanes = (lane_iota((40, 128)) & 63) >> 3
    upper, lower = rows[:40], rows[40:]
    result = jnp.where(lanes == 0, lower, upper)
    result = jnp.where(lanes == 2, pltpu.roll(lower, 8, 1), result)
    return jnp.where(lanes == 3, pltpu.roll(upper, 8, 1), result)


def own_sides(to_left, to_right, sides, fine):
    for i, (ref, shift) in enumerate(((to_right, 2), (to_left, 126))):
        rows = pltpu.roll(ref[...].astype(F32), shift, 1)
        if fine:
            sides[i, :40, :] = fine_lanes(rows)
        else:
            sides[i] = rows


def edge_stack(sides, from_left, from_right, fine):
    both = []
    for i, ref in enumerate((from_left, from_right)):
        rows = ref[...].astype(F32)
        both.append(fine_lanes(rows) + sides[i, :40, :] if fine else rows + sides[i])
    before, after = both
    even = (lane_iota(before.shape) & 1) == 0
    middle = jnp.where(even, pltpu.roll(before, 127, 1), pltpu.roll(after, 1, 1))
    pieces = []
    for a in range(3):
        for rows in (before, middle, after):
            pieces.append(pltpu.roll(rows, 128 - 4 * a, 1) if a else rows)
        if fine:
            pieces.append(jnp.zeros((8, 128), F32))
    return jnp.concatenate(pieces, axis=0).astype(BF16)


def halved_dot(matrix, taps):
    half = matrix.shape[0] // 16 * 8
    return jnp.concatenate([dot(matrix[:half], taps), dot(matrix[half:], taps)], axis=0)


def inner_rows(weights, main, channels, width, count):
    matrix = weights[: 3 * channels, : 3 * width]
    result = []
    for pair in range(0, count, 2):
        pieces = [main[:width, (pair + a) * COLS : (pair + a + 2) * COLS] for a in range(3)]
        whole = dot(matrix, jnp.concatenate(pieces, axis=0))
        for row in range(2):
            cut = whole[:, row * COLS : (row + 1) * COLS]
            total = pltpu.roll(cut[:channels], 1, 1) + cut[channels : 2 * channels]
            result.append(total + pltpu.roll(cut[2 * channels :], COLS - 1, 1))
    return result


def outer_rows(weights, edge, channels, width, count):
    taps = edge.astype(BF16)
    block = dot(weights[: 3 * channels, :width], taps)
    for a in (1, 2):
        part = dot(weights[: 3 * channels, a * width : (a + 1) * width], taps)
        block = block + pltpu.roll(part, 128 - 4 * a, 1)
    first, middle, last = [block[e * channels : (e + 1) * channels] for e in range(3)]
    lanes = lane_iota((channels, 128))
    left = first + jnp.where((lanes & 3) == 0, pltpu.roll(middle, 127, 1), 0.0)
    right = last + jnp.where((lanes & 3) == 3, pltpu.roll(middle, 1, 1), 0.0)
    result = []
    for row in range(count):
        head = pltpu.roll(left, 128 - 4 * row, 1) if row else left
        head = jnp.where(lanes < 2, head, 0.0)
        tail = jnp.where(lanes >= 126, pltpu.roll(right, 124 - 4 * row, 1), 0.0)
        result.append(jnp.concatenate([head, tail], axis=1))
    return result


def tangent_main_kernel(
    own, above, below, to_left, to_right, fwd1, fwd2, columns, inner, slope, sides, stack, hidden
):
    def run(channels, width, depth, count):
        padded = depth // 3
        for place in range(count):
            pieces = []
            for a in range(3):
                start = (place + a) * 2 * COLS
                pieces.append(stack[:padded, start : start + 2 * COLS])
            both = dot(fwd1[:width, :depth], jnp.concatenate(pieces, axis=0))
            steep = 1.0 - jnp.tanh(both[:, :COLS] + columns[:width, 0:1]) ** 2
            span = slice(place * COLS, (place + 1) * COLS)
            hidden[:width, span] = (steep * both[:, COLS:] * kept(1, count, place)).astype(BF16)
            slope[:width, span] = steep.astype(BF16)
        for row, result in enumerate(inner_rows(fwd2, hidden, channels, width, count - 2)):
            inner[:channels, row * COLS : (row + 1) * COLS] = result

    def store(field, place, rows):
        start = place * 2 * COLS + field * COLS
        stack[: rows.shape[0], start : start + COLS] = rows

    @pl.when(is_air())
    def _():
        own_sides(to_left, to_right, sides, False)
        air_rows(own, above, below, 2, store)
        run(80, 512, 720, 4)

    @pl.when(is_sea())
    def _():
        own_sides(to_left, to_right, sides, True)
        sea_rows(own, above, below, 2, store)
        run(40, 256, 384, 6)


def tangent_edge_kernel(
    own, sides, from_left, from_right, inner, fwd1, fwd2, columns,
    y, slope, payload,
):
    def run(channels, width, depth, count):
        stack = edge_stack(sides, from_left, from_right, channels == 40)
        both = halved_dot(fwd1[:width, :depth], stack)
        steep = 1.0 - jnp.tanh(both + columns[:width, 0:1]) ** 2
        slope[:width, :] = steep.astype(BF16)
        edge = steep * pltpu.roll(both, 64, 1) * edge_kept(count)
        rows = outer_rows(fwd2, edge, channels, width, count - 2)
        return [
            inner[:channels, i * COLS : (i + 1) * COLS] + row for i, row in enumerate(rows)
        ]

    @pl.when(is_air())
    def _():
        for r, result in enumerate(run(80, 512, 720, 4)):
            y[:, r * COLS : (r + 1) * COLS] = result
            for f in range(2):
                flux = jnp.sum(columns[:80, 1 + f : 2 + f] * result, axis=0, keepdims=True)
                for part in range(2):
                    line = f * 4 + r * 2 + part
                    payload[line : line + 1, :] = flux[:, part * 128 : (part + 1) * 128]

    @pl.when(is_sea())
    def _():
        for fine, result in enumerate(run(40, 256, 384, 6)):
            y[:40, fine * COLS : (fine + 1) * COLS] = result
            half, r = divmod(fine, 2)
            line = own[80 + 40 * half : 88 + 40 * half, r * COLS : (r + 1) * COLS].astype(F32)
            for part in range(2):
                place = fine * 2 + part
                payload[place : place + 1, :] = line[:1, part * 128 : (part + 1) * 128]


def couple_kernel(y, near, far, hot, picked, mask, columns, image, back_near, back_far):
    window = jnp.concatenate([near[...], far[...]], axis=0)
    parts = dot(split_parts(window), hot[...])

    def span(slot):
        return slice(slot * CELLS, (slot + 1) * CELLS)

    def gather(slots):
        total = None
        for slot in slots:
            chosen = (parts[:16, span(slot)] + parts[16:, span(slot)]) * picked[:, span(slot)]
            total = chosen if total is None else total + chosen
        return total[:8] + total[8:]

    def scatter(values):
        pieces = [picked[:, span(slot)] * values[slot // 4] for slot in range(SLOTS)]
        spread = split_parts(jnp.concatenate(pieces, axis=1))
        total = lax.dot_general(
            spread, hot[...], (((1,), (1,)), ((), ())), preferred_element_type=F32
        )
        total = total[:16] + total[16:]
        back_near[...] = total[:8]
        back_far[...] = total[8:]

    @pl.when(is_air())
    def _():
        aloft = columns[:80, 3:4]
        lifted = jnp.sum(gather(range(SLOTS)), axis=0, keepdims=True)
        rounded = (y[:, :CELLS] + aloft * lifted).astype(BF16)
        image[...] = rounded
        surface = jnp.sum(aloft * rounded.astype(F32), axis=0, keepdims=True)
        scatter([surface, surface])

    @pl.when(is_sea())
    def _():
        forcing_weight = columns[:40, 4:6]
        fields = (lax.broadcasted_iota(jnp.int32, (16, CELLS), 0) & 4) == 0
        halves = []
        pulled = []
        for half in range(2):
            folded = gather(range(4 * half, 4 * half + 4))
            forcing = [jnp.sum(folded[4 * f : 4 * f + 4], axis=0, keepdims=True) for f in range(2)]
            added = forcing_weight[:, :1] * forcing[0] + forcing_weight[:, 1:] * forcing[1]
            fine = mask[half : half + 1, :] * (y[:40, span(half)] + added)
            rounded = fine.astype(BF16).astype(F32)
            halves.append(rounded)
            first, other = [
                jnp.sum(forcing_weight[:, f : f + 1] * rounded, axis=0, keepdims=True) for f in range(2)
            ]
            pulled.append(jnp.where(fields, first, other))
        image[...] = jnp.concatenate(halves, axis=0).astype(BF16)
        scatter(pulled)


def cotangent_kernel(image, near, far, columns, cotangent):
    @pl.when(is_air())
    def _():
        arrived = near[...] + far[...]
        total = image[...].astype(F32)
        for f in range(2):
            row = jnp.concatenate([arrived[f * 4 + q : f * 4 + q + 1, :] for q in range(4)], axis=1)
            total = total + columns[:80, 1 + f : 2 + f] * row
        cotangent[...] = total.astype(BF16)

    @pl.when(is_sea())
    def _():
        cotangent[...] = image[...]


def spread_rows(target, rows):
    line = lax.broadcasted_iota(jnp.int32, (160, 160), 0)
    place = lane_iota((160, 160))
    order = jnp.where(place == (line & 1) * 80 + (line >> 1), 1.0, 0.0).astype(BF16)
    stacked = jnp.concatenate(rows, axis=0).astype(BF16)
    target[0] = dot(order, stacked).astype(BF16).reshape(80, ROWS, COLS)


def unpack_kernel(packed, image):
    wide = packed[...].astype(F32)
    spread_rows(image, [wide[:, r * COLS : (r + 1) * COLS] for r in range(ROWS)])


def adjoint_main_kernel(
    own, above, below, to_left, to_right, bwd1, bwd2, slope, inner, sides, stack, hidden
):
    def run(channels, width, depth, count):
        padded = depth // 3
        for pair in range(0, count, 2):
            pieces = []
            for a in range(3):
                pieces.append(stack[:padded, (pair + a) * COLS : (pair + a + 2) * COLS])
            back = dot(bwd1[:width, :depth], jnp.concatenate(pieces, axis=0))
            span = slice(pair * COLS, (pair + 2) * COLS)
            back = back * slope[:width, span].astype(F32) * kept(2, count, pair)
            hidden[:width, span] = back.astype(BF16)
        for row, result in enumerate(inner_rows(bwd2, hidden, channels, width, count - 2)):
            inner[:channels, row * COLS : (row + 1) * COLS] = result

    def store(field, place, rows):
        stack[: rows.shape[0], place * COLS : (place + 1) * COLS] = rows

    @pl.when(is_air())
    def _():
        own_sides(to_left, to_right, sides, False)
        air_rows(own, above, below, 1, store)
        run(80, 512, 720, 4)

    @pl.when(is_sea())
    def _():
        own_sides(to_left, to_right, sides, True)
        sea_rows(own, above, below, 1, store)
        run(40, 256, 384, 6)


def adjoint_edge_kernel(
    sides, from_left, from_right, inner, slope, bwd1, bwd2, near, far, product
):
    def run(channels, width, depth, count):
        stack = edge_stack(sides, from_left, from_right, channels == 40)
        edge = halved_dot(bwd1[:width, :depth], stack)
        edge = edge * slope[:width, :].astype(F32)
        edge = jnp.where(edge_kept(count) > 0.0, edge, 0.0)
        rows = outer_rows(bwd2, edge, channels, width, count - 2)
        return [
            inner[:channels, i * COLS : (i + 1) * COLS] + row for i, row in enumerate(rows)
        ]

    @pl.when(is_air())
    def _():
        spread_rows(product, run(80, 512, 720, 4))

    @pl.when(is_sea())
    def _():
        results = run(40, 256, 384, 6)
        arrived = near[...] + far[...]
        channel = lax.broadcasted_iota(jnp.int32, (40, COLS), 0)
        rows = []
        for r in range(ROWS):
            halves = []
            for half in range(2):
                fine = 2 * half + r
                row = jnp.concatenate(
                    [arrived[2 * fine + q : 2 * fine + q + 1, :] for q in range(2)], axis=1
                )
                halves.append(results[fine] + jnp.where(channel == 0, row, 0.0))
            rows.append(jnp.concatenate(halves, axis=0))
        spread_rows(product, rows)


def call(kernel, name, out_shape, inputs, scratch=(), limit=8, loads=False, idle=0):
    vmem = pl.BlockSpec(memory_space=pltpu.VMEM)
    source = vmem
    if loads:
        source = pl.BlockSpec(memory_space=pltpu.HBM)
        inputs = [pltpu.with_memory_space_constraint(array, pltpu.HBM) for array in inputs]
    for i in range(len(inputs) - idle, len(inputs)):
        inputs[i] = pltpu.with_memory_space_constraint(inputs[i], pltpu.HBM)
    return pl.pallas_call(
        kernel,
        name=name,
        out_shape=tuple(jax.ShapeDtypeStruct(shape, dtype) for shape, dtype in out_shape),
        in_specs=[source] * (len(inputs) - idle) + [pl.BlockSpec(memory_space=pltpu.HBM)] * idle,
        out_specs=tuple(vmem for _ in out_shape),
        scratch_shapes=list(scratch),
        compiler_params=pltpu.CompilerParams(vmem_limit_bytes=limit << 20),
    )(*inputs)


def lat_pair(block):
    count = lax.axis_size("lat")
    above = lax.ppermute(block, "lat", [(i, (i + 1) % count) for i in range(count)])
    below = lax.ppermute(block, "lat", [((i + 1) % count, i) for i in range(count)])
    return above, below


def lon_pair(to_left, to_right):
    count = lax.axis_size("lon")
    from_left = lax.ppermute(to_right, "lon", [(i, (i + 1) % count) for i in range(count)])
    from_right = lax.ppermute(to_left, "lon", [((i + 1) % count, i) for i in range(count)])
    return from_left, from_right


def across(near, far, shift):
    count = lax.axis_size("lon")
    same = lax.ppermute(near, "comp", [(0, 1), (1, 0)])
    route = []
    for part in range(2):
        for i in range(count):
            route.append((part * count + i, (1 - part) * count + (i + shift) % count))
    return same, lax.ppermute(far, ("comp", "lon"), route)


def shards(
    state,
    direction,
    air_first,
    air_bias,
    air_second,
    air_flux,
    aloft_reaction_to_seawarmth,
    sea_first,
    sea_bias,
    sea_second,
    sea_forcing,
    regrid_index,
    regrid_weight,
    land_mask,
):
    (own,) = call(
        pack_kernel,
        "pack",
        [((160, CELLS), BF16)],
        [state, direction],
        [pltpu.VMEM((2, 80, ROWS, COLS), BF16), pltpu.SemaphoreType.DMA((2,))],
        loads=True,
    )
    above, below = lat_pair(own)
    raw = [
        air_first.transpose(0, 2, 1),
        air_second,
        sea_first.transpose(0, 2, 1),
        sea_second,
        regrid_index,
        regrid_weight,
        land_mask,
        air_bias.reshape(1, 512),
        sea_bias.reshape(1, 256),
        air_flux,
        aloft_reaction_to_seawarmth.reshape(1, 80),
        sea_forcing.T,
    ]
    fwd1, fwd2, bwd1, bwd2, hot, picked, mask, columns = call(
        prepare_kernel,
        "prepare",
        [
            ((512, 720), BF16), ((240, 1536), BF16), ((512, 720), BF16), ((240, 1536), BF16),
            ((128, SLOTS * CELLS), BF16), ((16, SLOTS * CELLS), F32),
            ((2, CELLS), F32), ((512, 8), F32),
        ],
        raw,
        [pltpu.VMEM(array.shape, array.dtype) for array in raw] + [pltpu.SemaphoreType.DMA((12,))],
        limit=20,
        loads=True,
    )
    to_left, to_right = call(
        edge_kernel, "edges", [((80, 128), BF16)] * 2, [own, above, below, columns]
    )
    from_left, from_right = lon_pair(to_left, to_right)
    inner, slope, sides = call(
        tangent_main_kernel,
        "tangent_main",
        [((80, 2 * CELLS), F32), ((512, 6 * COLS), BF16), ((2, 80, 128), F32)],
        [own, above, below, to_left, to_right, fwd1, fwd2, columns],
        [pltpu.VMEM((240, 16 * COLS), BF16), pltpu.VMEM((512, 6 * COLS), BF16)],
        limit=16,
    )
    y, edge_slope, payload = call(
        tangent_edge_kernel,
        "tangent_edge",
        [((80, 2 * CELLS), F32), ((512, 128), BF16), ((8, 128), F32)],
        [own, sides, from_left, from_right, inner, fwd1, fwd2, columns],
        limit=16,
    )
    near, far = across(payload, payload, -1)
    image, back_near, back_far = call(
        couple_kernel,
        "couple",
        [((80, CELLS), BF16), ((8, 128), F32), ((8, 128), F32)],
        [y, near, far, hot, picked, mask, columns],
    )
    back_near, back_far = across(back_near, back_far, 1)
    (result,) = call(unpack_kernel, "unpack", [((1, 80, ROWS, COLS), BF16)], [image])
    (cotangent,) = call(
        cotangent_kernel, "cotangent", [((80, CELLS), BF16)],
        [image, back_near, back_far, columns],
    )
    above, below = lat_pair(cotangent)
    to_left, to_right = call(
        edge_kernel, "edges_back", [((80, 128), BF16)] * 2,
        [cotangent, above, below, result],
        idle=1,
    )
    from_left, from_right = lon_pair(to_left, to_right)
    inner, sides = call(
        adjoint_main_kernel,
        "adjoint_main",
        [((80, 2 * CELLS), F32), ((2, 80, 128), F32)],
        [cotangent, above, below, to_left, to_right, bwd1, bwd2, slope],
        [pltpu.VMEM((240, 8 * COLS), BF16), pltpu.VMEM((512, 6 * COLS), BF16)],
        limit=16,
    )
    (product,) = call(
        adjoint_edge_kernel,
        "adjoint_edge",
        [((1, 80, ROWS, COLS), BF16)],
        [
            sides, from_left, from_right, inner, edge_slope, bwd1, bwd2,
            back_near, back_far,
        ],
        limit=16,
    )
    return result, product


def solution(mesh):
    return jax.shard_map(
        shards,
        mesh=mesh,
        in_specs=(
            P("comp", None, "lat", "lon"),
            P("comp", None, "lat", "lon"),
            P(),
            P(),
            P(),
            P(),
            P(),
            P(),
            P(),
            P(),
            P(),
            P("comp", None, "lat", "lon"),
            P("comp", None, "lat", "lon"),
            P(None, "lat", "lon"),
        ),
        out_specs=(P("comp", None, "lat", "lon"), P("comp", None, "lat", "lon")),
        check_vma=False,
    )
```

```python
import functools

import jax
import jax.numpy as jnp
from jax import lax
from jax.experimental import pallas as pl
from jax.experimental.pallas import tpu as pltpu
from jax.sharding import PartitionSpec as P

F32 = jnp.float32
BF16 = jnp.bfloat16
ROWS = 2
COLS = 256
CELLS = ROWS * COLS
SLOTS = 8


def is_air():
    return lax.axis_index("comp") == 0


def is_sea():
    return lax.axis_index("comp") != 0


def at_top():
    return lax.axis_index("lat") == 0


def at_bottom():
    return lax.axis_index("lat") == lax.axis_size("lat") - 1


def lane_iota(shape):
    return lax.broadcasted_iota(jnp.int32, shape, 1)


def split_parts(values):
    high = values.astype(BF16)
    low = (values - high.astype(F32)).astype(BF16)
    return jnp.concatenate([high, low], axis=0)


def dot(left, right):
    return lax.dot_general(left, right, (((1,), (0,)), ((), ())), preferred_element_type=F32)


def sources(own, above, below):
    upper = jnp.where(at_top(), 0.0, 1.0).astype(F32)
    lower = jnp.where(at_bottom(), 0.0, 1.0).astype(F32)
    chosen = []
    for ref, scale in ((above, upper), (own, None), (below, lower)):
        for r in range(ROWS):

            def read(part, start, stop, ref=ref, scale=scale, r=r):
                rows = ref[part, r * COLS + start : r * COLS + stop].astype(F32)
                return rows if scale is None else rows * scale

            chosen.append((read, r))
    return chosen


def pack_kernel(state, direction, packed, edge, rows, sems):
    copies = []
    for field, ref in enumerate((state, direction)):
        copies.append(pltpu.make_async_copy(ref.at[0], rows.at[field], sems.at[field]))
        copies[-1].start()
    line = lax.broadcasted_iota(jnp.int32, (160, 160), 0)
    place = lane_iota((160, 160))
    source = jnp.where(line < 80, 2 * line, 2 * line - 159)
    order = jnp.where(place == source, 1.0, 0.0).astype(BF16)
    for field, copy in enumerate(copies):
        copy.wait()
        block = dot(order, rows[field].reshape(160, COLS)).astype(BF16)
        for r in range(ROWS):
            packed[field * 80 : field * 80 + 80, r * COLS : (r + 1) * COLS] = block[r * 80 : (r + 1) * 80]
    edge[...] = own_edges(packed, 2)


def load_all(copies):
    for copy in copies[4:]:
        copy.start()

    @pl.when(is_air())
    def _():
        for copy in copies[:2]:
            copy.start()

    @pl.when(is_sea())
    def _():
        for copy in copies[2:4]:
            copy.start()

    for copy in copies[4:]:
        copy.wait()


def make_weights(to, back, flip, to_target, back_target):
    channels = to.shape[1]
    padded = -(-3 * channels // 16) * 16
    hidden = to.shape[2]
    pieces = []
    for a in range(3):
        for e in range(3):
            tap = 3 * a + e
            pieces.append(to[8 - tap if flip else tap].astype(F32))
        if padded > 3 * channels:
            pieces.append(jnp.zeros((padded - 3 * channels, hidden), F32))
    stacked = jnp.concatenate(pieces, axis=0)
    to_target[:hidden, : 3 * padded] = stacked.T.astype(BF16)
    for a in range(3):
        pieces = []
        for e in range(3):
            tap = 3 * a + e
            pieces.append(back[8 - tap if flip else tap].astype(F32))
        stacked = jnp.concatenate(pieces, axis=0)
        back_target[: 3 * channels, a * hidden : (a + 1) * hidden] = stacked.astype(BF16)


def both_weights(copies, held, flip, to_target, back_target):
    @pl.when(is_air())
    def _():
        for copy in copies[:2]:
            copy.wait()
        make_weights(held[0], held[1], flip, to_target, back_target)

    @pl.when(is_sea())
    def _():
        for copy in copies[2:4]:
            copy.wait()
        make_weights(held[2], held[3], flip, to_target, back_target)


def copies_of(sources, held, sems):
    return [
        pltpu.make_async_copy(source, target, sems.at[i])
        for i, (source, target) in enumerate(zip(sources, held))
    ]


def forward_kernel(*refs):
    fwd1, fwd2, columns = refs[10:13]
    held = refs[13:22]
    copies = copies_of(refs[:9], held, refs[22])
    load_all(copies)
    bias_a, bias_o, flux, aloft, forcing = held[4:]
    pad = jnp.zeros((1, 512 - 80), F32)
    bias = jnp.where(is_air(), bias_a[...], jnp.concatenate([bias_o[...]] * 2, axis=1))
    rows = [bias] + [jnp.concatenate([flux[f : f + 1, :].astype(F32), pad], axis=1) for f in range(2)]
    rows.append(jnp.concatenate([aloft[...], pad], axis=1))
    pad = jnp.zeros((1, 512 - 40), F32)
    rows += [jnp.concatenate([forcing[f : f + 1, :].astype(F32), pad], axis=1) for f in range(2)]
    rows.append(jnp.zeros((2, 512), F32))
    columns[...] = jnp.concatenate(rows, axis=0).T
    both_weights(copies, held, False, fwd1, fwd2)


def backward_kernel(*refs):
    bwd1, bwd2, hot, picked, mask = refs[8:13]
    held = refs[13:20]
    copies = copies_of(refs[:7], held, refs[20])
    load_all(copies)
    index, weight, land = held[4:]

    def flat(rows):
        return jnp.concatenate([rows[r : r + 1] for r in range(ROWS)], axis=1)

    table = jnp.concatenate([flat(weight[0, s]) for s in range(SLOTS)], axis=0).astype(F32)
    place = jnp.concatenate([flat(index[0, s]) for s in range(SLOTS)], axis=0)
    line = ((place >> 8) & 1) * 8 + (place >> 9) * 2 + ((place >> 7) & 1)
    rows16 = lax.broadcasted_iota(jnp.int32, (16, CELLS), 0)
    mask[...] = jnp.concatenate([flat(land[s]) for s in range(2)], axis=0).astype(F32)
    whole = jnp.sum(table, axis=0, keepdims=True)
    upper = jnp.sum(table[:4], axis=0, keepdims=True)
    slot_row = lax.broadcasted_iota(jnp.int32, table.shape, 0)
    grouped = jnp.where(slot_row < 4, upper, whole - upper)
    share = table / jnp.where(is_air(), whole, grouped)
    folded = jnp.where(is_air(), rows16, rows16 & 11)
    lanes = lax.broadcasted_iota(jnp.int32, (128, CELLS), 0)
    for slot in range(SLOTS):
        span = slice(slot * CELLS, (slot + 1) * CELLS)
        picked[:, span] = jnp.where(folded == line[slot : slot + 1], share[slot : slot + 1], 0.0)
        low = place[slot : slot + 1, :] & 127
        hot[:, span] = jnp.where(lanes == low, 1.0, 0.0).astype(BF16)
    both_weights(copies, held, True, bwd1, bwd2)


def own_edges(rows, fields):
    lanes = lane_iota((80, 128)) >> 1
    result = jnp.zeros((80, 128), F32)
    for field in range(fields):
        part = slice(field * 80, (field + 1) * 80)
        for r in range(ROWS):
            shift = 64 * field + 4 * (ROWS + r) + 2
            initial = rows[part, r * COLS : r * COLS + 128].astype(F32)
            last = rows[part, r * COLS + 128 : (r + 1) * COLS].astype(F32)
            result = jnp.where(lanes == shift // 2, pltpu.roll(initial, shift, 1), result)
            result = jnp.where(lanes == shift // 2 - 1, pltpu.roll(last, shift, 1), result)
    return result.astype(BF16)


def edge_kernel(own, above, below, merged):
    upper = jnp.where(at_top(), 0.0, 1.0).astype(F32)
    lower = jnp.where(at_bottom(), 0.0, 1.0).astype(F32)
    total = own[...].astype(F32) + pltpu.roll(above[...].astype(F32), 120, 1) * upper
    merged[...] = (total + pltpu.roll(below[...].astype(F32), 8, 1) * lower).astype(BF16)


def shifted_rows(main, fill):
    pieces = [pltpu.roll(main, 1, 1), main, pltpu.roll(main, COLS - 1, 1)]
    if fill:
        pieces.append(jnp.zeros((fill, COLS), F32))
    return jnp.concatenate(pieces, axis=0).astype(BF16)


def air_rows(own, above, below, fields, store):
    for field in range(fields):
        part = slice(field * 80, (field + 1) * 80)
        for place, (read, r) in enumerate(sources(own, above, below)):
            store(field, place, shifted_rows(read(part, 0, COLS), 0))


def sea_rows(own, above, below, fields, store):
    for field in range(fields):
        part = slice(field * 80, (field + 1) * 80)
        for place, (read, r) in enumerate(sources(own, above, below)):
            main = read(part, 0, COLS)
            for half in range(2):
                fine = 2 * (2 * (place // 2) + half - 1) + r
                if 0 <= fine < 8:
                    store(field, fine, shifted_rows(main[half * 40 : half * 40 + 40], 8))


def kept(rows, count, first_row):
    lanes = lane_iota((1, rows * COLS))
    row = first_row + lanes // COLS
    column = lanes % COLS
    drop = (column == 0) | (column == COLS - 1)
    drop = drop | (at_top() & (row == 0)) | (at_bottom() & (row == count - 1))
    return jnp.where(drop, 0.0, 1.0).astype(F32)


def edge_kept(count):
    lanes = lane_iota((1, 128))
    row = lanes >> 2
    drop = (row >= count) | (at_top() & (row == 0)) | (at_bottom() & (row == count - 1))
    return jnp.where(drop, 0.0, 1.0).astype(F32)


def fine_lanes(rows):
    lanes = (lane_iota((40, 128)) & 63) >> 3
    upper, lower = rows[:40], rows[40:]
    result = jnp.where(lanes == 0, lower, upper)
    result = jnp.where(lanes == 2, pltpu.roll(lower, 8, 1), result)
    return jnp.where(lanes == 3, pltpu.roll(upper, 8, 1), result)


def own_sides(edges, sides, fine):
    rows = edges[...].astype(F32)
    for i, shift in enumerate((2, 126)):
        side = pltpu.roll(rows, shift, 1)
        if fine:
            sides[i, :40, :] = fine_lanes(side)
        else:
            sides[i] = side


def edge_stack(sides, from_left, from_right, fine):
    both = []
    for i, ref in enumerate((from_left, from_right)):
        rows = ref[...].astype(F32)
        rows = fine_lanes(rows) if fine else rows
        side = sides[i, :40, :] if fine else sides[i]
        head = (lane_iota(rows.shape) & 3) < 2
        both.append(jnp.where(head, rows, side) if i == 0 else jnp.where(head, side, rows))
    before, after = both
    even = (lane_iota(before.shape) & 1) == 0
    middle = jnp.where(even, pltpu.roll(before, 127, 1), pltpu.roll(after, 1, 1))
    pieces = []
    for a in range(3):
        for rows in (before, middle, after):
            pieces.append(pltpu.roll(rows, 128 - 4 * a, 1) if a else rows)
        if fine:
            pieces.append(jnp.zeros((8, 128), F32))
    return jnp.concatenate(pieces, axis=0).astype(BF16)


def halved_dot(matrix, taps):
    half = matrix.shape[0] // 16 * 8
    return jnp.concatenate([dot(matrix[:half], taps), dot(matrix[half:], taps)], axis=0)


def inner_rows(weights, main, channels, width, count):
    matrix = weights[: 3 * channels, : 3 * width]
    result = []
    for pair in range(0, count, 2):
        pieces = [main[:width, (pair + a) * COLS : (pair + a + 2) * COLS] for a in range(3)]
        whole = dot(matrix, jnp.concatenate(pieces, axis=0))
        for row in range(2):
            cut = whole[:, row * COLS : (row + 1) * COLS]
            total = pltpu.roll(cut[:channels], 1, 1) + cut[channels : 2 * channels]
            result.append(total + pltpu.roll(cut[2 * channels :], COLS - 1, 1))
    return result


def outer_rows(weights, edge, channels, width, count):
    taps = edge.astype(BF16)
    block = dot(weights[: 3 * channels, :width], taps)
    for a in (1, 2):
        part = dot(weights[: 3 * channels, a * width : (a + 1) * width], taps)
        block = block + pltpu.roll(part, 128 - 4 * a, 1)
    first, middle, last = [block[e * channels : (e + 1) * channels] for e in range(3)]
    lanes = lane_iota((channels, 128))
    left = first + jnp.where((lanes & 3) == 0, pltpu.roll(middle, 127, 1), 0.0)
    right = last + jnp.where((lanes & 3) == 3, pltpu.roll(middle, 1, 1), 0.0)
    result = []
    for row in range(count):
        head = pltpu.roll(left, 128 - 4 * row, 1) if row else left
        head = jnp.where(lanes < 2, head, 0.0)
        tail = jnp.where(lanes >= 126, pltpu.roll(right, 124 - 4 * row, 1), 0.0)
        result.append(jnp.concatenate([head, tail], axis=1))
    return result


def tangent_main_kernel(
    own, above, below, edges, fwd1, fwd2, columns, inner, slope, sides, stack, hidden
):
    def run(channels, width, depth, count):
        padded = depth // 3
        for place in range(count):
            pieces = []
            for a in range(3):
                start = (place + a) * 2 * COLS
                pieces.append(stack[:padded, start : start + 2 * COLS])
            both = dot(fwd1[:width, :depth], jnp.concatenate(pieces, axis=0))
            steep = 1.0 - jnp.tanh(both[:, :COLS] + columns[:width, 0:1]) ** 2
            span = slice(place * COLS, (place + 1) * COLS)
            hidden[:width, span] = (steep * both[:, COLS:] * kept(1, count, place)).astype(BF16)
            slope[:width, span] = steep.astype(BF16)
        for row, result in enumerate(inner_rows(fwd2, hidden, channels, width, count - 2)):
            inner[:channels, row * COLS : (row + 1) * COLS] = result

    def store(field, place, rows):
        start = place * 2 * COLS + field * COLS
        stack[: rows.shape[0], start : start + COLS] = rows

    @pl.when(is_air())
    def _():
        own_sides(edges, sides, False)
        air_rows(own, above, below, 2, store)
        run(80, 512, 720, 4)

    @pl.when(is_sea())
    def _():
        own_sides(edges, sides, True)
        sea_rows(own, above, below, 2, store)
        run(40, 256, 384, 6)


def tangent_edge_kernel(
    own, sides, from_left, from_right, inner, fwd1, fwd2, columns,
    y, slope, payload,
):
    def run(channels, width, depth, count):
        stack = edge_stack(sides, from_left, from_right, channels == 40)
        both = halved_dot(fwd1[:width, :depth], stack)
        steep = 1.0 - jnp.tanh(both + columns[:width, 0:1]) ** 2
        slope[:width, :] = steep.astype(BF16)
        edge = steep * pltpu.roll(both, 64, 1) * edge_kept(count)
        rows = outer_rows(fwd2, edge, channels, width, count - 2)
        return [
            inner[:channels, i * COLS : (i + 1) * COLS] + row for i, row in enumerate(rows)
        ]

    @pl.when(is_air())
    def _():
        for r, result in enumerate(run(80, 512, 720, 4)):
            y[:, r * COLS : (r + 1) * COLS] = result
            for f in range(2):
                flux = jnp.sum(columns[:80, 1 + f : 2 + f] * result, axis=0, keepdims=True)
                for part in range(2):
                    line = f * 4 + r * 2 + part
                    payload[line : line + 1, :] = flux[:, part * 128 : (part + 1) * 128]

    @pl.when(is_sea())
    def _():
        for fine, result in enumerate(run(40, 256, 384, 6)):
            y[:40, fine * COLS : (fine + 1) * COLS] = result
            half, r = divmod(fine, 2)
            line = own[80 + 40 * half : 88 + 40 * half, r * COLS : (r + 1) * COLS].astype(F32)
            for part in range(2):
                place = fine * 2 + part
                payload[place : place + 1, :] = line[:1, part * 128 : (part + 1) * 128]


def couple_kernel(y, near, far, hot, picked, mask, columns, image, back_near, back_far):
    window = jnp.concatenate([near[...], far[...]], axis=0)
    parts = dot(split_parts(window), hot[...])

    def span(slot):
        return slice(slot * CELLS, (slot + 1) * CELLS)

    def gather(slots):
        total = None
        for slot in slots:
            chosen = (parts[:16, span(slot)] + parts[16:, span(slot)]) * picked[:, span(slot)]
            total = chosen if total is None else total + chosen
        return total[:8] + total[8:]

    def scatter(values):
        pieces = [picked[:, span(slot)] * values[slot // 4] for slot in range(SLOTS)]
        spread = split_parts(jnp.concatenate(pieces, axis=1))
        total = lax.dot_general(
            spread, hot[...], (((1,), (1,)), ((), ())), preferred_element_type=F32
        )
        total = total[:16] + total[16:]
        back_near[...] = total[:8]
        back_far[...] = total[8:]

    @pl.when(is_air())
    def _():
        aloft = columns[:80, 3:4]
        lifted = jnp.sum(gather(range(SLOTS)), axis=0, keepdims=True)
        rounded = (y[:, :CELLS] + aloft * lifted).astype(BF16)
        image[...] = rounded
        surface = jnp.sum(aloft * rounded.astype(F32), axis=0, keepdims=True)
        scatter([surface, surface])

    @pl.when(is_sea())
    def _():
        forcing_weight = columns[:40, 4:6]
        fields = (lax.broadcasted_iota(jnp.int32, (16, CELLS), 0) & 4) == 0
        halves = []
        pulled = []
        for half in range(2):
            folded = gather(range(4 * half, 4 * half + 4))
            forcing = [jnp.sum(folded[4 * f : 4 * f + 4], axis=0, keepdims=True) for f in range(2)]
            added = forcing_weight[:, :1] * forcing[0] + forcing_weight[:, 1:] * forcing[1]
            fine = mask[half : half + 1, :] * (y[:40, span(half)] + added)
            rounded = fine.astype(BF16).astype(F32)
            halves.append(rounded)
            first, other = [
                jnp.sum(forcing_weight[:, f : f + 1] * rounded, axis=0, keepdims=True) for f in range(2)
            ]
            pulled.append(jnp.where(fields, first, other))
        image[...] = jnp.concatenate(halves, axis=0).astype(BF16)
        scatter(pulled)


def cotangent_kernel(image, near, far, columns, after, cotangent, edge):
    @pl.when(is_air())
    def _():
        arrived = near[...] + far[...]
        total = image[...].astype(F32)
        for f in range(2):
            row = jnp.concatenate([arrived[f * 4 + q : f * 4 + q + 1, :] for q in range(4)], axis=1)
            total = total + columns[:80, 1 + f : 2 + f] * row
        cotangent[...] = total.astype(BF16)

    @pl.when(is_sea())
    def _():
        cotangent[...] = image[...]

    edge[...] = own_edges(cotangent, 1)


def spread_rows(target, rows):
    line = lax.broadcasted_iota(jnp.int32, (160, 160), 0)
    place = lane_iota((160, 160))
    order = jnp.where(place == (line & 1) * 80 + (line >> 1), 1.0, 0.0).astype(BF16)
    stacked = jnp.concatenate(rows, axis=0).astype(BF16)
    target[0] = dot(order, stacked).astype(BF16).reshape(80, ROWS, COLS)


def unpack_kernel(packed, image):
    wide = packed[...].astype(F32)
    spread_rows(image, [wide[:, r * COLS : (r + 1) * COLS] for r in range(ROWS)])


def adjoint_main_kernel(
    own, above, below, edges, bwd1, bwd2, slope, inner, sides, stack, hidden
):
    def run(channels, width, depth, count):
        padded = depth // 3
        for pair in range(0, count, 2):
            pieces = []
            for a in range(3):
                pieces.append(stack[:padded, (pair + a) * COLS : (pair + a + 2) * COLS])
            back = dot(bwd1[:width, :depth], jnp.concatenate(pieces, axis=0))
            span = slice(pair * COLS, (pair + 2) * COLS)
            back = back * slope[:width, span].astype(F32) * kept(2, count, pair)
            hidden[:width, span] = back.astype(BF16)
        for row, result in enumerate(inner_rows(bwd2, hidden, channels, width, count - 2)):
            inner[:channels, row * COLS : (row + 1) * COLS] = result

    def store(field, place, rows):
        stack[: rows.shape[0], place * COLS : (place + 1) * COLS] = rows

    @pl.when(is_air())
    def _():
        own_sides(edges, sides, False)
        air_rows(own, above, below, 1, store)
        run(80, 512, 720, 4)

    @pl.when(is_sea())
    def _():
        own_sides(edges, sides, True)
        sea_rows(own, above, below, 1, store)
        run(40, 256, 384, 6)


def adjoint_edge_kernel(
    sides, from_left, from_right, inner, slope, bwd1, bwd2, near, far, product
):
    def run(channels, width, depth, count):
        stack = edge_stack(sides, from_left, from_right, channels == 40)
        edge = halved_dot(bwd1[:width, :depth], stack)
        edge = edge * slope[:width, :].astype(F32)
        edge = jnp.where(edge_kept(count) > 0.0, edge, 0.0)
        rows = outer_rows(bwd2, edge, channels, width, count - 2)
        return [
            inner[:channels, i * COLS : (i + 1) * COLS] + row for i, row in enumerate(rows)
        ]

    @pl.when(is_air())
    def _():
        spread_rows(product, run(80, 512, 720, 4))

    @pl.when(is_sea())
    def _():
        results = run(40, 256, 384, 6)
        arrived = near[...] + far[...]
        channel = lax.broadcasted_iota(jnp.int32, (40, COLS), 0)
        rows = []
        for r in range(ROWS):
            halves = []
            for half in range(2):
                fine = 2 * half + r
                row = jnp.concatenate(
                    [arrived[2 * fine + q : 2 * fine + q + 1, :] for q in range(2)], axis=1
                )
                halves.append(results[fine] + jnp.where(channel == 0, row, 0.0))
            rows.append(jnp.concatenate(halves, axis=0))
        spread_rows(product, rows)


def call(kernel, name, out_shape, inputs, scratch=(), limit=8, stay=()):
    vmem = pl.BlockSpec(memory_space=pltpu.VMEM)
    hbm = pl.BlockSpec(memory_space=pltpu.HBM)
    inputs = [
        pltpu.with_memory_space_constraint(x, pltpu.HBM) if i in stay else x
        for i, x in enumerate(inputs)
    ]
    return pl.pallas_call(
        kernel,
        name=name,
        out_shape=tuple(jax.ShapeDtypeStruct(shape, dtype) for shape, dtype in out_shape),
        in_specs=[hbm if i in stay else vmem for i in range(len(inputs))],
        out_specs=tuple(vmem for _ in out_shape),
        scratch_shapes=list(scratch),
        compiler_params=pltpu.CompilerParams(vmem_limit_bytes=limit << 20),
    )(*inputs)


def lat_pair(block):
    count = lax.axis_size("lat")
    above = lax.ppermute(block, "lat", [(i, (i + 1) % count) for i in range(count)])
    below = lax.ppermute(block, "lat", [((i + 1) % count, i) for i in range(count)])
    return above, below


def lon_pair(block):
    count = lax.axis_size("lon")
    from_left = lax.ppermute(block, "lon", [(i, (i + 1) % count) for i in range(count)])
    from_right = lax.ppermute(block, "lon", [((i + 1) % count, i) for i in range(count)])
    return from_left, from_right


def across(near, far, shift):
    count = lax.axis_size("lon")
    same = lax.ppermute(near, "comp", [(0, 1), (1, 0)])
    route = []
    for part in range(2):
        for i in range(count):
            route.append((part * count + i, (1 - part) * count + (i + shift) % count))
    return same, lax.ppermute(far, ("comp", "lon"), route)


def shards(
    state,
    direction,
    air_first,
    air_bias,
    air_second,
    air_flux,
    aloft_reaction_to_seawarmth,
    sea_first,
    sea_bias,
    sea_second,
    sea_forcing,
    regrid_index,
    regrid_weight,
    land_mask,
):
    def held(arrays):
        buffers = [pltpu.VMEM(array.shape, array.dtype) for array in arrays]
        return buffers + [pltpu.SemaphoreType.DMA((len(arrays),))]

    block = ((80, 128), BF16)
    own, edge = call(
        pack_kernel,
        "pack",
        [((160, CELLS), BF16), block],
        [state, direction],
        [pltpu.VMEM((2, 80, ROWS, COLS), BF16), pltpu.SemaphoreType.DMA((2,))],
        stay=range(2),
    )
    edge_above, edge_below = lat_pair(edge)
    above, below = lat_pair(own)
    (edges,) = call(edge_kernel, "edges", [block], [edge, edge_above, edge_below])
    from_left, from_right = lon_pair(edges)
    first_a = air_first.transpose(0, 2, 1)
    first_o = sea_first.transpose(0, 2, 1)
    raw = [
        first_a,
        air_second,
        first_o,
        sea_second,
        air_bias.reshape(1, 512),
        sea_bias.reshape(1, 256),
        air_flux,
        aloft_reaction_to_seawarmth.reshape(1, 80),
        sea_forcing.T,
    ]
    fwd1, fwd2, columns = call(
        forward_kernel,
        "forward",
        [((512, 720), BF16), ((240, 1536), BF16), ((512, 8), F32)],
        raw + [edges],
        held(raw),
        limit=16,
        stay=range(len(raw)),
    )
    inner, slope, sides = call(
        tangent_main_kernel,
        "tangent_main",
        [((80, 2 * CELLS), F32), ((512, 6 * COLS), BF16), ((2, 80, 128), F32)],
        [own, above, below, edges, fwd1, fwd2, columns],
        [pltpu.VMEM((240, 16 * COLS), BF16), pltpu.VMEM((512, 6 * COLS), BF16)],
        limit=16,
    )
    y, edge_slope, payload = call(
        tangent_edge_kernel,
        "tangent_edge",
        [((80, 2 * CELLS), F32), ((512, 128), BF16), ((8, 128), F32)],
        [own, sides, from_left, from_right, inner, fwd1, fwd2, columns],
        limit=16,
    )
    near, far = across(payload, payload, -1)
    raw = [air_second, first_a, sea_second, first_o, regrid_index, regrid_weight, land_mask]
    bwd1, bwd2, hot, picked, mask = call(
        backward_kernel,
        "backward",
        [
            ((512, 720), BF16), ((240, 1536), BF16), ((128, SLOTS * CELLS), BF16),
            ((16, SLOTS * CELLS), F32), ((2, CELLS), F32),
        ],
        raw + [payload],
        held(raw),
        limit=16,
        stay=range(len(raw)),
    )
    image, back_near, back_far = call(
        couple_kernel,
        "couple",
        [((80, CELLS), BF16), ((8, 128), F32), ((8, 128), F32)],
        [y, near, far, hot, picked, mask, columns],
    )
    back_near, back_far = across(back_near, back_far, 1)
    (result,) = call(unpack_kernel, "unpack", [((1, 80, ROWS, COLS), BF16)], [image])
    cotangent, edge = call(
        cotangent_kernel,
        "cotangent",
        [((80, CELLS), BF16), block],
        [image, back_near, back_far, columns, result],
        stay=(4,),
    )
    edge_above, edge_below = lat_pair(edge)
    above, below = lat_pair(cotangent)
    (edges,) = call(edge_kernel, "edges_back", [block], [edge, edge_above, edge_below])
    from_left, from_right = lon_pair(edges)
    inner, sides = call(
        adjoint_main_kernel,
        "adjoint_main",
        [((80, 2 * CELLS), F32), ((2, 80, 128), F32)],
        [cotangent, above, below, edges, bwd1, bwd2, slope],
        [pltpu.VMEM((240, 8 * COLS), BF16), pltpu.VMEM((512, 6 * COLS), BF16)],
        limit=16,
    )
    (product,) = call(
        adjoint_edge_kernel,
        "adjoint_edge",
        [((1, 80, ROWS, COLS), BF16)],
        [sides, from_left, from_right, inner, edge_slope, bwd1, bwd2, back_near, back_far],
        limit=16,
    )
    return result, product


def solution(mesh):
    return jax.shard_map(
        shards,
        mesh=mesh,
        in_specs=(
            P("comp", None, "lat", "lon"),
            P("comp", None, "lat", "lon"),
            P(),
            P(),
            P(),
            P(),
            P(),
            P(),
            P(),
            P(),
            P(),
            P("comp", None, "lat", "lon"),
            P("comp", None, "lat", "lon"),
            P(None, "lat", "lon"),
        ),
        out_specs=(P("comp", None, "lat", "lon"), P("comp", None, "lat", "lon")),
        check_vma=False,
    )
```

```python
import jax
import jax.numpy as jnp
from jax import lax
from jax.experimental import pallas as pl
from jax.experimental.pallas import tpu as pltpu
from jax.sharding import PartitionSpec as P


F32 = jnp.float32
BF16 = jnp.bfloat16
ROWS = 2
COLS = 256
CELLS = ROWS * COLS
SLOTS = 8


def is_air():
    return lax.axis_index("comp") == 0


def is_sea():
    return lax.axis_index("comp") != 0


def at_top():
    return lax.axis_index("lat") == 0


def at_bottom():
    return lax.axis_index("lat") == lax.axis_size("lat") - 1


def lane_iota(shape):
    return lax.broadcasted_iota(jnp.int32, shape, 1)


def split_parts(values):
    high = values.astype(BF16)
    low = (values - high.astype(F32)).astype(BF16)
    return jnp.concatenate([high, low], axis=0)


def dot(left, right):
    return lax.dot_general(left, right, (((1,), (0,)), ((), ())), preferred_element_type=F32)


def sources(own, above, below):
    upper = jnp.where(at_top(), 0.0, 1.0).astype(F32)
    lower = jnp.where(at_bottom(), 0.0, 1.0).astype(F32)
    chosen = []
    for ref, scale in ((above, upper), (own, None), (below, lower)):
        for r in range(ROWS):

            def read(part, start, stop, ref=ref, scale=scale, r=r):
                rows = ref[part, r * COLS + start : r * COLS + stop].astype(F32)
                return rows if scale is None else rows * scale

            chosen.append((read, r))
    return chosen


def pack_kernel(state, direction, packed, edge, rows, sems):
    copies = []
    for field, ref in enumerate((state, direction)):
        copies.append(pltpu.make_async_copy(ref.at[0], rows.at[field], sems.at[field]))
        copies[-1].start()
    line = lax.broadcasted_iota(jnp.int32, (160, 160), 0)
    place = lane_iota((160, 160))
    source = jnp.where(line < 80, 2 * line, 2 * line - 159)
    order = jnp.where(place == source, 1.0, 0.0).astype(BF16)
    for field, copy in enumerate(copies):
        copy.wait()
        block = dot(order, rows[field].reshape(160, COLS)).astype(BF16)
        for r in range(ROWS):
            packed[field * 80 : field * 80 + 80, r * COLS : (r + 1) * COLS] = block[r * 80 : (r + 1) * 80]
    edge[...] = own_edges(packed, 2)


def load_all(copies):
    for copy in copies[4:]:
        copy.start()

    @pl.when(is_air())
    def _():
        for copy in copies[:2]:
            copy.start()

    @pl.when(is_sea())
    def _():
        for copy in copies[2:4]:
            copy.start()

    for copy in copies[4:]:
        copy.wait()


def make_weights(to, back, flip, to_target, back_target):
    channels = to.shape[1]
    padded = -(-3 * channels // 16) * 16
    hidden = to.shape[2]
    pieces = []
    for a in range(3):
        for e in range(3):
            tap = 3 * a + e
            pieces.append(to[8 - tap if flip else tap].astype(F32))
        if padded > 3 * channels:
            pieces.append(jnp.zeros((padded - 3 * channels, hidden), F32))
    stacked = jnp.concatenate(pieces, axis=0)
    to_target[:hidden, : 3 * padded] = stacked.T.astype(BF16)
    for a in range(3):
        pieces = []
        for e in range(3):
            tap = 3 * a + e
            pieces.append(back[8 - tap if flip else tap].astype(F32))
        stacked = jnp.concatenate(pieces, axis=0)
        back_target[: 3 * channels, a * hidden : (a + 1) * hidden] = stacked.astype(BF16)


def both_weights(copies, held, flip, to_target, back_target):
    @pl.when(is_air())
    def _():
        for copy in copies[:2]:
            copy.wait()
        make_weights(held[0], held[1], flip, to_target, back_target)

    @pl.when(is_sea())
    def _():
        for copy in copies[2:4]:
            copy.wait()
        make_weights(held[2], held[3], flip, to_target, back_target)


def copies_of(sources, held, sems):
    return [
        pltpu.make_async_copy(source, target, sems.at[i])
        for i, (source, target) in enumerate(zip(sources, held))
    ]


def forward_kernel(*refs):
    fwd1, fwd2, columns = refs[10:13]
    held = refs[13:22]
    copies = copies_of(refs[:9], held, refs[22])
    load_all(copies)
    bias_a, bias_o, flux, aloft, forcing = held[4:]
    pad = jnp.zeros((1, 512 - 80), F32)
    bias = jnp.where(is_air(), bias_a[...], jnp.concatenate([bias_o[...]] * 2, axis=1))
    rows = [bias] + [jnp.concatenate([flux[f : f + 1, :].astype(F32), pad], axis=1) for f in range(2)]
    rows.append(jnp.concatenate([aloft[...], pad], axis=1))
    pad = jnp.zeros((1, 512 - 40), F32)
    rows += [jnp.concatenate([forcing[f : f + 1, :].astype(F32), pad], axis=1) for f in range(2)]
    rows.append(jnp.zeros((2, 512), F32))
    columns[...] = jnp.concatenate(rows, axis=0).T
    both_weights(copies, held, False, fwd1, fwd2)


def backward_kernel(*refs):
    bwd1, bwd2, hot, picked, mask = refs[8:13]
    held = refs[13:20]
    copies = copies_of(refs[:7], held, refs[20])
    load_all(copies)
    index, weight, land = held[4:]

    def flat(rows):
        return jnp.concatenate([rows[r : r + 1] for r in range(ROWS)], axis=1)

    table = jnp.concatenate([flat(weight[0, s]) for s in range(SLOTS)], axis=0).astype(F32)
    place = jnp.concatenate([flat(index[0, s]) for s in range(SLOTS)], axis=0)
    line = ((place >> 8) & 1) * 8 + (place >> 9) * 2 + ((place >> 7) & 1)
    rows16 = lax.broadcasted_iota(jnp.int32, (16, CELLS), 0)
    mask[...] = jnp.concatenate([flat(land[s]) for s in range(2)], axis=0).astype(F32)
    whole = jnp.sum(table, axis=0, keepdims=True)
    upper = jnp.sum(table[:4], axis=0, keepdims=True)
    slot_row = lax.broadcasted_iota(jnp.int32, table.shape, 0)
    grouped = jnp.where(slot_row < 4, upper, whole - upper)
    share = table / jnp.where(is_air(), whole, grouped)
    folded = jnp.where(is_air(), rows16, rows16 & 11)
    lanes = lax.broadcasted_iota(jnp.int32, (128, CELLS), 0)
    for slot in range(SLOTS):
        span = slice(slot * CELLS, (slot + 1) * CELLS)
        picked[:, span] = jnp.where(folded == line[slot : slot + 1], share[slot : slot + 1], 0.0)
        low = place[slot : slot + 1, :] & 127
        hot[:, span] = jnp.where(lanes == low, 1.0, 0.0).astype(BF16)
    both_weights(copies, held, True, bwd1, bwd2)


def own_edges(rows, fields):
    lanes = lane_iota((80, 128)) >> 1
    result = jnp.zeros((80, 128), F32)
    for field in range(fields):
        part = slice(field * 80, (field + 1) * 80)
        for r in range(ROWS):
            shift = 64 * field + 4 * (ROWS + r) + 2
            initial = rows[part, r * COLS : r * COLS + 128].astype(F32)
            last = rows[part, r * COLS + 128 : (r + 1) * COLS].astype(F32)
            result = jnp.where(lanes == shift // 2, pltpu.roll(initial, shift, 1), result)
            result = jnp.where(lanes == shift // 2 - 1, pltpu.roll(last, shift, 1), result)
    return result.astype(BF16)


def edge_kernel(own, above, below, merged):
    upper = jnp.where(at_top(), 0.0, 1.0).astype(F32)
    lower = jnp.where(at_bottom(), 0.0, 1.0).astype(F32)
    total = own[...].astype(F32) + pltpu.roll(above[...].astype(F32), 120, 1) * upper
    merged[...] = (total + pltpu.roll(below[...].astype(F32), 8, 1) * lower).astype(BF16)


def shifted_rows(main, fill):
    pieces = [pltpu.roll(main, 1, 1), main, pltpu.roll(main, COLS - 1, 1)]
    if fill:
        pieces.append(jnp.zeros((fill, COLS), F32))
    return jnp.concatenate(pieces, axis=0).astype(BF16)


def air_rows(own, above, below, fields, store):
    for field in range(fields):
        part = slice(field * 80, (field + 1) * 80)
        for place, (read, r) in enumerate(sources(own, above, below)):
            store(field, place, shifted_rows(read(part, 0, COLS), 0))


def sea_rows(own, above, below, fields, store):
    for field in range(fields):
        part = slice(field * 80, (field + 1) * 80)
        for place, (read, r) in enumerate(sources(own, above, below)):
            main = read(part, 0, COLS)
            for half in range(2):
                fine = 2 * (2 * (place // 2) + half - 1) + r
                if 0 <= fine < 8:
                    store(field, fine, shifted_rows(main[half * 40 : half * 40 + 40], 8))


def kept(rows, count, first_row):
    lanes = lane_iota((1, rows * COLS))
    row = first_row + lanes // COLS
    column = lanes % COLS
    drop = (column == 0) | (column == COLS - 1)
    drop = drop | (at_top() & (row == 0)) | (at_bottom() & (row == count - 1))
    return jnp.where(drop, 0.0, 1.0).astype(F32)


def edge_kept(count):
    lanes = lane_iota((1, 128))
    row = lanes >> 2
    drop = (row >= count) | (at_top() & (row == 0)) | (at_bottom() & (row == count - 1))
    return jnp.where(drop, 0.0, 1.0).astype(F32)


def fine_lanes(rows):
    lanes = (lane_iota((40, 128)) & 63) >> 3
    upper, lower = rows[:40], rows[40:]
    result = jnp.where(lanes == 0, lower, upper)
    result = jnp.where(lanes == 2, pltpu.roll(lower, 8, 1), result)
    return jnp.where(lanes == 3, pltpu.roll(upper, 8, 1), result)


def own_sides(edges, sides, fine):
    rows = edges[...].astype(F32)
    for i, shift in enumerate((2, 126)):
        side = pltpu.roll(rows, shift, 1)
        if fine:
            sides[i, :40, :] = fine_lanes(side)
        else:
            sides[i] = side


def edge_stack(sides, from_left, from_right, fine):
    both = []
    for i, ref in enumerate((from_left, from_right)):
        rows = ref[...].astype(F32)
        rows = fine_lanes(rows) if fine else rows
        side = sides[i, :40, :] if fine else sides[i]
        head = (lane_iota(rows.shape) & 3) < 2
        both.append(jnp.where(head, rows, side) if i == 0 else jnp.where(head, side, rows))
    before, after = both
    even = (lane_iota(before.shape) & 1) == 0
    middle = jnp.where(even, pltpu.roll(before, 127, 1), pltpu.roll(after, 1, 1))
    pieces = []
    for a in range(3):
        for rows in (before, middle, after):
            pieces.append(pltpu.roll(rows, 128 - 4 * a, 1) if a else rows)
        if fine:
            pieces.append(jnp.zeros((8, 128), F32))
    return jnp.concatenate(pieces, axis=0).astype(BF16)


def halved_dot(matrix, taps):
    half = matrix.shape[0] // 16 * 8
    return jnp.concatenate([dot(matrix[:half], taps), dot(matrix[half:], taps)], axis=0)


def inner_rows(weights, main, channels, width, count):
    matrix = weights[: 3 * channels, : 3 * width]
    result = []
    for pair in range(0, count, 2):
        pieces = [main[:width, (pair + a) * COLS : (pair + a + 2) * COLS] for a in range(3)]
        whole = dot(matrix, jnp.concatenate(pieces, axis=0))
        for row in range(2):
            cut = whole[:, row * COLS : (row + 1) * COLS]
            total = pltpu.roll(cut[:channels], 1, 1) + cut[channels : 2 * channels]
            result.append(total + pltpu.roll(cut[2 * channels :], COLS - 1, 1))
    return result


def outer_rows(weights, edge, channels, width, count):
    taps = edge.astype(BF16)
    block = dot(weights[: 3 * channels, :width], taps)
    for a in (1, 2):
        part = dot(weights[: 3 * channels, a * width : (a + 1) * width], taps)
        block = block + pltpu.roll(part, 128 - 4 * a, 1)
    first, middle, last = [block[e * channels : (e + 1) * channels] for e in range(3)]
    lanes = lane_iota((channels, 128))
    left = first + jnp.where((lanes & 3) == 0, pltpu.roll(middle, 127, 1), 0.0)
    right = last + jnp.where((lanes & 3) == 3, pltpu.roll(middle, 1, 1), 0.0)
    result = []
    for row in range(count):
        head = pltpu.roll(left, 128 - 4 * row, 1) if row else left
        head = jnp.where(lanes < 2, head, 0.0)
        tail = jnp.where(lanes >= 126, pltpu.roll(right, 124 - 4 * row, 1), 0.0)
        result.append(jnp.concatenate([head, tail], axis=1))
    return result


def tangent_main_kernel(
    own, above, below, edges, fwd1, fwd2, columns, inner, slope, sides, stack, hidden
):
    def run(channels, width, depth, count):
        padded = depth // 3
        for place in range(count):
            pieces = []
            for a in range(3):
                start = (place + a) * 2 * COLS
                pieces.append(stack[:padded, start : start + 2 * COLS])
            both = dot(fwd1[:width, :depth], jnp.concatenate(pieces, axis=0))
            steep = 1.0 - jnp.tanh(both[:, :COLS] + columns[:width, 0:1]) ** 2
            span = slice(place * COLS, (place + 1) * COLS)
            hidden[:width, span] = (steep * both[:, COLS:] * kept(1, count, place)).astype(BF16)
            slope[:width, span] = steep.astype(BF16)
        for row, result in enumerate(inner_rows(fwd2, hidden, channels, width, count - 2)):
            inner[:channels, row * COLS : (row + 1) * COLS] = result

    def store(field, place, rows):
        start = place * 2 * COLS + field * COLS
        stack[: rows.shape[0], start : start + COLS] = rows

    @pl.when(is_air())
    def _():
        own_sides(edges, sides, False)
        air_rows(own, above, below, 2, store)
        run(80, 512, 720, 4)

    @pl.when(is_sea())
    def _():
        own_sides(edges, sides, True)
        sea_rows(own, above, below, 2, store)
        run(40, 256, 384, 6)


def tangent_edge_kernel(
    own, sides, from_left, from_right, inner, fwd1, fwd2, columns,
    y, slope, payload,
):
    def run(channels, width, depth, count):
        stack = edge_stack(sides, from_left, from_right, channels == 40)
        both = halved_dot(fwd1[:width, :depth], stack)
        steep = 1.0 - jnp.tanh(both + columns[:width, 0:1]) ** 2
        slope[:width, :] = steep.astype(BF16)
        edge = steep * pltpu.roll(both, 64, 1) * edge_kept(count)
        rows = outer_rows(fwd2, edge, channels, width, count - 2)
        return [
            inner[:channels, i * COLS : (i + 1) * COLS] + row for i, row in enumerate(rows)
        ]

    @pl.when(is_air())
    def _():
        for r, result in enumerate(run(80, 512, 720, 4)):
            y[:, r * COLS : (r + 1) * COLS] = result
            for f in range(2):
                flux = jnp.sum(columns[:80, 1 + f : 2 + f] * result, axis=0, keepdims=True)
                for part in range(2):
                    line = f * 4 + r * 2 + part
                    payload[line : line + 1, :] = flux[:, part * 128 : (part + 1) * 128]

    @pl.when(is_sea())
    def _():
        for fine, result in enumerate(run(40, 256, 384, 6)):
            y[:40, fine * COLS : (fine + 1) * COLS] = result
            half, r = divmod(fine, 2)
            line = own[80 + 40 * half : 88 + 40 * half, r * COLS : (r + 1) * COLS].astype(F32)
            for part in range(2):
                place = fine * 2 + part
                payload[place : place + 1, :] = line[:1, part * 128 : (part + 1) * 128]


def couple_kernel(y, near, far, hot, picked, mask, columns, image, back_near, back_far):
    window = jnp.concatenate([near[...], far[...]], axis=0)
    parts = dot(split_parts(window), hot[...])

    def span(slot):
        return slice(slot * CELLS, (slot + 1) * CELLS)

    def gather(slots):
        total = None
        for slot in slots:
            chosen = (parts[:16, span(slot)] + parts[16:, span(slot)]) * picked[:, span(slot)]
            total = chosen if total is None else total + chosen
        return total[:8] + total[8:]

    def scatter(values):
        pieces = [picked[:, span(slot)] * values[slot // 4] for slot in range(SLOTS)]
        spread = split_parts(jnp.concatenate(pieces, axis=1))
        total = lax.dot_general(
            spread, hot[...], (((1,), (1,)), ((), ())), preferred_element_type=F32
        )
        total = total[:16] + total[16:]
        back_near[...] = total[:8]
        back_far[...] = total[8:]

    @pl.when(is_air())
    def _():
        aloft = columns[:80, 3:4]
        lifted = jnp.sum(gather(range(SLOTS)), axis=0, keepdims=True)
        rounded = (y[:, :CELLS] + aloft * lifted).astype(BF16)
        image[...] = rounded
        surface = jnp.sum(aloft * rounded.astype(F32), axis=0, keepdims=True)
        scatter([surface, surface])

    @pl.when(is_sea())
    def _():
        forcing_weight = columns[:40, 4:6]
        fields = (lax.broadcasted_iota(jnp.int32, (16, CELLS), 0) & 4) == 0
        halves = []
        pulled = []
        for half in range(2):
            folded = gather(range(4 * half, 4 * half + 4))
            forcing = [jnp.sum(folded[4 * f : 4 * f + 4], axis=0, keepdims=True) for f in range(2)]
            added = forcing_weight[:, :1] * forcing[0] + forcing_weight[:, 1:] * forcing[1]
            fine = mask[half : half + 1, :] * (y[:40, span(half)] + added)
            rounded = fine.astype(BF16).astype(F32)
            halves.append(rounded)
            first, other = [
                jnp.sum(forcing_weight[:, f : f + 1] * rounded, axis=0, keepdims=True) for f in range(2)
            ]
            pulled.append(jnp.where(fields, first, other))
        image[...] = jnp.concatenate(halves, axis=0).astype(BF16)
        scatter(pulled)


def cotangent_kernel(image, near, far, columns, after, cotangent, edge):
    @pl.when(is_air())
    def _():
        arrived = near[...] + far[...]
        total = image[...].astype(F32)
        for f in range(2):
            row = jnp.concatenate([arrived[f * 4 + q : f * 4 + q + 1, :] for q in range(4)], axis=1)
            total = total + columns[:80, 1 + f : 2 + f] * row
        cotangent[...] = total.astype(BF16)

    @pl.when(is_sea())
    def _():
        cotangent[...] = image[...]

    edge[...] = own_edges(cotangent, 1)


def spread_rows(target, rows):
    line = lax.broadcasted_iota(jnp.int32, (160, 160), 0)
    place = lane_iota((160, 160))
    order = jnp.where(place == (line & 1) * 80 + (line >> 1), 1.0, 0.0).astype(BF16)
    stacked = jnp.concatenate(rows, axis=0).astype(BF16)
    target[0] = dot(order, stacked).astype(BF16).reshape(80, ROWS, COLS)


def unpack_kernel(packed, image):
    wide = packed[...].astype(F32)
    spread_rows(image, [wide[:, r * COLS : (r + 1) * COLS] for r in range(ROWS)])


def adjoint_main_kernel(
    own, above, below, edges, bwd1, bwd2, slope, inner, sides, stack, hidden
):
    def run(channels, width, depth, count):
        padded = depth // 3
        for pair in range(0, count, 2):
            pieces = []
            for a in range(3):
                pieces.append(stack[:padded, (pair + a) * COLS : (pair + a + 2) * COLS])
            back = dot(bwd1[:width, :depth], jnp.concatenate(pieces, axis=0))
            span = slice(pair * COLS, (pair + 2) * COLS)
            back = back * slope[:width, span].astype(F32) * kept(2, count, pair)
            hidden[:width, span] = back.astype(BF16)
        for row, result in enumerate(inner_rows(bwd2, hidden, channels, width, count - 2)):
            inner[:channels, row * COLS : (row + 1) * COLS] = result

    def store(field, place, rows):
        stack[: rows.shape[0], place * COLS : (place + 1) * COLS] = rows

    @pl.when(is_air())
    def _():
        own_sides(edges, sides, False)
        air_rows(own, above, below, 1, store)
        run(80, 512, 720, 4)

    @pl.when(is_sea())
    def _():
        own_sides(edges, sides, True)
        sea_rows(own, above, below, 1, store)
        run(40, 256, 384, 6)


def adjoint_edge_kernel(
    sides, from_left, from_right, inner, slope, bwd1, bwd2, near, far, product
):
    def run(channels, width, depth, count):
        stack = edge_stack(sides, from_left, from_right, channels == 40)
        edge = halved_dot(bwd1[:width, :depth], stack)
        edge = edge * slope[:width, :].astype(F32)
        edge = jnp.where(edge_kept(count) > 0.0, edge, 0.0)
        rows = outer_rows(bwd2, edge, channels, width, count - 2)
        return [
            inner[:channels, i * COLS : (i + 1) * COLS] + row for i, row in enumerate(rows)
        ]

    @pl.when(is_air())
    def _():
        spread_rows(product, run(80, 512, 720, 4))

    @pl.when(is_sea())
    def _():
        results = run(40, 256, 384, 6)
        arrived = near[...] + far[...]
        channel = lax.broadcasted_iota(jnp.int32, (40, COLS), 0)
        rows = []
        for r in range(ROWS):
            halves = []
            for half in range(2):
                fine = 2 * half + r
                row = jnp.concatenate(
                    [arrived[2 * fine + q : 2 * fine + q + 1, :] for q in range(2)], axis=1
                )
                halves.append(results[fine] + jnp.where(channel == 0, row, 0.0))
            rows.append(jnp.concatenate(halves, axis=0))
        spread_rows(product, rows)


def call(kernel, out_shape, inputs, scratch=(), limit=8, stay=()):
    vmem = pl.BlockSpec(memory_space=pltpu.VMEM)
    hbm = pl.BlockSpec(memory_space=pltpu.HBM)
    inputs = [
        pltpu.with_memory_space_constraint(x, pltpu.HBM) if i in stay else x
        for i, x in enumerate(inputs)
    ]
    return pl.pallas_call(
        kernel,
        out_shape=tuple(jax.ShapeDtypeStruct(shape, dtype) for shape, dtype in out_shape),
        in_specs=[hbm if i in stay else vmem for i in range(len(inputs))],
        out_specs=tuple(vmem for _ in out_shape),
        scratch_shapes=list(scratch),
        compiler_params=pltpu.CompilerParams(vmem_limit_bytes=limit << 20),
    )(*inputs)


def lat_pair(block):
    count = lax.axis_size("lat")
    above = lax.ppermute(block, "lat", [(i, (i + 1) % count) for i in range(count)])
    below = lax.ppermute(block, "lat", [((i + 1) % count, i) for i in range(count)])
    return above, below


def lon_pair(block):
    count = lax.axis_size("lon")
    from_left = lax.ppermute(block, "lon", [(i, (i + 1) % count) for i in range(count)])
    from_right = lax.ppermute(block, "lon", [((i + 1) % count, i) for i in range(count)])
    return from_left, from_right


def across(near, far, shift):
    count = lax.axis_size("lon")
    same = lax.ppermute(near, "comp", [(0, 1), (1, 0)])
    route = []
    for part in range(2):
        for i in range(count):
            route.append((part * count + i, (1 - part) * count + (i + shift) % count))
    return same, lax.ppermute(far, ("comp", "lon"), route)


def shards(
    state,
    direction,
    air_first,
    air_bias,
    air_second,
    air_flux,
    aloft_reaction_to_seawarmth,
    sea_first,
    sea_bias,
    sea_second,
    sea_forcing,
    regrid_index,
    regrid_weight,
    land_mask,
):
    def held(arrays):
        buffers = [pltpu.VMEM(array.shape, array.dtype) for array in arrays]
        return buffers + [pltpu.SemaphoreType.DMA((len(arrays),))]

    block = ((80, 128), BF16)
    own, edge = call(
        pack_kernel,
        [((160, CELLS), BF16), block],
        [state, direction],
        [pltpu.VMEM((2, 80, ROWS, COLS), BF16), pltpu.SemaphoreType.DMA((2,))],
        stay=range(2),
    )
    edge_above, edge_below = lat_pair(edge)
    above, below = lat_pair(own)
    (edges,) = call(edge_kernel, [block], [edge, edge_above, edge_below])
    from_left, from_right = lon_pair(edges)
    first_a = air_first.transpose(0, 2, 1)
    first_o = sea_first.transpose(0, 2, 1)
    raw = [
        first_a,
        air_second,
        first_o,
        sea_second,
        air_bias.reshape(1, 512),
        sea_bias.reshape(1, 256),
        air_flux,
        aloft_reaction_to_seawarmth.reshape(1, 80),
        sea_forcing.T,
    ]
    fwd1, fwd2, columns = call(
        forward_kernel,
        [((512, 720), BF16), ((240, 1536), BF16), ((512, 8), F32)],
        raw + [edges],
        held(raw),
        limit=16,
        stay=range(len(raw)),
    )
    inner, slope, sides = call(
        tangent_main_kernel,
        [((80, 2 * CELLS), F32), ((512, 6 * COLS), BF16), ((2, 80, 128), F32)],
        [own, above, below, edges, fwd1, fwd2, columns],
        [pltpu.VMEM((240, 16 * COLS), BF16), pltpu.VMEM((512, 6 * COLS), BF16)],
        limit=16,
    )
    y, edge_slope, payload = call(
        tangent_edge_kernel,
        [((80, 2 * CELLS), F32), ((512, 128), BF16), ((8, 128), F32)],
        [own, sides, from_left, from_right, inner, fwd1, fwd2, columns],
        limit=16,
    )
    near, far = across(payload, payload, -1)
    raw = [air_second, first_a, sea_second, first_o, regrid_index, regrid_weight, land_mask]
    bwd1, bwd2, hot, picked, mask = call(
        backward_kernel,
        [
            ((512, 720), BF16), ((240, 1536), BF16), ((128, SLOTS * CELLS), BF16),
            ((16, SLOTS * CELLS), F32), ((2, CELLS), F32),
        ],
        raw + [payload],
        held(raw),
        limit=16,
        stay=range(len(raw)),
    )
    image, back_near, back_far = call(
        couple_kernel,
        [((80, CELLS), BF16), ((8, 128), F32), ((8, 128), F32)],
        [y, near, far, hot, picked, mask, columns],
    )
    back_near, back_far = across(back_near, back_far, 1)
    (result,) = call(unpack_kernel, [((1, 80, ROWS, COLS), BF16)], [image])
    cotangent, edge = call(
        cotangent_kernel,
        [((80, CELLS), BF16), block],
        [image, back_near, back_far, columns, result],
        stay=(4,),
    )
    edge_above, edge_below = lat_pair(edge)
    above, below = lat_pair(cotangent)
    (edges,) = call(edge_kernel, [block], [edge, edge_above, edge_below])
    from_left, from_right = lon_pair(edges)
    inner, sides = call(
        adjoint_main_kernel,
        [((80, 2 * CELLS), F32), ((2, 80, 128), F32)],
        [cotangent, above, below, edges, bwd1, bwd2, slope],
        [pltpu.VMEM((240, 8 * COLS), BF16), pltpu.VMEM((512, 6 * COLS), BF16)],
        limit=16,
    )
    (product,) = call(
        adjoint_edge_kernel,
        [((1, 80, ROWS, COLS), BF16)],
        [sides, from_left, from_right, inner, edge_slope, bwd1, bwd2, back_near, back_far],
        limit=16,
    )
    return result, product


def solution(mesh):
    return jax.shard_map(
        shards,
        mesh=mesh,
        in_specs=(
            P("comp", None, "lat", "lon"),
            P("comp", None, "lat", "lon"),
            P(),
            P(),
            P(),
            P(),
            P(),
            P(),
            P(),
            P(),
            P(),
            P("comp", None, "lat", "lon"),
            P("comp", None, "lat", "lon"),
            P(None, "lat", "lon"),
        ),
        out_specs=(P("comp", None, "lat", "lon"), P("comp", None, "lat", "lon")),
        check_vma=False,
    )
```

```python
import jax
import jax.numpy as jnp
from jax import lax
from jax.experimental import pallas as pl
from jax.experimental.pallas import tpu as pltpu
from jax.sharding import PartitionSpec as P


F32 = jnp.float32
BF16 = jnp.bfloat16
ROWS = 2
COLS = 256
CELLS = ROWS * COLS
SLOTS = 8


def is_air():
    return lax.axis_index("comp") == 0


def is_sea():
    return lax.axis_index("comp") != 0


def at_top():
    return lax.axis_index("lat") == 0


def at_bottom():
    return lax.axis_index("lat") == lax.axis_size("lat") - 1


def lane_iota(shape):
    return lax.broadcasted_iota(jnp.int32, shape, 1)


def split_parts(values):
    high = values.astype(BF16)
    low = (values - high.astype(F32)).astype(BF16)
    return jnp.concatenate([high, low], axis=0)


def dot(left, right):
    return lax.dot_general(left, right, (((1,), (0,)), ((), ())), preferred_element_type=F32)


def sources(own, above, below):
    upper = jnp.where(at_top(), 0.0, 1.0).astype(F32)
    lower = jnp.where(at_bottom(), 0.0, 1.0).astype(F32)
    chosen = []
    for ref, scale in ((above, upper), (own, None), (below, lower)):
        for r in range(ROWS):

            def read(part, start, stop, ref=ref, scale=scale, r=r):
                rows = ref[part, r * COLS + start : r * COLS + stop].astype(F32)
                return rows if scale is None else rows * scale

            chosen.append((read, r))
    return chosen


def pack_kernel(state, direction, packed, edge, rows, sems):
    copies = []
    for field, ref in enumerate((state, direction)):
        copies.append(pltpu.make_async_copy(ref.at[0], rows.at[field], sems.at[field]))
        copies[-1].start()
    line = lax.broadcasted_iota(jnp.int32, (160, 160), 0)
    place = lane_iota((160, 160))
    source = jnp.where(line < 80, 2 * line, 2 * line - 159)
    order = jnp.where(place == source, 1.0, 0.0).astype(BF16)
    for field, copy in enumerate(copies):
        copy.wait()
        block = dot(order, rows[field].reshape(160, COLS)).astype(BF16)
        for r in range(ROWS):
            packed[field * 80 : field * 80 + 80, r * COLS : (r + 1) * COLS] = block[r * 80 : (r + 1) * 80]
    edge[...] = own_edges(packed, 2)


def load_all(copies):
    for copy in copies[4:]:
        copy.start()

    @pl.when(is_air())
    def _():
        for copy in copies[:2]:
            copy.start()

    @pl.when(is_sea())
    def _():
        for copy in copies[2:4]:
            copy.start()

    for copy in copies[4:]:
        copy.wait()


def make_weights(to, back, flip, to_target, back_target):
    channels = to.shape[1]
    padded = -(-3 * channels // 16) * 16
    hidden = to.shape[2]
    pieces = []
    for a in range(3):
        for e in range(3):
            tap = 3 * a + e
            pieces.append(to[8 - tap if flip else tap].astype(F32))
        if padded > 3 * channels:
            pieces.append(jnp.zeros((padded - 3 * channels, hidden), F32))
    stacked = jnp.concatenate(pieces, axis=0)
    to_target[:hidden, : 3 * padded] = stacked.T.astype(BF16)
    for a in range(3):
        pieces = []
        for e in range(3):
            tap = 3 * a + e
            pieces.append(back[8 - tap if flip else tap].astype(F32))
        stacked = jnp.concatenate(pieces, axis=0)
        back_target[: 3 * channels, a * hidden : (a + 1) * hidden] = stacked.astype(BF16)


def both_weights(copies, held, flip, to_target, back_target):
    @pl.when(is_air())
    def _():
        for copy in copies[:2]:
            copy.wait()
        make_weights(held[0], held[1], flip, to_target, back_target)

    @pl.when(is_sea())
    def _():
        for copy in copies[2:4]:
            copy.wait()
        make_weights(held[2], held[3], flip, to_target, back_target)


def copies_of(sources, held, sems):
    return [
        pltpu.make_async_copy(source, target, sems.at[i])
        for i, (source, target) in enumerate(zip(sources, held))
    ]


def forward_kernel(*refs):
    fwd1, fwd2, columns = refs[10:13]
    held = refs[13:22]
    copies = copies_of(refs[:9], held, refs[22])
    load_all(copies)
    bias_a, bias_o, flux, aloft, forcing = held[4:]
    pad = jnp.zeros((1, 512 - 80), F32)
    bias = jnp.where(is_air(), bias_a[...], jnp.concatenate([bias_o[...]] * 2, axis=1))
    rows = [bias] + [jnp.concatenate([flux[f : f + 1, :].astype(F32), pad], axis=1) for f in range(2)]
    rows.append(jnp.concatenate([aloft[...], pad], axis=1))
    pad = jnp.zeros((1, 512 - 40), F32)
    rows += [jnp.concatenate([forcing[f : f + 1, :].astype(F32), pad], axis=1) for f in range(2)]
    rows.append(jnp.zeros((2, 512), F32))
    columns[...] = jnp.concatenate(rows, axis=0).T
    both_weights(copies, held, False, fwd1, fwd2)


def backward_kernel(*refs):
    bwd1, bwd2, hot, picked, mask = refs[8:13]
    held = refs[13:20]
    copies = copies_of(refs[:7], held, refs[20])
    load_all(copies)
    index, weight, land = held[4:]

    def flat(rows):
        return jnp.concatenate([rows[r : r + 1] for r in range(ROWS)], axis=1)

    table = jnp.concatenate([flat(weight[0, s]) for s in range(SLOTS)], axis=0).astype(F32)
    place = jnp.concatenate([flat(index[0, s]) for s in range(SLOTS)], axis=0)
    line = ((place >> 8) & 1) * 8 + (place >> 9) * 2 + ((place >> 7) & 1)
    rows16 = lax.broadcasted_iota(jnp.int32, (16, CELLS), 0)
    mask[...] = jnp.concatenate([flat(land[s]) for s in range(2)], axis=0).astype(F32)
    whole = jnp.sum(table, axis=0, keepdims=True)
    upper = jnp.sum(table[:4], axis=0, keepdims=True)
    slot_row = lax.broadcasted_iota(jnp.int32, table.shape, 0)
    grouped = jnp.where(slot_row < 4, upper, whole - upper)
    share = table / jnp.where(is_air(), whole, grouped)
    folded = jnp.where(is_air(), rows16, rows16 & 11)
    lanes = lax.broadcasted_iota(jnp.int32, (128, CELLS), 0)
    for slot in range(SLOTS):
        span = slice(slot * CELLS, (slot + 1) * CELLS)
        picked[:, span] = jnp.where(folded == line[slot : slot + 1], share[slot : slot + 1], 0.0)
        low = place[slot : slot + 1, :] & 127
        hot[:, span] = jnp.where(lanes == low, 1.0, 0.0).astype(BF16)
    both_weights(copies, held, True, bwd1, bwd2)


def own_edges(rows, fields):
    lanes = lane_iota((80, 128)) >> 1
    result = jnp.zeros((80, 128), F32)
    for field in range(fields):
        part = slice(field * 80, (field + 1) * 80)
        for r in range(ROWS):
            shift = 64 * field + 4 * (ROWS + r) + 2
            initial = rows[part, r * COLS : r * COLS + 128].astype(F32)
            last = rows[part, r * COLS + 128 : (r + 1) * COLS].astype(F32)
            result = jnp.where(lanes == shift // 2, pltpu.roll(initial, shift, 1), result)
            result = jnp.where(lanes == shift // 2 - 1, pltpu.roll(last, shift, 1), result)
    return result.astype(BF16)


def edge_kernel(own, above, below, after, merged):
    upper = jnp.where(at_top(), 0.0, 1.0).astype(F32)
    lower = jnp.where(at_bottom(), 0.0, 1.0).astype(F32)
    total = own[...].astype(F32) + pltpu.roll(above[...].astype(F32), 120, 1) * upper
    merged[...] = (total + pltpu.roll(below[...].astype(F32), 8, 1) * lower).astype(BF16)


def shifted_rows(main, fill):
    pieces = [pltpu.roll(main, 1, 1), main, pltpu.roll(main, COLS - 1, 1)]
    if fill:
        pieces.append(jnp.zeros((fill, COLS), F32))
    return jnp.concatenate(pieces, axis=0).astype(BF16)


def air_rows(own, above, below, fields, store):
    for field in range(fields):
        part = slice(field * 80, (field + 1) * 80)
        for place, (read, r) in enumerate(sources(own, above, below)):
            store(field, place, shifted_rows(read(part, 0, COLS), 0))


def sea_rows(own, above, below, fields, store):
    for field in range(fields):
        part = slice(field * 80, (field + 1) * 80)
        for place, (read, r) in enumerate(sources(own, above, below)):
            main = read(part, 0, COLS)
            for half in range(2):
                fine = 2 * (2 * (place // 2) + half - 1) + r
                if 0 <= fine < 8:
                    store(field, fine, shifted_rows(main[half * 40 : half * 40 + 40], 8))


def kept(rows, count, first_row):
    lanes = lane_iota((1, rows * COLS))
    row = first_row + lanes // COLS
    column = lanes % COLS
    drop = (column == 0) | (column == COLS - 1)
    drop = drop | (at_top() & (row == 0)) | (at_bottom() & (row == count - 1))
    return jnp.where(drop, 0.0, 1.0).astype(F32)


def edge_kept(count):
    lanes = lane_iota((1, 128))
    row = lanes >> 2
    drop = (row >= count) | (at_top() & (row == 0)) | (at_bottom() & (row == count - 1))
    return jnp.where(drop, 0.0, 1.0).astype(F32)


def fine_lanes(rows):
    lanes = (lane_iota((40, 128)) & 63) >> 3
    upper, lower = rows[:40], rows[40:]
    result = jnp.where(lanes == 0, lower, upper)
    result = jnp.where(lanes == 2, pltpu.roll(lower, 8, 1), result)
    return jnp.where(lanes == 3, pltpu.roll(upper, 8, 1), result)


def own_sides(edges, sides, fine):
    rows = edges[...].astype(F32)
    for i, shift in enumerate((2, 126)):
        side = pltpu.roll(rows, shift, 1)
        if fine:
            sides[i, :40, :] = fine_lanes(side)
        else:
            sides[i] = side


def edge_stack(sides, from_left, from_right, fine):
    both = []
    for i, ref in enumerate((from_left, from_right)):
        rows = ref[...].astype(F32)
        rows = fine_lanes(rows) if fine else rows
        side = sides[i, :40, :] if fine else sides[i]
        head = (lane_iota(rows.shape) & 3) < 2
        both.append(jnp.where(head, rows, side) if i == 0 else jnp.where(head, side, rows))
    before, after = both
    even = (lane_iota(before.shape) & 1) == 0
    middle = jnp.where(even, pltpu.roll(before, 127, 1), pltpu.roll(after, 1, 1))
    pieces = []
    for a in range(3):
        for rows in (before, middle, after):
            pieces.append(pltpu.roll(rows, 128 - 4 * a, 1) if a else rows)
        if fine:
            pieces.append(jnp.zeros((8, 128), F32))
    return jnp.concatenate(pieces, axis=0).astype(BF16)


def halved_dot(matrix, taps):
    half = matrix.shape[0] // 16 * 8
    return jnp.concatenate([dot(matrix[:half], taps), dot(matrix[half:], taps)], axis=0)


def inner_rows(weights, main, channels, width, count):
    matrix = weights[: 3 * channels, : 3 * width]
    result = []
    for pair in range(0, count, 2):
        pieces = [main[:width, (pair + a) * COLS : (pair + a + 2) * COLS] for a in range(3)]
        whole = dot(matrix, jnp.concatenate(pieces, axis=0))
        for row in range(2):
            cut = whole[:, row * COLS : (row + 1) * COLS]
            total = pltpu.roll(cut[:channels], 1, 1) + cut[channels : 2 * channels]
            result.append(total + pltpu.roll(cut[2 * channels :], COLS - 1, 1))
    return result


def outer_rows(weights, edge, channels, width, count):
    taps = edge.astype(BF16)
    block = dot(weights[: 3 * channels, :width], taps)
    for a in (1, 2):
        part = dot(weights[: 3 * channels, a * width : (a + 1) * width], taps)
        block = block + pltpu.roll(part, 128 - 4 * a, 1)
    first, middle, last = [block[e * channels : (e + 1) * channels] for e in range(3)]
    lanes = lane_iota((channels, 128))
    left = first + jnp.where((lanes & 3) == 0, pltpu.roll(middle, 127, 1), 0.0)
    right = last + jnp.where((lanes & 3) == 3, pltpu.roll(middle, 1, 1), 0.0)
    result = []
    for row in range(count):
        head = pltpu.roll(left, 128 - 4 * row, 1) if row else left
        head = jnp.where(lanes < 2, head, 0.0)
        tail = jnp.where(lanes >= 126, pltpu.roll(right, 124 - 4 * row, 1), 0.0)
        result.append(jnp.concatenate([head, tail], axis=1))
    return result


def tangent_main_kernel(
    own, above, below, edges, fwd1, fwd2, columns, inner, slope, sides, stack, hidden
):
    def run(channels, width, depth, count):
        padded = depth // 3
        for place in range(count):
            pieces = []
            for a in range(3):
                start = (place + a) * 2 * COLS
                pieces.append(stack[:padded, start : start + 2 * COLS])
            both = dot(fwd1[:width, :depth], jnp.concatenate(pieces, axis=0))
            steep = 1.0 - jnp.tanh(both[:, :COLS] + columns[:width, 0:1]) ** 2
            span = slice(place * COLS, (place + 1) * COLS)
            hidden[:width, span] = (steep * both[:, COLS:] * kept(1, count, place)).astype(BF16)
            slope[:width, span] = steep.astype(BF16)
        for row, result in enumerate(inner_rows(fwd2, hidden, channels, width, count - 2)):
            inner[:channels, row * COLS : (row + 1) * COLS] = result

    def store(field, place, rows):
        start = place * 2 * COLS + field * COLS
        stack[: rows.shape[0], start : start + COLS] = rows

    @pl.when(is_air())
    def _():
        own_sides(edges, sides, False)
        air_rows(own, above, below, 2, store)
        run(80, 512, 720, 4)

    @pl.when(is_sea())
    def _():
        own_sides(edges, sides, True)
        sea_rows(own, above, below, 2, store)
        run(40, 256, 384, 6)


def tangent_edge_kernel(
    own, sides, from_left, from_right, inner, fwd1, fwd2, columns,
    y, slope, payload,
):
    def run(channels, width, depth, count):
        stack = edge_stack(sides, from_left, from_right, channels == 40)
        both = halved_dot(fwd1[:width, :depth], stack)
        steep = 1.0 - jnp.tanh(both + columns[:width, 0:1]) ** 2
        slope[:width, :] = steep.astype(BF16)
        edge = steep * pltpu.roll(both, 64, 1) * edge_kept(count)
        rows = outer_rows(fwd2, edge, channels, width, count - 2)
        return [
            inner[:channels, i * COLS : (i + 1) * COLS] + row for i, row in enumerate(rows)
        ]

    @pl.when(is_air())
    def _():
        for r, result in enumerate(run(80, 512, 720, 4)):
            y[:, r * COLS : (r + 1) * COLS] = result
            for f in range(2):
                flux = jnp.sum(columns[:80, 1 + f : 2 + f] * result, axis=0, keepdims=True)
                for part in range(2):
                    line = f * 4 + r * 2 + part
                    payload[line : line + 1, :] = flux[:, part * 128 : (part + 1) * 128]

    @pl.when(is_sea())
    def _():
        for fine, result in enumerate(run(40, 256, 384, 6)):
            y[:40, fine * COLS : (fine + 1) * COLS] = result
            half, r = divmod(fine, 2)
            line = own[80 + 40 * half : 88 + 40 * half, r * COLS : (r + 1) * COLS].astype(F32)
            for part in range(2):
                place = fine * 2 + part
                payload[place : place + 1, :] = line[:1, part * 128 : (part + 1) * 128]


def couple_kernel(y, near, far, hot, picked, mask, columns, image, back_near, back_far):
    window = jnp.concatenate([near[...], far[...]], axis=0)
    parts = dot(split_parts(window), hot[...])

    def span(slot):
        return slice(slot * CELLS, (slot + 1) * CELLS)

    def gather(slots):
        total = None
        for slot in slots:
            chosen = (parts[:16, span(slot)] + parts[16:, span(slot)]) * picked[:, span(slot)]
            total = chosen if total is None else total + chosen
        return total[:8] + total[8:]

    def scatter(values):
        pieces = [picked[:, span(slot)] * values[slot // 4] for slot in range(SLOTS)]
        spread = split_parts(jnp.concatenate(pieces, axis=1))
        total = lax.dot_general(
            spread, hot[...], (((1,), (1,)), ((), ())), preferred_element_type=F32
        )
        total = total[:16] + total[16:]
        back_near[...] = total[:8]
        back_far[...] = total[8:]

    @pl.when(is_air())
    def _():
        aloft = columns[:80, 3:4]
        lifted = jnp.sum(gather(range(SLOTS)), axis=0, keepdims=True)
        rounded = (y[:, :CELLS] + aloft * lifted).astype(BF16)
        image[...] = rounded
        surface = jnp.sum(aloft * rounded.astype(F32), axis=0, keepdims=True)
        scatter([surface, surface])

    @pl.when(is_sea())
    def _():
        forcing_weight = columns[:40, 4:6]
        fields = (lax.broadcasted_iota(jnp.int32, (16, CELLS), 0) & 4) == 0
        halves = []
        pulled = []
        for half in range(2):
            folded = gather(range(4 * half, 4 * half + 4))
            forcing = [jnp.sum(folded[4 * f : 4 * f + 4], axis=0, keepdims=True) for f in range(2)]
            added = forcing_weight[:, :1] * forcing[0] + forcing_weight[:, 1:] * forcing[1]
            fine = mask[half : half + 1, :] * (y[:40, span(half)] + added)
            rounded = fine.astype(BF16).astype(F32)
            halves.append(rounded)
            first, other = [
                jnp.sum(forcing_weight[:, f : f + 1] * rounded, axis=0, keepdims=True) for f in range(2)
            ]
            pulled.append(jnp.where(fields, first, other))
        image[...] = jnp.concatenate(halves, axis=0).astype(BF16)
        scatter(pulled)


def cotangent_kernel(image, near, far, columns, after, cotangent, edge):
    @pl.when(is_air())
    def _():
        arrived = near[...] + far[...]
        total = image[...].astype(F32)
        for f in range(2):
            row = jnp.concatenate([arrived[f * 4 + q : f * 4 + q + 1, :] for q in range(4)], axis=1)
            total = total + columns[:80, 1 + f : 2 + f] * row
        cotangent[...] = total.astype(BF16)

    @pl.when(is_sea())
    def _():
        cotangent[...] = image[...]

    edge[...] = own_edges(cotangent, 1)


def spread_rows(target, rows):
    line = lax.broadcasted_iota(jnp.int32, (160, 160), 0)
    place = lane_iota((160, 160))
    order = jnp.where(place == (line & 1) * 80 + (line >> 1), 1.0, 0.0).astype(BF16)
    stacked = jnp.concatenate(rows, axis=0).astype(BF16)
    target[0] = dot(order, stacked).astype(BF16).reshape(80, ROWS, COLS)


def unpack_kernel(packed, image):
    wide = packed[...].astype(F32)
    spread_rows(image, [wide[:, r * COLS : (r + 1) * COLS] for r in range(ROWS)])


def adjoint_main_kernel(
    own, above, below, edges, bwd1, bwd2, slope, inner, sides, stack, hidden
):
    def run(channels, width, depth, count):
        padded = depth // 3
        for pair in range(0, count, 2):
            pieces = []
            for a in range(3):
                pieces.append(stack[:padded, (pair + a) * COLS : (pair + a + 2) * COLS])
            back = dot(bwd1[:width, :depth], jnp.concatenate(pieces, axis=0))
            span = slice(pair * COLS, (pair + 2) * COLS)
            back = back * slope[:width, span].astype(F32) * kept(2, count, pair)
            hidden[:width, span] = back.astype(BF16)
        for row, result in enumerate(inner_rows(bwd2, hidden, channels, width, count - 2)):
            inner[:channels, row * COLS : (row + 1) * COLS] = result

    def store(field, place, rows):
        stack[: rows.shape[0], place * COLS : (place + 1) * COLS] = rows

    @pl.when(is_air())
    def _():
        own_sides(edges, sides, False)
        air_rows(own, above, below, 1, store)
        run(80, 512, 720, 4)

    @pl.when(is_sea())
    def _():
        own_sides(edges, sides, True)
        sea_rows(own, above, below, 1, store)
        run(40, 256, 384, 6)


def adjoint_edge_kernel(
    sides, from_left, from_right, inner, slope, bwd1, bwd2, near, far, product
):
    def run(channels, width, depth, count):
        stack = edge_stack(sides, from_left, from_right, channels == 40)
        edge = halved_dot(bwd1[:width, :depth], stack)
        edge = edge * slope[:width, :].astype(F32)
        edge = jnp.where(edge_kept(count) > 0.0, edge, 0.0)
        rows = outer_rows(bwd2, edge, channels, width, count - 2)
        return [
            inner[:channels, i * COLS : (i + 1) * COLS] + row for i, row in enumerate(rows)
        ]

    @pl.when(is_air())
    def _():
        spread_rows(product, run(80, 512, 720, 4))

    @pl.when(is_sea())
    def _():
        results = run(40, 256, 384, 6)
        arrived = near[...] + far[...]
        channel = lax.broadcasted_iota(jnp.int32, (40, COLS), 0)
        rows = []
        for r in range(ROWS):
            halves = []
            for half in range(2):
                fine = 2 * half + r
                row = jnp.concatenate(
                    [arrived[2 * fine + q : 2 * fine + q + 1, :] for q in range(2)], axis=1
                )
                halves.append(results[fine] + jnp.where(channel == 0, row, 0.0))
            rows.append(jnp.concatenate(halves, axis=0))
        spread_rows(product, rows)


def call(kernel, out_shape, inputs, scratch=(), limit=8, stay=()):
    vmem = pl.BlockSpec(memory_space=pltpu.VMEM)
    hbm = pl.BlockSpec(memory_space=pltpu.HBM)
    inputs = [
        pltpu.with_memory_space_constraint(x, pltpu.HBM) if i in stay else x
        for i, x in enumerate(inputs)
    ]
    return pl.pallas_call(
        kernel,
        out_shape=tuple(jax.ShapeDtypeStruct(shape, dtype) for shape, dtype in out_shape),
        in_specs=[hbm if i in stay else vmem for i in range(len(inputs))],
        out_specs=tuple(vmem for _ in out_shape),
        scratch_shapes=list(scratch),
        compiler_params=pltpu.CompilerParams(vmem_limit_bytes=limit << 20),
    )(*inputs)


def lat_pair(block):
    count = lax.axis_size("lat")
    above = lax.ppermute(block, "lat", [(i, (i + 1) % count) for i in range(count)])
    below = lax.ppermute(block, "lat", [((i + 1) % count, i) for i in range(count)])
    return above, below


def lon_pair(block):
    count = lax.axis_size("lon")
    from_left = lax.ppermute(block, "lon", [(i, (i + 1) % count) for i in range(count)])
    from_right = lax.ppermute(block, "lon", [((i + 1) % count, i) for i in range(count)])
    return from_left, from_right


def across(near, far, shift):
    count = lax.axis_size("lon")
    same = lax.ppermute(near, "comp", [(0, 1), (1, 0)])
    route = []
    for part in range(2):
        for i in range(count):
            route.append((part * count + i, (1 - part) * count + (i + shift) % count))
    return same, lax.ppermute(far, ("comp", "lon"), route)


def shards(
    state,
    direction,
    air_first,
    air_bias,
    air_second,
    air_flux,
    aloft_reaction_to_seawarmth,
    sea_first,
    sea_bias,
    sea_second,
    sea_forcing,
    regrid_index,
    regrid_weight,
    land_mask,
):
    def held(arrays):
        buffers = [pltpu.VMEM(array.shape, array.dtype) for array in arrays]
        return buffers + [pltpu.SemaphoreType.DMA((len(arrays),))]

    block = ((80, 128), BF16)
    own, edge = call(
        pack_kernel,
        [((160, CELLS), BF16), block],
        [state, direction],
        [pltpu.VMEM((2, 80, ROWS, COLS), BF16), pltpu.SemaphoreType.DMA((2,))],
        stay=range(2),
    )
    edge_above, edge_below = lat_pair(edge)
    above, below = lat_pair(own)
    first_a = air_first.transpose(0, 2, 1)
    first_o = sea_first.transpose(0, 2, 1)
    raw = [
        first_a,
        air_second,
        first_o,
        sea_second,
        air_bias.reshape(1, 512),
        sea_bias.reshape(1, 256),
        air_flux,
        aloft_reaction_to_seawarmth.reshape(1, 80),
        sea_forcing.T,
    ]
    fwd1, fwd2, columns = call(
        forward_kernel,
        [((512, 720), BF16), ((240, 1536), BF16), ((512, 8), F32)],
        raw + [edge],
        held(raw),
        limit=16,
        stay=range(len(raw)),
    )
    (edges,) = call(edge_kernel, [block], [edge, edge_above, edge_below, columns])
    from_left, from_right = lon_pair(edges)
    inner, slope, sides = call(
        tangent_main_kernel,
        [((80, 2 * CELLS), F32), ((512, 6 * COLS), BF16), ((2, 80, 128), F32)],
        [own, above, below, edges, fwd1, fwd2, columns],
        [pltpu.VMEM((240, 16 * COLS), BF16), pltpu.VMEM((512, 6 * COLS), BF16)],
        limit=16,
    )
    y, edge_slope, payload = call(
        tangent_edge_kernel,
        [((80, 2 * CELLS), F32), ((512, 128), BF16), ((8, 128), F32)],
        [own, sides, from_left, from_right, inner, fwd1, fwd2, columns],
        limit=16,
    )
    near, far = across(payload, payload, -1)
    raw = [air_second, first_a, sea_second, first_o, regrid_index, regrid_weight, land_mask]
    bwd1, bwd2, hot, picked, mask = call(
        backward_kernel,
        [
            ((512, 720), BF16), ((240, 1536), BF16), ((128, SLOTS * CELLS), BF16),
            ((16, SLOTS * CELLS), F32), ((2, CELLS), F32),
        ],
        raw + [payload],
        held(raw),
        limit=16,
        stay=range(len(raw)),
    )
    image, back_near, back_far = call(
        couple_kernel,
        [((80, CELLS), BF16), ((8, 128), F32), ((8, 128), F32)],
        [y, near, far, hot, picked, mask, columns],
    )
    back_near, back_far = across(back_near, back_far, 1)
    (result,) = call(unpack_kernel, [((1, 80, ROWS, COLS), BF16)], [image])
    cotangent, edge = call(
        cotangent_kernel,
        [((80, CELLS), BF16), block],
        [image, back_near, back_far, columns, result],
        stay=(4,),
    )
    edge_above, edge_below = lat_pair(edge)
    above, below = lat_pair(cotangent)
    (edges,) = call(edge_kernel, [block], [edge, edge_above, edge_below, columns])
    from_left, from_right = lon_pair(edges)
    inner, sides = call(
        adjoint_main_kernel,
        [((80, 2 * CELLS), F32), ((2, 80, 128), F32)],
        [cotangent, above, below, edges, bwd1, bwd2, slope],
        [pltpu.VMEM((240, 8 * COLS), BF16), pltpu.VMEM((512, 6 * COLS), BF16)],
        limit=16,
    )
    (product,) = call(
        adjoint_edge_kernel,
        [((1, 80, ROWS, COLS), BF16)],
        [sides, from_left, from_right, inner, edge_slope, bwd1, bwd2, back_near, back_far],
        limit=16,
    )
    return result, product


def solution(mesh):
    return jax.shard_map(
        shards,
        mesh=mesh,
        in_specs=(
            P("comp", None, "lat", "lon"),
            P("comp", None, "lat", "lon"),
            P(),
            P(),
            P(),
            P(),
            P(),
            P(),
            P(),
            P(),
            P(),
            P("comp", None, "lat", "lon"),
            P("comp", None, "lat", "lon"),
            P(None, "lat", "lon"),
        ),
        out_specs=(P("comp", None, "lat", "lon"), P("comp", None, "lat", "lon")),
        check_vma=False,
    )
```

```python
import jax
import jax.numpy as jnp
from jax import lax
from jax.experimental import pallas as pl
from jax.experimental.pallas import tpu as pltpu
from jax.sharding import PartitionSpec as P


F32 = jnp.float32
BF16 = jnp.bfloat16
ROWS = 2
COLS = 256
CELLS = ROWS * COLS
SLOTS = 8


def is_air():
    return lax.axis_index("comp") == 0


def is_sea():
    return lax.axis_index("comp") != 0


def at_top():
    return lax.axis_index("lat") == 0


def at_bottom():
    return lax.axis_index("lat") == lax.axis_size("lat") - 1


def lane_iota(shape):
    return lax.broadcasted_iota(jnp.int32, shape, 1)


def split_parts(values):
    high = values.astype(BF16)
    low = (values - high.astype(F32)).astype(BF16)
    return jnp.concatenate([high, low], axis=0)


def dot(left, right):
    return lax.dot_general(left, right, (((1,), (0,)), ((), ())), preferred_element_type=F32)


def sources(own, above, below):
    upper = jnp.where(at_top(), 0.0, 1.0).astype(F32)
    lower = jnp.where(at_bottom(), 0.0, 1.0).astype(F32)
    chosen = []
    for ref, scale in ((above, upper), (own, None), (below, lower)):
        for r in range(ROWS):

            def read(part, start, stop, ref=ref, scale=scale, r=r):
                rows = ref[part, r * COLS + start : r * COLS + stop].astype(F32)
                return rows if scale is None else rows * scale

            chosen.append((read, r))
    return chosen


def pack_kernel(state, direction, packed, edge, rows, sems):
    copies = []
    for field, ref in enumerate((state, direction)):
        copies.append(pltpu.make_async_copy(ref.at[0], rows.at[field], sems.at[field]))
        copies[-1].start()
    line = lax.broadcasted_iota(jnp.int32, (160, 160), 0)
    place = lane_iota((160, 160))
    source = jnp.where(line < 80, 2 * line, 2 * line - 159)
    order = jnp.where(place == source, 1.0, 0.0).astype(BF16)
    for field, copy in enumerate(copies):
        copy.wait()
        block = dot(order, rows[field].reshape(160, COLS)).astype(BF16)
        for r in range(ROWS):
            packed[field * 80 : field * 80 + 80, r * COLS : (r + 1) * COLS] = block[r * 80 : (r + 1) * 80]
    edge[...] = own_edges(packed, 2)


def load_all(copies):
    for copy in copies[4:]:
        copy.start()

    @pl.when(is_air())
    def _():
        for copy in copies[:2]:
            copy.start()

    @pl.when(is_sea())
    def _():
        for copy in copies[2:4]:
            copy.start()

    for copy in copies[4:]:
        copy.wait()


def make_weights(to, back, flip, to_target, back_target):
    channels = to.shape[1]
    padded = -(-3 * channels // 16) * 16
    hidden = to.shape[2]
    pieces = []
    for a in range(3):
        for e in range(3):
            tap = 3 * a + e
            pieces.append(to[8 - tap if flip else tap].astype(F32))
        if padded > 3 * channels:
            pieces.append(jnp.zeros((padded - 3 * channels, hidden), F32))
    stacked = jnp.concatenate(pieces, axis=0)
    to_target[:hidden, : 3 * padded] = stacked.T.astype(BF16)
    for a in range(3):
        pieces = []
        for e in range(3):
            tap = 3 * a + e
            pieces.append(back[8 - tap if flip else tap].astype(F32))
        stacked = jnp.concatenate(pieces, axis=0)
        back_target[: 3 * channels, a * hidden : (a + 1) * hidden] = stacked.astype(BF16)


def both_weights(copies, held, flip, to_target, back_target):
    @pl.when(is_air())
    def _():
        for copy in copies[:2]:
            copy.wait()
        make_weights(held[0], held[1], flip, to_target, back_target)

    @pl.when(is_sea())
    def _():
        for copy in copies[2:4]:
            copy.wait()
        make_weights(held[2], held[3], flip, to_target, back_target)


def copies_of(sources, held, sems):
    return [
        pltpu.make_async_copy(source, target, sems.at[i])
        for i, (source, target) in enumerate(zip(sources, held))
    ]


def forward_kernel(*refs):
    fwd1, fwd2, columns = refs[10:13]
    held = refs[13:22]
    copies = copies_of(refs[:9], held, refs[22])
    load_all(copies)
    bias_a, bias_o, flux, aloft, forcing = held[4:]
    pad = jnp.zeros((1, 512 - 80), F32)
    bias = jnp.where(is_air(), bias_a[...], jnp.concatenate([bias_o[...]] * 2, axis=1))
    rows = [bias] + [jnp.concatenate([flux[f : f + 1, :].astype(F32), pad], axis=1) for f in range(2)]
    rows.append(jnp.concatenate([aloft[...], pad], axis=1))
    pad = jnp.zeros((1, 512 - 40), F32)
    rows += [jnp.concatenate([forcing[f : f + 1, :].astype(F32), pad], axis=1) for f in range(2)]
    rows.append(jnp.zeros((2, 512), F32))
    columns[...] = jnp.concatenate(rows, axis=0).T
    both_weights(copies, held, False, fwd1, fwd2)


def backward_kernel(*refs):
    bwd1, bwd2, hot, picked, mask = refs[8:13]
    held = refs[13:20]
    copies = copies_of(refs[:7], held, refs[20])
    load_all(copies)
    index, weight, land = held[4:]

    def flat(rows):
        return jnp.concatenate([rows[r : r + 1] for r in range(ROWS)], axis=1)

    table = jnp.concatenate([flat(weight[0, s]) for s in range(SLOTS)], axis=0).astype(F32)
    place = jnp.concatenate([flat(index[0, s]) for s in range(SLOTS)], axis=0)
    line = ((place >> 8) & 1) * 8 + (place >> 9) * 2 + ((place >> 7) & 1)
    rows16 = lax.broadcasted_iota(jnp.int32, (16, CELLS), 0)
    mask[...] = jnp.concatenate([flat(land[s]) for s in range(2)], axis=0).astype(F32)
    whole = jnp.sum(table, axis=0, keepdims=True)
    upper = jnp.sum(table[:4], axis=0, keepdims=True)
    slot_row = lax.broadcasted_iota(jnp.int32, table.shape, 0)
    grouped = jnp.where(slot_row < 4, upper, whole - upper)
    share = table / jnp.where(is_air(), whole, grouped)
    folded = jnp.where(is_air(), rows16, rows16 & 11)
    lanes = lax.broadcasted_iota(jnp.int32, (128, CELLS), 0)
    for slot in range(SLOTS):
        span = slice(slot * CELLS, (slot + 1) * CELLS)
        picked[:, span] = jnp.where(folded == line[slot : slot + 1], share[slot : slot + 1], 0.0)
        low = place[slot : slot + 1, :] & 127
        hot[:, span] = jnp.where(lanes == low, 1.0, 0.0).astype(BF16)
    both_weights(copies, held, True, bwd1, bwd2)


def own_edges(rows, fields):
    lanes = lane_iota((80, 128)) >> 1
    result = jnp.zeros((80, 128), F32)
    for field in range(fields):
        part = slice(field * 80, (field + 1) * 80)
        for r in range(ROWS):
            shift = 64 * field + 4 * (ROWS + r) + 2
            initial = rows[part, r * COLS : r * COLS + 128].astype(F32)
            last = rows[part, r * COLS + 128 : (r + 1) * COLS].astype(F32)
            result = jnp.where(lanes == shift // 2, pltpu.roll(initial, shift, 1), result)
            result = jnp.where(lanes == shift // 2 - 1, pltpu.roll(last, shift, 1), result)
    return result.astype(BF16)


def edge_kernel(own, above, below, after, merged):
    upper = jnp.where(at_top(), 0.0, 1.0).astype(F32)
    lower = jnp.where(at_bottom(), 0.0, 1.0).astype(F32)
    total = own[...].astype(F32) + pltpu.roll(above[...].astype(F32), 120, 1) * upper
    merged[...] = (total + pltpu.roll(below[...].astype(F32), 8, 1) * lower).astype(BF16)


def shifted_rows(main, fill):
    pieces = [pltpu.roll(main, 1, 1), main, pltpu.roll(main, COLS - 1, 1)]
    if fill:
        pieces.append(jnp.zeros((fill, COLS), F32))
    return jnp.concatenate(pieces, axis=0).astype(BF16)


def air_rows(own, above, below, fields, store):
    for field in range(fields):
        part = slice(field * 80, (field + 1) * 80)
        for place, (read, r) in enumerate(sources(own, above, below)):
            store(field, place, shifted_rows(read(part, 0, COLS), 0))


def sea_rows(own, above, below, fields, store):
    for field in range(fields):
        part = slice(field * 80, (field + 1) * 80)
        for place, (read, r) in enumerate(sources(own, above, below)):
            main = read(part, 0, COLS)
            for half in range(2):
                fine = 2 * (2 * (place // 2) + half - 1) + r
                if 0 <= fine < 8:
                    store(field, fine, shifted_rows(main[half * 40 : half * 40 + 40], 8))


def kept(rows, count, first_row):
    lanes = lane_iota((1, rows * COLS))
    row = first_row + lanes // COLS
    column = lanes % COLS
    drop = (column == 0) | (column == COLS - 1)
    drop = drop | (at_top() & (row == 0)) | (at_bottom() & (row == count - 1))
    return jnp.where(drop, 0.0, 1.0).astype(F32)


def edge_kept(count):
    lanes = lane_iota((1, 128))
    row = lanes >> 2
    drop = (row >= count) | (at_top() & (row == 0)) | (at_bottom() & (row == count - 1))
    return jnp.where(drop, 0.0, 1.0).astype(F32)


def fine_lanes(rows):
    lanes = (lane_iota((40, 128)) & 63) >> 3
    upper, lower = rows[:40], rows[40:]
    result = jnp.where(lanes == 0, lower, upper)
    result = jnp.where(lanes == 2, pltpu.roll(lower, 8, 1), result)
    return jnp.where(lanes == 3, pltpu.roll(upper, 8, 1), result)


def own_sides(edges, sides, fine):
    rows = edges[...].astype(F32)
    for i, shift in enumerate((2, 126)):
        side = pltpu.roll(rows, shift, 1)
        if fine:
            sides[i, :40, :] = fine_lanes(side)
        else:
            sides[i] = side


def edge_stack(sides, near, far, fine):
    both = []
    even = lax.axis_index("lon") % 2 == 0
    near, far = near[...].astype(F32), far[...].astype(F32)
    from_left = jnp.where(even, far, near)
    from_right = jnp.where(even, near, far)
    for i, rows in enumerate((from_left, from_right)):
        rows = fine_lanes(rows) if fine else rows
        side = sides[i, :40, :] if fine else sides[i]
        head = (lane_iota(rows.shape) & 3) < 2
        both.append(jnp.where(head, rows, side) if i == 0 else jnp.where(head, side, rows))
    before, after = both
    even = (lane_iota(before.shape) & 1) == 0
    middle = jnp.where(even, pltpu.roll(before, 127, 1), pltpu.roll(after, 1, 1))
    pieces = []
    for a in range(3):
        for rows in (before, middle, after):
            pieces.append(pltpu.roll(rows, 128 - 4 * a, 1) if a else rows)
        if fine:
            pieces.append(jnp.zeros((8, 128), F32))
    return jnp.concatenate(pieces, axis=0).astype(BF16)


def halved_dot(matrix, taps):
    half = matrix.shape[0] // 16 * 8
    return jnp.concatenate([dot(matrix[:half], taps), dot(matrix[half:], taps)], axis=0)


def inner_rows(weights, main, channels, width, count):
    matrix = weights[: 3 * channels, : 3 * width]
    result = []
    for pair in range(0, count, 2):
        pieces = [main[:width, (pair + a) * COLS : (pair + a + 2) * COLS] for a in range(3)]
        whole = dot(matrix, jnp.concatenate(pieces, axis=0))
        for row in range(2):
            cut = whole[:, row * COLS : (row + 1) * COLS]
            total = pltpu.roll(cut[:channels], 1, 1) + cut[channels : 2 * channels]
            result.append(total + pltpu.roll(cut[2 * channels :], COLS - 1, 1))
    return result


def outer_rows(weights, edge, channels, width, count):
    taps = edge.astype(BF16)
    block = dot(weights[: 3 * channels, :width], taps)
    for a in (1, 2):
        part = dot(weights[: 3 * channels, a * width : (a + 1) * width], taps)
        block = block + pltpu.roll(part, 128 - 4 * a, 1)
    first, middle, last = [block[e * channels : (e + 1) * channels] for e in range(3)]
    lanes = lane_iota((channels, 128))
    left = first + jnp.where((lanes & 3) == 0, pltpu.roll(middle, 127, 1), 0.0)
    right = last + jnp.where((lanes & 3) == 3, pltpu.roll(middle, 1, 1), 0.0)
    result = []
    for row in range(count):
        head = pltpu.roll(left, 128 - 4 * row, 1) if row else left
        head = jnp.where(lanes < 2, head, 0.0)
        tail = jnp.where(lanes >= 126, pltpu.roll(right, 124 - 4 * row, 1), 0.0)
        result.append(jnp.concatenate([head, tail], axis=1))
    return result


def tangent_main_kernel(
    own, above, below, edges, fwd1, fwd2, columns, inner, slope, sides, stack, hidden
):
    def run(channels, width, depth, count):
        padded = depth // 3
        for place in range(count):
            pieces = []
            for a in range(3):
                start = (place + a) * 2 * COLS
                pieces.append(stack[:padded, start : start + 2 * COLS])
            both = dot(fwd1[:width, :depth], jnp.concatenate(pieces, axis=0))
            steep = 1.0 - jnp.tanh(both[:, :COLS] + columns[:width, 0:1]) ** 2
            span = slice(place * COLS, (place + 1) * COLS)
            hidden[:width, span] = (steep * both[:, COLS:] * kept(1, count, place)).astype(BF16)
            slope[:width, span] = steep.astype(BF16)
        for row, result in enumerate(inner_rows(fwd2, hidden, channels, width, count - 2)):
            inner[:channels, row * COLS : (row + 1) * COLS] = result

    def store(field, place, rows):
        start = place * 2 * COLS + field * COLS
        stack[: rows.shape[0], start : start + COLS] = rows

    @pl.when(is_air())
    def _():
        own_sides(edges, sides, False)
        air_rows(own, above, below, 2, store)
        run(80, 512, 720, 4)

    @pl.when(is_sea())
    def _():
        own_sides(edges, sides, True)
        sea_rows(own, above, below, 2, store)
        run(40, 256, 384, 6)


def tangent_edge_kernel(
    own, sides, from_left, from_right, inner, fwd1, fwd2, columns,
    y, slope, payload,
):
    def run(channels, width, depth, count):
        stack = edge_stack(sides, from_left, from_right, channels == 40)
        both = halved_dot(fwd1[:width, :depth], stack)
        steep = 1.0 - jnp.tanh(both + columns[:width, 0:1]) ** 2
        slope[:width, :] = steep.astype(BF16)
        edge = steep * pltpu.roll(both, 64, 1) * edge_kept(count)
        rows = outer_rows(fwd2, edge, channels, width, count - 2)
        return [
            inner[:channels, i * COLS : (i + 1) * COLS] + row for i, row in enumerate(rows)
        ]

    @pl.when(is_air())
    def _():
        for r, result in enumerate(run(80, 512, 720, 4)):
            y[:, r * COLS : (r + 1) * COLS] = result
            for f in range(2):
                flux = jnp.sum(columns[:80, 1 + f : 2 + f] * result, axis=0, keepdims=True)
                for part in range(2):
                    line = f * 4 + r * 2 + part
                    payload[line : line + 1, :] = flux[:, part * 128 : (part + 1) * 128]

    @pl.when(is_sea())
    def _():
        for fine, result in enumerate(run(40, 256, 384, 6)):
            y[:40, fine * COLS : (fine + 1) * COLS] = result
            half, r = divmod(fine, 2)
            line = own[80 + 40 * half : 88 + 40 * half, r * COLS : (r + 1) * COLS].astype(F32)
            for part in range(2):
                place = fine * 2 + part
                payload[place : place + 1, :] = line[:1, part * 128 : (part + 1) * 128]


def couple_kernel(y, near, far, hot, picked, mask, columns, image, back_near, back_far):
    window = jnp.concatenate([near[...], far[...]], axis=0)
    parts = dot(split_parts(window), hot[...])

    def span(slot):
        return slice(slot * CELLS, (slot + 1) * CELLS)

    def gather(slots):
        total = None
        for slot in slots:
            chosen = (parts[:16, span(slot)] + parts[16:, span(slot)]) * picked[:, span(slot)]
            total = chosen if total is None else total + chosen
        return total[:8] + total[8:]

    def scatter(values):
        pieces = [picked[:, span(slot)] * values[slot // 4] for slot in range(SLOTS)]
        spread = split_parts(jnp.concatenate(pieces, axis=1))
        total = lax.dot_general(
            spread, hot[...], (((1,), (1,)), ((), ())), preferred_element_type=F32
        )
        total = total[:16] + total[16:]
        back_near[...] = total[:8]
        back_far[...] = total[8:]

    @pl.when(is_air())
    def _():
        aloft = columns[:80, 3:4]
        lifted = jnp.sum(gather(range(SLOTS)), axis=0, keepdims=True)
        rounded = (y[:, :CELLS] + aloft * lifted).astype(BF16)
        image[...] = rounded
        surface = jnp.sum(aloft * rounded.astype(F32), axis=0, keepdims=True)
        scatter([surface, surface])

    @pl.when(is_sea())
    def _():
        forcing_weight = columns[:40, 4:6]
        fields = (lax.broadcasted_iota(jnp.int32, (16, CELLS), 0) & 4) == 0
        halves = []
        pulled = []
        for half in range(2):
            folded = gather(range(4 * half, 4 * half + 4))
            forcing = [jnp.sum(folded[4 * f : 4 * f + 4], axis=0, keepdims=True) for f in range(2)]
            added = forcing_weight[:, :1] * forcing[0] + forcing_weight[:, 1:] * forcing[1]
            fine = mask[half : half + 1, :] * (y[:40, span(half)] + added)
            rounded = fine.astype(BF16).astype(F32)
            halves.append(rounded)
            first, other = [
                jnp.sum(forcing_weight[:, f : f + 1] * rounded, axis=0, keepdims=True) for f in range(2)
            ]
            pulled.append(jnp.where(fields, first, other))
        image[...] = jnp.concatenate(halves, axis=0).astype(BF16)
        scatter(pulled)


def cotangent_kernel(image, near, far, columns, after, cotangent, edge):
    @pl.when(is_air())
    def _():
        arrived = near[...] + far[...]
        total = image[...].astype(F32)
        for f in range(2):
            row = jnp.concatenate([arrived[f * 4 + q : f * 4 + q + 1, :] for q in range(4)], axis=1)
            total = total + columns[:80, 1 + f : 2 + f] * row
        cotangent[...] = total.astype(BF16)

    @pl.when(is_sea())
    def _():
        cotangent[...] = image[...]

    edge[...] = own_edges(cotangent, 1)


def spread_rows(target, rows):
    line = lax.broadcasted_iota(jnp.int32, (160, 160), 0)
    place = lane_iota((160, 160))
    order = jnp.where(place == (line & 1) * 80 + (line >> 1), 1.0, 0.0).astype(BF16)
    stacked = jnp.concatenate(rows, axis=0).astype(BF16)
    target[0] = dot(order, stacked).astype(BF16).reshape(80, ROWS, COLS)


def unpack_kernel(packed, image):
    wide = packed[...].astype(F32)
    spread_rows(image, [wide[:, r * COLS : (r + 1) * COLS] for r in range(ROWS)])


def adjoint_main_kernel(
    own, above, below, edges, bwd1, bwd2, slope, inner, sides, stack, hidden
):
    def run(channels, width, depth, count):
        padded = depth // 3
        for pair in range(0, count, 2):
            pieces = []
            for a in range(3):
                pieces.append(stack[:padded, (pair + a) * COLS : (pair + a + 2) * COLS])
            back = dot(bwd1[:width, :depth], jnp.concatenate(pieces, axis=0))
            span = slice(pair * COLS, (pair + 2) * COLS)
            back = back * slope[:width, span].astype(F32) * kept(2, count, pair)
            hidden[:width, span] = back.astype(BF16)
        for row, result in enumerate(inner_rows(bwd2, hidden, channels, width, count - 2)):
            inner[:channels, row * COLS : (row + 1) * COLS] = result

    def store(field, place, rows):
        stack[: rows.shape[0], place * COLS : (place + 1) * COLS] = rows

    @pl.when(is_air())
    def _():
        own_sides(edges, sides, False)
        air_rows(own, above, below, 1, store)
        run(80, 512, 720, 4)

    @pl.when(is_sea())
    def _():
        own_sides(edges, sides, True)
        sea_rows(own, above, below, 1, store)
        run(40, 256, 384, 6)


def adjoint_edge_kernel(
    sides, from_left, from_right, inner, slope, bwd1, bwd2, near, far, product
):
    def run(channels, width, depth, count):
        stack = edge_stack(sides, from_left, from_right, channels == 40)
        edge = halved_dot(bwd1[:width, :depth], stack)
        edge = edge * slope[:width, :].astype(F32)
        edge = jnp.where(edge_kept(count) > 0.0, edge, 0.0)
        rows = outer_rows(bwd2, edge, channels, width, count - 2)
        return [
            inner[:channels, i * COLS : (i + 1) * COLS] + row for i, row in enumerate(rows)
        ]

    @pl.when(is_air())
    def _():
        spread_rows(product, run(80, 512, 720, 4))

    @pl.when(is_sea())
    def _():
        results = run(40, 256, 384, 6)
        arrived = near[...] + far[...]
        channel = lax.broadcasted_iota(jnp.int32, (40, COLS), 0)
        rows = []
        for r in range(ROWS):
            halves = []
            for half in range(2):
                fine = 2 * half + r
                row = jnp.concatenate(
                    [arrived[2 * fine + q : 2 * fine + q + 1, :] for q in range(2)], axis=1
                )
                halves.append(results[fine] + jnp.where(channel == 0, row, 0.0))
            rows.append(jnp.concatenate(halves, axis=0))
        spread_rows(product, rows)


def call(kernel, out_shape, inputs, scratch=(), limit=8, stay=()):
    vmem = pl.BlockSpec(memory_space=pltpu.VMEM)
    hbm = pl.BlockSpec(memory_space=pltpu.HBM)
    inputs = [
        pltpu.with_memory_space_constraint(x, pltpu.HBM) if i in stay else x
        for i, x in enumerate(inputs)
    ]
    return pl.pallas_call(
        kernel,
        out_shape=tuple(jax.ShapeDtypeStruct(shape, dtype) for shape, dtype in out_shape),
        in_specs=[hbm if i in stay else vmem for i in range(len(inputs))],
        out_specs=tuple(vmem for _ in out_shape),
        scratch_shapes=list(scratch),
        compiler_params=pltpu.CompilerParams(vmem_limit_bytes=limit << 20),
    )(*inputs)


def lat_pair(block):
    count = lax.axis_size("lat")
    above = lax.ppermute(block, "lat", [(i, (i + 1) % count) for i in range(count)])
    below = lax.ppermute(block, "lat", [((i + 1) % count, i) for i in range(count)])
    return above, below


def lon_pair(block):
    count = lax.axis_size("lon")
    near = lax.ppermute(block, "lon", [(i, i ^ 1) for i in range(count)])
    route = [(i, (i + (1 if i % 2 else -1)) % count) for i in range(count)]
    far = lax.ppermute(block, "lon", route)
    return near, far


def across(near, far, shift):
    count = lax.axis_size("lon")
    same = lax.ppermute(near, "comp", [(0, 1), (1, 0)])
    route = []
    for part in range(2):
        for i in range(count):
            route.append((part * count + i, (1 - part) * count + (i + shift) % count))
    return same, lax.ppermute(far, ("comp", "lon"), route)


def shards(
    state,
    direction,
    air_first,
    air_bias,
    air_second,
    air_flux,
    aloft_reaction_to_seawarmth,
    sea_first,
    sea_bias,
    sea_second,
    sea_forcing,
    regrid_index,
    regrid_weight,
    land_mask,
):
    def held(arrays):
        buffers = [pltpu.VMEM(array.shape, array.dtype) for array in arrays]
        return buffers + [pltpu.SemaphoreType.DMA((len(arrays),))]

    block = ((80, 128), BF16)
    own, edge = call(
        pack_kernel,
        [((160, CELLS), BF16), block],
        [state, direction],
        [pltpu.VMEM((2, 80, ROWS, COLS), BF16), pltpu.SemaphoreType.DMA((2,))],
        stay=range(2),
    )
    edge_above, edge_below = lat_pair(edge)
    above, below = lat_pair(own)
    first_a = air_first.transpose(0, 2, 1)
    first_o = sea_first.transpose(0, 2, 1)
    raw = [
        first_a,
        air_second,
        first_o,
        sea_second,
        air_bias.reshape(1, 512),
        sea_bias.reshape(1, 256),
        air_flux,
        aloft_reaction_to_seawarmth.reshape(1, 80),
        sea_forcing.T,
    ]
    fwd1, fwd2, columns = call(
        forward_kernel,
        [((512, 720), BF16), ((240, 1536), BF16), ((512, 8), F32)],
        raw + [edge],
        held(raw),
        limit=16,
        stay=range(len(raw)),
    )
    (edges,) = call(edge_kernel, [block], [edge, edge_above, edge_below, columns])
    from_left, from_right = lon_pair(edges)
    inner, slope, sides = call(
        tangent_main_kernel,
        [((80, 2 * CELLS), F32), ((512, 6 * COLS), BF16), ((2, 80, 128), F32)],
        [own, above, below, edges, fwd1, fwd2, columns],
        [pltpu.VMEM((240, 16 * COLS), BF16), pltpu.VMEM((512, 6 * COLS), BF16)],
        limit=16,
    )
    y, edge_slope, payload = call(
        tangent_edge_kernel,
        [((80, 2 * CELLS), F32), ((512, 128), BF16), ((8, 128), F32)],
        [own, sides, from_left, from_right, inner, fwd1, fwd2, columns],
        limit=16,
    )
    near, far = across(payload, payload, -1)
    raw = [air_second, first_a, sea_second, first_o, regrid_index, regrid_weight, land_mask]
    bwd1, bwd2, hot, picked, mask = call(
        backward_kernel,
        [
            ((512, 720), BF16), ((240, 1536), BF16), ((128, SLOTS * CELLS), BF16),
            ((16, SLOTS * CELLS), F32), ((2, CELLS), F32),
        ],
        raw + [payload],
        held(raw),
        limit=16,
        stay=range(len(raw)),
    )
    image, back_near, back_far = call(
        couple_kernel,
        [((80, CELLS), BF16), ((8, 128), F32), ((8, 128), F32)],
        [y, near, far, hot, picked, mask, columns],
    )
    back_near, back_far = across(back_near, back_far, 1)
    (result,) = call(unpack_kernel, [((1, 80, ROWS, COLS), BF16)], [image])
    cotangent, edge = call(
        cotangent_kernel,
        [((80, CELLS), BF16), block],
        [image, back_near, back_far, columns, result],
        stay=(4,),
    )
    edge_above, edge_below = lat_pair(edge)
    above, below = lat_pair(cotangent)
    (edges,) = call(edge_kernel, [block], [edge, edge_above, edge_below, columns])
    from_left, from_right = lon_pair(edges)
    inner, sides = call(
        adjoint_main_kernel,
        [((80, 2 * CELLS), F32), ((2, 80, 128), F32)],
        [cotangent, above, below, edges, bwd1, bwd2, slope],
        [pltpu.VMEM((240, 8 * COLS), BF16), pltpu.VMEM((512, 6 * COLS), BF16)],
        limit=16,
    )
    (product,) = call(
        adjoint_edge_kernel,
        [((1, 80, ROWS, COLS), BF16)],
        [sides, from_left, from_right, inner, edge_slope, bwd1, bwd2, back_near, back_far],
        limit=16,
    )
    return result, product


def solution(mesh):
    return jax.shard_map(
        shards,
        mesh=mesh,
        in_specs=(
            P("comp", None, "lat", "lon"),
            P("comp", None, "lat", "lon"),
            P(),
            P(),
            P(),
            P(),
            P(),
            P(),
            P(),
            P(),
            P(),
            P("comp", None, "lat", "lon"),
            P("comp", None, "lat", "lon"),
            P(None, "lat", "lon"),
        ),
        out_specs=(P("comp", None, "lat", "lon"), P("comp", None, "lat", "lon")),
        check_vma=False,
    )
```

```python
import jax
import jax.numpy as jnp
from jax import lax
from jax.experimental import pallas as pl
from jax.experimental.pallas import tpu as pltpu
from jax.sharding import PartitionSpec as P


F32 = jnp.float32
BF16 = jnp.bfloat16
ROWS = 2
COLS = 256
CELLS = ROWS * COLS
SLOTS = 8


def is_air():
    return lax.axis_index("comp") == 0


def is_sea():
    return lax.axis_index("comp") != 0


def at_top():
    return lax.axis_index("lat") == 0


def at_bottom():
    return lax.axis_index("lat") == lax.axis_size("lat") - 1


def lane_iota(shape):
    return lax.broadcasted_iota(jnp.int32, shape, 1)


def split_parts(values):
    high = values.astype(BF16)
    low = (values - high.astype(F32)).astype(BF16)
    return jnp.concatenate([high, low], axis=0)


def dot(left, right):
    return lax.dot_general(left, right, (((1,), (0,)), ((), ())), preferred_element_type=F32)


def sources(own, above, below):
    upper = jnp.where(at_top(), 0.0, 1.0).astype(F32)
    lower = jnp.where(at_bottom(), 0.0, 1.0).astype(F32)
    chosen = []
    for ref, scale in ((above, upper), (own, None), (below, lower)):
        for r in range(ROWS):

            def read(part, start, stop, ref=ref, scale=scale, r=r):
                rows = ref[part, r * COLS + start : r * COLS + stop].astype(F32)
                return rows if scale is None else rows * scale

            chosen.append((read, r))
    return chosen


def pack_kernel(state, direction, packed, edge, rows, sems):
    copies = []
    for field, ref in enumerate((state, direction)):
        copies.append(pltpu.make_async_copy(ref.at[0], rows.at[field], sems.at[field]))
        copies[-1].start()
    line = lax.broadcasted_iota(jnp.int32, (160, 160), 0)
    place = lane_iota((160, 160))
    source = jnp.where(line < 80, 2 * line, 2 * line - 159)
    order = jnp.where(place == source, 1.0, 0.0).astype(BF16)
    for field, copy in enumerate(copies):
        copy.wait()
        block = dot(order, rows[field].reshape(160, COLS)).astype(BF16)
        for r in range(ROWS):
            packed[field * 80 : field * 80 + 80, r * COLS : (r + 1) * COLS] = block[r * 80 : (r + 1) * 80]
    edge[...] = own_edges(packed, 2)


def load_all(copies):
    for copy in copies[4:]:
        copy.start()

    @pl.when(is_air())
    def _():
        for copy in copies[:2]:
            copy.start()

    @pl.when(is_sea())
    def _():
        for copy in copies[2:4]:
            copy.start()

    for copy in copies[4:]:
        copy.wait()


def make_weights(to, back, flip, to_target, back_target):
    channels = to.shape[1]
    padded = -(-3 * channels // 16) * 16
    hidden = to.shape[2]
    pieces = []
    for a in range(3):
        for e in range(3):
            tap = 3 * a + e
            pieces.append(to[8 - tap if flip else tap].astype(F32))
        if padded > 3 * channels:
            pieces.append(jnp.zeros((padded - 3 * channels, hidden), F32))
    stacked = jnp.concatenate(pieces, axis=0)
    to_target[:hidden, : 3 * padded] = stacked.T.astype(BF16)
    for a in range(3):
        pieces = []
        for e in range(3):
            tap = 3 * a + e
            pieces.append(back[8 - tap if flip else tap].astype(F32))
        stacked = jnp.concatenate(pieces, axis=0)
        back_target[: 3 * channels, a * hidden : (a + 1) * hidden] = stacked.astype(BF16)


def both_weights(copies, held, flip, to_target, back_target):
    @pl.when(is_air())
    def _():
        for copy in copies[:2]:
            copy.wait()
        make_weights(held[0], held[1], flip, to_target, back_target)

    @pl.when(is_sea())
    def _():
        for copy in copies[2:4]:
            copy.wait()
        make_weights(held[2], held[3], flip, to_target, back_target)


def copies_of(sources, held, sems):
    return [
        pltpu.make_async_copy(source, target, sems.at[i])
        for i, (source, target) in enumerate(zip(sources, held))
    ]


def forward_kernel(*refs):
    fwd1, fwd2, columns = refs[10:13]
    held = refs[13:22]
    copies = copies_of(refs[:9], held, refs[22])
    load_all(copies)
    bias_a, bias_o, flux, aloft, forcing = held[4:]
    pad = jnp.zeros((1, 512 - 80), F32)
    bias = jnp.where(is_air(), bias_a[...], jnp.concatenate([bias_o[...]] * 2, axis=1))
    rows = [bias] + [jnp.concatenate([flux[f : f + 1, :].astype(F32), pad], axis=1) for f in range(2)]
    rows.append(jnp.concatenate([aloft[...], pad], axis=1))
    pad = jnp.zeros((1, 512 - 40), F32)
    rows += [jnp.concatenate([forcing[f : f + 1, :].astype(F32), pad], axis=1) for f in range(2)]
    rows.append(jnp.zeros((2, 512), F32))
    columns[...] = jnp.concatenate(rows, axis=0).T
    both_weights(copies, held, False, fwd1, fwd2)


def backward_kernel(*refs):
    bwd1, bwd2, hot, picked, mask = refs[8:13]
    held = refs[13:20]
    copies = copies_of(refs[:7], held, refs[20])
    load_all(copies)
    index, weight, land = held[4:]

    def flat(rows):
        return jnp.concatenate([rows[r : r + 1] for r in range(ROWS)], axis=1)

    table = jnp.concatenate([flat(weight[0, s]) for s in range(SLOTS)], axis=0).astype(F32)
    place = jnp.concatenate([flat(index[0, s]) for s in range(SLOTS)], axis=0)
    line = ((place >> 8) & 1) * 8 + (place >> 9) * 2 + ((place >> 7) & 1)
    rows16 = lax.broadcasted_iota(jnp.int32, (16, CELLS), 0)
    mask[...] = jnp.concatenate([flat(land[s]) for s in range(2)], axis=0).astype(F32)
    whole = jnp.sum(table, axis=0, keepdims=True)
    upper = jnp.sum(table[:4], axis=0, keepdims=True)
    slot_row = lax.broadcasted_iota(jnp.int32, table.shape, 0)
    grouped = jnp.where(slot_row < 4, upper, whole - upper)
    share = table / jnp.where(is_air(), whole, grouped)
    folded = jnp.where(is_air(), rows16, rows16 & 11)
    lanes = lax.broadcasted_iota(jnp.int32, (128, CELLS), 0)
    for slot in range(SLOTS):
        span = slice(slot * CELLS, (slot + 1) * CELLS)
        picked[:, span] = jnp.where(folded == line[slot : slot + 1], share[slot : slot + 1], 0.0)
        low = place[slot : slot + 1, :] & 127
        hot[:, span] = jnp.where(lanes == low, 1.0, 0.0).astype(BF16)
    both_weights(copies, held, True, bwd1, bwd2)


def own_edges(rows, fields):
    lanes = lane_iota((80, 128)) >> 1
    result = jnp.zeros((80, 128), F32)
    for field in range(fields):
        part = slice(field * 80, (field + 1) * 80)
        for r in range(ROWS):
            shift = 64 * field + 4 * (ROWS + r) + 2
            initial = rows[part, r * COLS : r * COLS + 128].astype(F32)
            last = rows[part, r * COLS + 128 : (r + 1) * COLS].astype(F32)
            result = jnp.where(lanes == shift // 2, pltpu.roll(initial, shift, 1), result)
            result = jnp.where(lanes == shift // 2 - 1, pltpu.roll(last, shift, 1), result)
    return result.astype(BF16)


def edge_kernel(own, above, below, after, merged):
    upper = jnp.where(at_top(), 0.0, 1.0).astype(F32)
    lower = jnp.where(at_bottom(), 0.0, 1.0).astype(F32)
    total = own[...].astype(F32) + pltpu.roll(above[...].astype(F32), 120, 1) * upper
    merged[...] = (total + pltpu.roll(below[...].astype(F32), 8, 1) * lower).astype(BF16)


def bulk_edge_kernel(own, above, below, merged):
    upper = jnp.where(at_top(), 0.0, 1.0).astype(F32)
    lower = jnp.where(at_bottom(), 0.0, 1.0).astype(F32)
    sides = [own_edges(ref, 1).astype(F32) for ref in (own, above, below)]
    total = sides[0] + pltpu.roll(sides[1], 120, 1) * upper
    merged[...] = (total + pltpu.roll(sides[2], 8, 1) * lower).astype(BF16)


def shifted_rows(main, fill):
    pieces = [pltpu.roll(main, 1, 1), main, pltpu.roll(main, COLS - 1, 1)]
    if fill:
        pieces.append(jnp.zeros((fill, COLS), F32))
    return jnp.concatenate(pieces, axis=0).astype(BF16)


def air_rows(own, above, below, fields, store):
    for field in range(fields):
        part = slice(field * 80, (field + 1) * 80)
        for place, (read, r) in enumerate(sources(own, above, below)):
            store(field, place, shifted_rows(read(part, 0, COLS), 0))


def sea_rows(own, above, below, fields, store):
    for field in range(fields):
        part = slice(field * 80, (field + 1) * 80)
        for place, (read, r) in enumerate(sources(own, above, below)):
            main = read(part, 0, COLS)
            for half in range(2):
                fine = 2 * (2 * (place // 2) + half - 1) + r
                if 0 <= fine < 8:
                    store(field, fine, shifted_rows(main[half * 40 : half * 40 + 40], 8))


def kept(rows, count, first_row):
    lanes = lane_iota((1, rows * COLS))
    row = first_row + lanes // COLS
    column = lanes % COLS
    drop = (column == 0) | (column == COLS - 1)
    drop = drop | (at_top() & (row == 0)) | (at_bottom() & (row == count - 1))
    return jnp.where(drop, 0.0, 1.0).astype(F32)


def edge_kept(count):
    lanes = lane_iota((1, 128))
    row = lanes >> 2
    drop = (row >= count) | (at_top() & (row == 0)) | (at_bottom() & (row == count - 1))
    return jnp.where(drop, 0.0, 1.0).astype(F32)


def fine_lanes(rows):
    lanes = (lane_iota((40, 128)) & 63) >> 3
    upper, lower = rows[:40], rows[40:]
    result = jnp.where(lanes == 0, lower, upper)
    result = jnp.where(lanes == 2, pltpu.roll(lower, 8, 1), result)
    return jnp.where(lanes == 3, pltpu.roll(upper, 8, 1), result)


def own_sides(edges, sides, fine):
    rows = edges[...].astype(F32)
    for i, shift in enumerate((2, 126)):
        side = pltpu.roll(rows, shift, 1)
        if fine:
            sides[i, :40, :] = fine_lanes(side)
        else:
            sides[i] = side


def edge_stack(sides, from_left, from_right, fine):
    both = []
    for i, ref in enumerate((from_left, from_right)):
        rows = ref[...].astype(F32)
        rows = fine_lanes(rows) if fine else rows
        side = sides[i, :40, :] if fine else sides[i]
        head = (lane_iota(rows.shape) & 3) < 2
        both.append(jnp.where(head, rows, side) if i == 0 else jnp.where(head, side, rows))
    before, after = both
    even = (lane_iota(before.shape) & 1) == 0
    middle = jnp.where(even, pltpu.roll(before, 127, 1), pltpu.roll(after, 1, 1))
    pieces = []
    for a in range(3):
        for rows in (before, middle, after):
            pieces.append(pltpu.roll(rows, 128 - 4 * a, 1) if a else rows)
        if fine:
            pieces.append(jnp.zeros((8, 128), F32))
    return jnp.concatenate(pieces, axis=0).astype(BF16)


def halved_dot(matrix, taps):
    half = matrix.shape[0] // 16 * 8
    return jnp.concatenate([dot(matrix[:half], taps), dot(matrix[half:], taps)], axis=0)


def inner_rows(weights, main, channels, width, count):
    matrix = weights[: 3 * channels, : 3 * width]
    result = []
    for pair in range(0, count, 2):
        pieces = [main[:width, (pair + a) * COLS : (pair + a + 2) * COLS] for a in range(3)]
        whole = dot(matrix, jnp.concatenate(pieces, axis=0))
        for row in range(2):
            cut = whole[:, row * COLS : (row + 1) * COLS]
            total = pltpu.roll(cut[:channels], 1, 1) + cut[channels : 2 * channels]
            result.append(total + pltpu.roll(cut[2 * channels :], COLS - 1, 1))
    return result


def outer_rows(weights, edge, channels, width, count):
    taps = edge.astype(BF16)
    block = dot(weights[: 3 * channels, :width], taps)
    for a in (1, 2):
        part = dot(weights[: 3 * channels, a * width : (a + 1) * width], taps)
        block = block + pltpu.roll(part, 128 - 4 * a, 1)
    first, middle, last = [block[e * channels : (e + 1) * channels] for e in range(3)]
    lanes = lane_iota((channels, 128))
    left = first + jnp.where((lanes & 3) == 0, pltpu.roll(middle, 127, 1), 0.0)
    right = last + jnp.where((lanes & 3) == 3, pltpu.roll(middle, 1, 1), 0.0)
    result = []
    for row in range(count):
        head = pltpu.roll(left, 128 - 4 * row, 1) if row else left
        head = jnp.where(lanes < 2, head, 0.0)
        tail = jnp.where(lanes >= 126, pltpu.roll(right, 124 - 4 * row, 1), 0.0)
        result.append(jnp.concatenate([head, tail], axis=1))
    return result


def tangent_main_kernel(
    own, above, below, edges, fwd1, fwd2, columns, inner, slope, sides, stack, hidden
):
    def run(channels, width, depth, count):
        padded = depth // 3
        for place in range(count):
            pieces = []
            for a in range(3):
                start = (place + a) * 2 * COLS
                pieces.append(stack[:padded, start : start + 2 * COLS])
            both = dot(fwd1[:width, :depth], jnp.concatenate(pieces, axis=0))
            steep = 1.0 - jnp.tanh(both[:, :COLS] + columns[:width, 0:1]) ** 2
            span = slice(place * COLS, (place + 1) * COLS)
            hidden[:width, span] = (steep * both[:, COLS:] * kept(1, count, place)).astype(BF16)
            slope[:width, span] = steep.astype(BF16)
        for row, result in enumerate(inner_rows(fwd2, hidden, channels, width, count - 2)):
            inner[:channels, row * COLS : (row + 1) * COLS] = result

    def store(field, place, rows):
        start = place * 2 * COLS + field * COLS
        stack[: rows.shape[0], start : start + COLS] = rows

    @pl.when(is_air())
    def _():
        own_sides(edges, sides, False)
        air_rows(own, above, below, 2, store)
        run(80, 512, 720, 4)

    @pl.when(is_sea())
    def _():
        own_sides(edges, sides, True)
        sea_rows(own, above, below, 2, store)
        run(40, 256, 384, 6)


def tangent_edge_kernel(
    own, sides, from_left, from_right, inner, fwd1, fwd2, columns,
    y, slope, payload,
):
    def run(channels, width, depth, count):
        stack = edge_stack(sides, from_left, from_right, channels == 40)
        both = halved_dot(fwd1[:width, :depth], stack)
        steep = 1.0 - jnp.tanh(both + columns[:width, 0:1]) ** 2
        slope[:width, :] = steep.astype(BF16)
        edge = steep * pltpu.roll(both, 64, 1) * edge_kept(count)
        rows = outer_rows(fwd2, edge, channels, width, count - 2)
        return [
            inner[:channels, i * COLS : (i + 1) * COLS] + row for i, row in enumerate(rows)
        ]

    @pl.when(is_air())
    def _():
        for r, result in enumerate(run(80, 512, 720, 4)):
            y[:, r * COLS : (r + 1) * COLS] = result
            for f in range(2):
                flux = jnp.sum(columns[:80, 1 + f : 2 + f] * result, axis=0, keepdims=True)
                for part in range(2):
                    line = f * 4 + r * 2 + part
                    payload[line : line + 1, :] = flux[:, part * 128 : (part + 1) * 128]

    @pl.when(is_sea())
    def _():
        for fine, result in enumerate(run(40, 256, 384, 6)):
            y[:40, fine * COLS : (fine + 1) * COLS] = result
            half, r = divmod(fine, 2)
            line = own[80 + 40 * half : 88 + 40 * half, r * COLS : (r + 1) * COLS].astype(F32)
            for part in range(2):
                place = fine * 2 + part
                payload[place : place + 1, :] = line[:1, part * 128 : (part + 1) * 128]


def couple_kernel(y, near, far, hot, picked, mask, columns, image, back_near, back_far):
    window = jnp.concatenate([near[...], far[...]], axis=0)
    parts = dot(split_parts(window), hot[...])

    def span(slot):
        return slice(slot * CELLS, (slot + 1) * CELLS)

    def gather(slots):
        total = None
        for slot in slots:
            chosen = (parts[:16, span(slot)] + parts[16:, span(slot)]) * picked[:, span(slot)]
            total = chosen if total is None else total + chosen
        return total[:8] + total[8:]

    def scatter(values):
        pieces = [picked[:, span(slot)] * values[slot // 4] for slot in range(SLOTS)]
        spread = split_parts(jnp.concatenate(pieces, axis=1))
        total = lax.dot_general(
            spread, hot[...], (((1,), (1,)), ((), ())), preferred_element_type=F32
        )
        total = total[:16] + total[16:]
        back_near[...] = total[:8]
        back_far[...] = total[8:]

    @pl.when(is_air())
    def _():
        aloft = columns[:80, 3:4]
        lifted = jnp.sum(gather(range(SLOTS)), axis=0, keepdims=True)
        rounded = (y[:, :CELLS] + aloft * lifted).astype(BF16)
        image[...] = rounded
        surface = jnp.sum(aloft * rounded.astype(F32), axis=0, keepdims=True)
        scatter([surface, surface])

    @pl.when(is_sea())
    def _():
        forcing_weight = columns[:40, 4:6]
        fields = (lax.broadcasted_iota(jnp.int32, (16, CELLS), 0) & 4) == 0
        halves = []
        pulled = []
        for half in range(2):
            folded = gather(range(4 * half, 4 * half + 4))
            forcing = [jnp.sum(folded[4 * f : 4 * f + 4], axis=0, keepdims=True) for f in range(2)]
            added = forcing_weight[:, :1] * forcing[0] + forcing_weight[:, 1:] * forcing[1]
            fine = mask[half : half + 1, :] * (y[:40, span(half)] + added)
            rounded = fine.astype(BF16).astype(F32)
            halves.append(rounded)
            first, other = [
                jnp.sum(forcing_weight[:, f : f + 1] * rounded, axis=0, keepdims=True) for f in range(2)
            ]
            pulled.append(jnp.where(fields, first, other))
        image[...] = jnp.concatenate(halves, axis=0).astype(BF16)
        scatter(pulled)


def cotangent_kernel(image, near, far, columns, after, cotangent):
    @pl.when(is_air())
    def _():
        arrived = near[...] + far[...]
        total = image[...].astype(F32)
        for f in range(2):
            row = jnp.concatenate([arrived[f * 4 + q : f * 4 + q + 1, :] for q in range(4)], axis=1)
            total = total + columns[:80, 1 + f : 2 + f] * row
        cotangent[...] = total.astype(BF16)

    @pl.when(is_sea())
    def _():
        cotangent[...] = image[...]


def spread_rows(target, rows):
    line = lax.broadcasted_iota(jnp.int32, (160, 160), 0)
    place = lane_iota((160, 160))
    order = jnp.where(place == (line & 1) * 80 + (line >> 1), 1.0, 0.0).astype(BF16)
    stacked = jnp.concatenate(rows, axis=0).astype(BF16)
    target[0] = dot(order, stacked).astype(BF16).reshape(80, ROWS, COLS)


def unpack_kernel(packed, image):
    wide = packed[...].astype(F32)
    spread_rows(image, [wide[:, r * COLS : (r + 1) * COLS] for r in range(ROWS)])


def adjoint_main_kernel(
    own, above, below, edges, bwd1, bwd2, slope, inner, sides, stack, hidden
):
    def run(channels, width, depth, count):
        padded = depth // 3
        for pair in range(0, count, 2):
            pieces = []
            for a in range(3):
                pieces.append(stack[:padded, (pair + a) * COLS : (pair + a + 2) * COLS])
            back = dot(bwd1[:width, :depth], jnp.concatenate(pieces, axis=0))
            span = slice(pair * COLS, (pair + 2) * COLS)
            back = back * slope[:width, span].astype(F32) * kept(2, count, pair)
            hidden[:width, span] = back.astype(BF16)
        for row, result in enumerate(inner_rows(bwd2, hidden, channels, width, count - 2)):
            inner[:channels, row * COLS : (row + 1) * COLS] = result

    def store(field, place, rows):
        stack[: rows.shape[0], place * COLS : (place + 1) * COLS] = rows

    @pl.when(is_air())
    def _():
        own_sides(edges, sides, False)
        air_rows(own, above, below, 1, store)
        run(80, 512, 720, 4)

    @pl.when(is_sea())
    def _():
        own_sides(edges, sides, True)
        sea_rows(own, above, below, 1, store)
        run(40, 256, 384, 6)


def adjoint_edge_kernel(
    sides, from_left, from_right, inner, slope, bwd1, bwd2, near, far, product
):
    def run(channels, width, depth, count):
        stack = edge_stack(sides, from_left, from_right, channels == 40)
        edge = halved_dot(bwd1[:width, :depth], stack)
        edge = edge * slope[:width, :].astype(F32)
        edge = jnp.where(edge_kept(count) > 0.0, edge, 0.0)
        rows = outer_rows(bwd2, edge, channels, width, count - 2)
        return [
            inner[:channels, i * COLS : (i + 1) * COLS] + row for i, row in enumerate(rows)
        ]

    @pl.when(is_air())
    def _():
        spread_rows(product, run(80, 512, 720, 4))

    @pl.when(is_sea())
    def _():
        results = run(40, 256, 384, 6)
        arrived = near[...] + far[...]
        channel = lax.broadcasted_iota(jnp.int32, (40, COLS), 0)
        rows = []
        for r in range(ROWS):
            halves = []
            for half in range(2):
                fine = 2 * half + r
                row = jnp.concatenate(
                    [arrived[2 * fine + q : 2 * fine + q + 1, :] for q in range(2)], axis=1
                )
                halves.append(results[fine] + jnp.where(channel == 0, row, 0.0))
            rows.append(jnp.concatenate(halves, axis=0))
        spread_rows(product, rows)


def call(kernel, out_shape, inputs, scratch=(), limit=8, stay=()):
    vmem = pl.BlockSpec(memory_space=pltpu.VMEM)
    hbm = pl.BlockSpec(memory_space=pltpu.HBM)
    inputs = [
        pltpu.with_memory_space_constraint(x, pltpu.HBM) if i in stay else x
        for i, x in enumerate(inputs)
    ]
    return pl.pallas_call(
        kernel,
        out_shape=tuple(jax.ShapeDtypeStruct(shape, dtype) for shape, dtype in out_shape),
        in_specs=[hbm if i in stay else vmem for i in range(len(inputs))],
        out_specs=tuple(vmem for _ in out_shape),
        scratch_shapes=list(scratch),
        compiler_params=pltpu.CompilerParams(vmem_limit_bytes=limit << 20),
    )(*inputs)


def lat_pair(block):
    count = lax.axis_size("lat")
    above = lax.ppermute(block, "lat", [(i, (i + 1) % count) for i in range(count)])
    below = lax.ppermute(block, "lat", [((i + 1) % count, i) for i in range(count)])
    return above, below


def lon_pair(block):
    count = lax.axis_size("lon")
    from_left = lax.ppermute(block, "lon", [(i, (i + 1) % count) for i in range(count)])
    from_right = lax.ppermute(block, "lon", [((i + 1) % count, i) for i in range(count)])
    return from_left, from_right


def across(near, far, shift):
    count = lax.axis_size("lon")
    same = lax.ppermute(near, "comp", [(0, 1), (1, 0)])
    route = []
    for part in range(2):
        for i in range(count):
            route.append((part * count + i, (1 - part) * count + (i + shift) % count))
    return same, lax.ppermute(far, ("comp", "lon"), route)


def shards(
    state,
    direction,
    air_first,
    air_bias,
    air_second,
    air_flux,
    aloft_reaction_to_seawarmth,
    sea_first,
    sea_bias,
    sea_second,
    sea_forcing,
    regrid_index,
    regrid_weight,
    land_mask,
):
    def held(arrays):
        buffers = [pltpu.VMEM(array.shape, array.dtype) for array in arrays]
        return buffers + [pltpu.SemaphoreType.DMA((len(arrays),))]

    block = ((80, 128), BF16)
    own, edge = call(
        pack_kernel,
        [((160, CELLS), BF16), block],
        [state, direction],
        [pltpu.VMEM((2, 80, ROWS, COLS), BF16), pltpu.SemaphoreType.DMA((2,))],
        stay=range(2),
    )
    edge_above, edge_below = lat_pair(edge)
    above, below = lat_pair(own)
    first_a = air_first.transpose(0, 2, 1)
    first_o = sea_first.transpose(0, 2, 1)
    raw = [
        first_a,
        air_second,
        first_o,
        sea_second,
        air_bias.reshape(1, 512),
        sea_bias.reshape(1, 256),
        air_flux,
        aloft_reaction_to_seawarmth.reshape(1, 80),
        sea_forcing.T,
    ]
    fwd1, fwd2, columns = call(
        forward_kernel,
        [((512, 720), BF16), ((240, 1536), BF16), ((512, 8), F32)],
        raw + [edge],
        held(raw),
        limit=16,
        stay=range(len(raw)),
    )
    (edges,) = call(edge_kernel, [block], [edge, edge_above, edge_below, columns])
    from_left, from_right = lon_pair(edges)
    inner, slope, sides = call(
        tangent_main_kernel,
        [((80, 2 * CELLS), F32), ((512, 6 * COLS), BF16), ((2, 80, 128), F32)],
        [own, above, below, edges, fwd1, fwd2, columns],
        [pltpu.VMEM((240, 16 * COLS), BF16), pltpu.VMEM((512, 6 * COLS), BF16)],
        limit=16,
    )
    y, edge_slope, payload = call(
        tangent_edge_kernel,
        [((80, 2 * CELLS), F32), ((512, 128), BF16), ((8, 128), F32)],
        [own, sides, from_left, from_right, inner, fwd1, fwd2, columns],
        limit=16,
    )
    near, far = across(payload, payload, -1)
    raw = [air_second, first_a, sea_second, first_o, regrid_index, regrid_weight, land_mask]
    bwd1, bwd2, hot, picked, mask = call(
        backward_kernel,
        [
            ((512, 720), BF16), ((240, 1536), BF16), ((128, SLOTS * CELLS), BF16),
            ((16, SLOTS * CELLS), F32), ((2, CELLS), F32),
        ],
        raw + [payload],
        held(raw),
        limit=16,
        stay=range(len(raw)),
    )
    image, back_near, back_far = call(
        couple_kernel,
        [((80, CELLS), BF16), ((8, 128), F32), ((8, 128), F32)],
        [y, near, far, hot, picked, mask, columns],
    )
    back_near, back_far = across(back_near, back_far, 1)
    (result,) = call(unpack_kernel, [((1, 80, ROWS, COLS), BF16)], [image])
    (cotangent,) = call(
        cotangent_kernel,
        [((80, CELLS), BF16)],
        [image, back_near, back_far, columns, result],
        stay=(4,),
    )
    above, below = lat_pair(cotangent)
    (edges,) = call(bulk_edge_kernel, [block], [cotangent, above, below])
    from_left, from_right = lon_pair(edges)
    inner, sides = call(
        adjoint_main_kernel,
        [((80, 2 * CELLS), F32), ((2, 80, 128), F32)],
        [cotangent, above, below, edges, bwd1, bwd2, slope],
        [pltpu.VMEM((240, 8 * COLS), BF16), pltpu.VMEM((512, 6 * COLS), BF16)],
        limit=16,
    )
    (product,) = call(
        adjoint_edge_kernel,
        [((1, 80, ROWS, COLS), BF16)],
        [sides, from_left, from_right, inner, edge_slope, bwd1, bwd2, back_near, back_far],
        limit=16,
    )
    return result, product


def solution(mesh):
    return jax.shard_map(
        shards,
        mesh=mesh,
        in_specs=(
            P("comp", None, "lat", "lon"),
            P("comp", None, "lat", "lon"),
            P(),
            P(),
            P(),
            P(),
            P(),
            P(),
            P(),
            P(),
            P(),
            P("comp", None, "lat", "lon"),
            P("comp", None, "lat", "lon"),
            P(None, "lat", "lon"),
        ),
        out_specs=(P("comp", None, "lat", "lon"), P("comp", None, "lat", "lon")),
        check_vma=False,
    )
```

```python
import jax
import jax.numpy as jnp
from jax import lax
from jax.experimental import pallas as pl
from jax.experimental.pallas import tpu as pltpu
from jax.sharding import PartitionSpec as P


F32 = jnp.float32
BF16 = jnp.bfloat16
ROWS = 2
COLS = 256
CELLS = ROWS * COLS
SLOTS = 8


def is_air():
    return lax.axis_index("comp") == 0


def is_sea():
    return lax.axis_index("comp") != 0


def at_top():
    return lax.axis_index("lat") == 0


def at_bottom():
    return lax.axis_index("lat") == lax.axis_size("lat") - 1


def lane_iota(shape):
    return lax.broadcasted_iota(jnp.int32, shape, 1)


def split_parts(values):
    high = values.astype(BF16)
    low = (values - high.astype(F32)).astype(BF16)
    return jnp.concatenate([high, low], axis=0)


def dot(left, right):
    return lax.dot_general(left, right, (((1,), (0,)), ((), ())), preferred_element_type=F32)


def sources(own, above, below):
    upper = jnp.where(at_top(), 0.0, 1.0).astype(F32)
    lower = jnp.where(at_bottom(), 0.0, 1.0).astype(F32)
    chosen = []
    for ref, scale in ((above, upper), (own, None), (below, lower)):
        for r in range(ROWS):

            def read(part, start, stop, ref=ref, scale=scale, r=r):
                rows = ref[part, r * COLS + start : r * COLS + stop].astype(F32)
                return rows if scale is None else rows * scale

            chosen.append((read, r))
    return chosen


def pack_kernel(state, direction, packed, rows, sems):
    copies = []
    for field, ref in enumerate((state, direction)):
        copies.append(pltpu.make_async_copy(ref.at[0], rows.at[field], sems.at[field]))
        copies[-1].start()
    line = lax.broadcasted_iota(jnp.int32, (160, 160), 0)
    place = lane_iota((160, 160))
    source = jnp.where(line < 80, 2 * line, 2 * line - 159)
    order = jnp.where(place == source, 1.0, 0.0).astype(BF16)
    for field, copy in enumerate(copies):
        copy.wait()
        block = dot(order, rows[field].reshape(160, COLS)).astype(BF16)
        for r in range(ROWS):
            packed[field * 80 : field * 80 + 80, r * COLS : (r + 1) * COLS] = block[r * 80 : (r + 1) * 80]


def prepare_kernel(*refs):
    sources = refs[:12]
    fwd1, fwd2, bwd1, bwd2, hot, picked, mask, columns = refs[12:20]
    held = refs[20:32]
    sems = refs[32]
    copies = [
        pltpu.make_async_copy(source, target, sems.at[i])
        for i, (source, target) in enumerate(zip(sources, held))
    ]
    first_a, second_a, first_o, second_o, index, weight, land, bias_a, bias_o, flux, aloft, forcing = held
    for copy in copies[4:]:
        copy.start()

    @pl.when(is_air())
    def _():
        for copy in copies[:2]:
            copy.start()

    @pl.when(is_sea())
    def _():
        for copy in copies[2:4]:
            copy.start()

    for copy in copies[4:]:
        copy.wait()

    def flat(rows):
        return jnp.concatenate([rows[r : r + 1] for r in range(ROWS)], axis=1)

    def weights(first, second, channels):
        padded = -(-3 * channels // 16) * 16
        hidden = first.shape[2]
        fill = jnp.zeros((padded - 3 * channels, hidden), F32)

        def to_hidden(source, flip, target):
            pieces = []
            for a in range(3):
                for e in range(3):
                    tap = 3 * a + e
                    pieces.append(source[8 - tap if flip else tap].astype(F32))
                if padded > 3 * channels:
                    pieces.append(fill)
            stacked = jnp.concatenate(pieces, axis=0)
            target[:hidden, : 3 * padded] = stacked.T.astype(BF16)

        def from_hidden(source, flip, target):
            for a in range(3):
                pieces = []
                for e in range(3):
                    tap = 3 * a + e
                    pieces.append(source[8 - tap if flip else tap].astype(F32))
                stacked = jnp.concatenate(pieces, axis=0)
                target[: 3 * channels, a * hidden : (a + 1) * hidden] = stacked.astype(BF16)

        to_hidden(first, False, fwd1)
        from_hidden(second, False, fwd2)
        to_hidden(second, True, bwd1)
        from_hidden(first, True, bwd2)

    table = jnp.concatenate([flat(weight[0, s]) for s in range(SLOTS)], axis=0).astype(F32)
    place = jnp.concatenate([flat(index[0, s]) for s in range(SLOTS)], axis=0)
    line = ((place >> 8) & 1) * 8 + (place >> 9) * 2 + ((place >> 7) & 1)
    rows16 = lax.broadcasted_iota(jnp.int32, (16, CELLS), 0)

    def select(share, folded):
        for slot in range(SLOTS):
            chosen = folded == line[slot : slot + 1]
            part = jnp.where(chosen, share[slot : slot + 1], 0.0)
            picked[:, slot * CELLS : (slot + 1) * CELLS] = part

    mask[...] = jnp.concatenate([flat(land[s]) for s in range(2)], axis=0).astype(F32)
    pad = jnp.zeros((1, 512 - 80), F32)
    bias = jnp.where(is_air(), bias_a[...], jnp.concatenate([bias_o[...]] * 2, axis=1))
    rows = [bias] + [jnp.concatenate([flux[f : f + 1, :].astype(F32), pad], axis=1) for f in range(2)]
    rows.append(jnp.concatenate([aloft[...], pad], axis=1))
    pad = jnp.zeros((1, 512 - 40), F32)
    rows += [jnp.concatenate([forcing[f : f + 1, :].astype(F32), pad], axis=1) for f in range(2)]
    rows.append(jnp.zeros((2, 512), F32))
    columns[...] = jnp.concatenate(rows, axis=0).T

    @pl.when(is_air())
    def _():
        for copy in copies[:2]:
            copy.wait()
        weights(first_a, second_a, first_a.shape[1])
        select(table / jnp.sum(table, axis=0, keepdims=True), rows16)

    @pl.when(is_sea())
    def _():
        for copy in copies[2:4]:
            copy.wait()
        weights(first_o, second_o, first_o.shape[1])
        upper = jnp.sum(table[:4], axis=0, keepdims=True)
        lower = jnp.sum(table[4:], axis=0, keepdims=True)
        slot = lax.broadcasted_iota(jnp.int32, table.shape, 0)
        select(table / jnp.where(slot < 4, upper, lower), rows16 & 11)

    lanes = lax.broadcasted_iota(jnp.int32, (128, CELLS), 0)
    for slot in range(SLOTS):
        low = place[slot : slot + 1, :] & 127
        hot[:, slot * CELLS : (slot + 1) * CELLS] = jnp.where(lanes == low, 1.0, 0.0).astype(BF16)


def edge_kernel(own, above, below, after, to_left, to_right):
    lanes = lane_iota((80, 128)) >> 1
    left = jnp.zeros((80, 128), F32)
    right = jnp.zeros((80, 128), F32)
    for field in range(own.shape[0] // 80):
        part = slice(field * 80, (field + 1) * 80)
        for place, (read, r) in enumerate(sources(own, above, below)):
            shift = 64 * field + 4 * place + 2
            initial = pltpu.roll(read(part, 0, 128), shift, 1)
            last = pltpu.roll(read(part, 128, COLS), shift, 1)
            pair = 32 * field + 2 * place
            left = jnp.where(lanes == pair + 1, initial, left)
            right = jnp.where(lanes == pair, last, right)
    to_left[...] = left.astype(BF16)
    to_right[...] = right.astype(BF16)


def shifted_rows(main, fill):
    pieces = [pltpu.roll(main, 1, 1), main, pltpu.roll(main, COLS - 1, 1)]
    if fill:
        pieces.append(jnp.zeros((fill, COLS), F32))
    return jnp.concatenate(pieces, axis=0).astype(BF16)


def air_rows(own, above, below, fields, store):
    for field in range(fields):
        part = slice(field * 80, (field + 1) * 80)
        for place, (read, r) in enumerate(sources(own, above, below)):
            store(field, place, shifted_rows(read(part, 0, COLS), 0))


def sea_rows(own, above, below, fields, store):
    for field in range(fields):
        part = slice(field * 80, (field + 1) * 80)
        for place, (read, r) in enumerate(sources(own, above, below)):
            main = read(part, 0, COLS)
            for half in range(2):
                fine = 2 * (2 * (place // 2) + half - 1) + r
                if 0 <= fine < 8:
                    store(field, fine, shifted_rows(main[half * 40 : half * 40 + 40], 8))


def kept(rows, count, first_row):
    lanes = lane_iota((1, rows * COLS))
    row = first_row + lanes // COLS
    column = lanes % COLS
    drop = (column == 0) | (column == COLS - 1)
    drop = drop | (at_top() & (row == 0)) | (at_bottom() & (row == count - 1))
    return jnp.where(drop, 0.0, 1.0).astype(F32)


def edge_kept(count):
    lanes = lane_iota((1, 128))
    row = lanes >> 2
    drop = (row >= count) | (at_top() & (row == 0)) | (at_bottom() & (row == count - 1))
    return jnp.where(drop, 0.0, 1.0).astype(F32)


def fine_lanes(rows):
    lanes = (lane_iota((40, 128)) & 63) >> 3
    upper, lower = rows[:40], rows[40:]
    result = jnp.where(lanes == 0, lower, upper)
    result = jnp.where(lanes == 2, pltpu.roll(lower, 8, 1), result)
    return jnp.where(lanes == 3, pltpu.roll(upper, 8, 1), result)


def own_sides(to_left, to_right, sides, fine):
    for i, (ref, shift) in enumerate(((to_right, 2), (to_left, 126))):
        rows = pltpu.roll(ref[...].astype(F32), shift, 1)
        if fine:
            sides[i, :40, :] = fine_lanes(rows)
        else:
            sides[i] = rows


def edge_stack(sides, from_left, from_right, fine):
    both = []
    for i, ref in enumerate((from_left, from_right)):
        rows = ref[...].astype(F32)
        both.append(fine_lanes(rows) + sides[i, :40, :] if fine else rows + sides[i])
    before, after = both
    even = (lane_iota(before.shape) & 1) == 0
    middle = jnp.where(even, pltpu.roll(before, 127, 1), pltpu.roll(after, 1, 1))
    pieces = []
    for a in range(3):
        for rows in (before, middle, after):
            pieces.append(pltpu.roll(rows, 128 - 4 * a, 1) if a else rows)
        if fine:
            pieces.append(jnp.zeros((8, 128), F32))
    return jnp.concatenate(pieces, axis=0).astype(BF16)


def halved_dot(matrix, taps):
    half = matrix.shape[0] // 16 * 8
    return jnp.concatenate([dot(matrix[:half], taps), dot(matrix[half:], taps)], axis=0)


def inner_rows(weights, main, channels, width, count):
    matrix = weights[: 3 * channels, : 3 * width]
    result = []
    for pair in range(0, count, 2):
        pieces = [main[:width, (pair + a) * COLS : (pair + a + 2) * COLS] for a in range(3)]
        whole = dot(matrix, jnp.concatenate(pieces, axis=0))
        for row in range(2):
            cut = whole[:, row * COLS : (row + 1) * COLS]
            total = pltpu.roll(cut[:channels], 1, 1) + cut[channels : 2 * channels]
            result.append(total + pltpu.roll(cut[2 * channels :], COLS - 1, 1))
    return result


def outer_rows(weights, edge, channels, width, count):
    taps = edge.astype(BF16)
    block = dot(weights[: 3 * channels, :width], taps)
    for a in (1, 2):
        part = dot(weights[: 3 * channels, a * width : (a + 1) * width], taps)
        block = block + pltpu.roll(part, 128 - 4 * a, 1)
    first, middle, last = [block[e * channels : (e + 1) * channels] for e in range(3)]
    lanes = lane_iota((channels, 128))
    left = first + jnp.where((lanes & 3) == 0, pltpu.roll(middle, 127, 1), 0.0)
    right = last + jnp.where((lanes & 3) == 3, pltpu.roll(middle, 1, 1), 0.0)
    result = []
    for row in range(count):
        head = pltpu.roll(left, 128 - 4 * row, 1) if row else left
        head = jnp.where(lanes < 2, head, 0.0)
        tail = jnp.where(lanes >= 126, pltpu.roll(right, 124 - 4 * row, 1), 0.0)
        result.append(jnp.concatenate([head, tail], axis=1))
    return result


def tangent_main_kernel(
    own, above, below, to_left, to_right, fwd1, fwd2, columns, inner, slope, sides, stack, hidden
):
    def run(channels, width, depth, count):
        padded = depth // 3
        for place in range(count):
            pieces = []
            for a in range(3):
                start = (place + a) * 2 * COLS
                pieces.append(stack[:padded, start : start + 2 * COLS])
            both = dot(fwd1[:width, :depth], jnp.concatenate(pieces, axis=0))
            steep = 1.0 - jnp.tanh(both[:, :COLS] + columns[:width, 0:1]) ** 2
            span = slice(place * COLS, (place + 1) * COLS)
            hidden[:width, span] = (steep * both[:, COLS:] * kept(1, count, place)).astype(BF16)
            slope[:width, span] = steep.astype(BF16)
        for row, result in enumerate(inner_rows(fwd2, hidden, channels, width, count - 2)):
            inner[:channels, row * COLS : (row + 1) * COLS] = result

    def store(field, place, rows):
        start = place * 2 * COLS + field * COLS
        stack[: rows.shape[0], start : start + COLS] = rows

    @pl.when(is_air())
    def _():
        own_sides(to_left, to_right, sides, False)
        air_rows(own, above, below, 2, store)
        run(80, 512, 720, 4)

    @pl.when(is_sea())
    def _():
        own_sides(to_left, to_right, sides, True)
        sea_rows(own, above, below, 2, store)
        run(40, 256, 384, 6)


def tangent_edge_kernel(
    own, sides, from_left, from_right, inner, fwd1, fwd2, columns,
    y, slope, payload,
):
    def run(channels, width, depth, count):
        stack = edge_stack(sides, from_left, from_right, channels == 40)
        both = halved_dot(fwd1[:width, :depth], stack)
        steep = 1.0 - jnp.tanh(both + columns[:width, 0:1]) ** 2
        slope[:width, :] = steep.astype(BF16)
        edge = steep * pltpu.roll(both, 64, 1) * edge_kept(count)
        rows = outer_rows(fwd2, edge, channels, width, count - 2)
        return [
            inner[:channels, i * COLS : (i + 1) * COLS] + row for i, row in enumerate(rows)
        ]

    @pl.when(is_air())
    def _():
        for r, result in enumerate(run(80, 512, 720, 4)):
            y[:, r * COLS : (r + 1) * COLS] = result
            for f in range(2):
                flux = jnp.sum(columns[:80, 1 + f : 2 + f] * result, axis=0, keepdims=True)
                for part in range(2):
                    line = f * 4 + r * 2 + part
                    payload[line : line + 1, :] = flux[:, part * 128 : (part + 1) * 128]

    @pl.when(is_sea())
    def _():
        for fine, result in enumerate(run(40, 256, 384, 6)):
            y[:40, fine * COLS : (fine + 1) * COLS] = result
            half, r = divmod(fine, 2)
            line = own[80 + 40 * half : 88 + 40 * half, r * COLS : (r + 1) * COLS].astype(F32)
            for part in range(2):
                place = fine * 2 + part
                payload[place : place + 1, :] = line[:1, part * 128 : (part + 1) * 128]


def couple_kernel(y, near, far, hot, picked, mask, columns, image, back_near, back_far):
    window = jnp.concatenate([near[...], far[...]], axis=0)
    parts = dot(split_parts(window), hot[...])

    def span(slot):
        return slice(slot * CELLS, (slot + 1) * CELLS)

    def gather(slots):
        total = None
        for slot in slots:
            chosen = (parts[:16, span(slot)] + parts[16:, span(slot)]) * picked[:, span(slot)]
            total = chosen if total is None else total + chosen
        return total[:8] + total[8:]

    def scatter(values):
        pieces = [picked[:, span(slot)] * values[slot // 4] for slot in range(SLOTS)]
        spread = split_parts(jnp.concatenate(pieces, axis=1))
        total = lax.dot_general(
            spread, hot[...], (((1,), (1,)), ((), ())), preferred_element_type=F32
        )
        total = total[:16] + total[16:]
        back_near[...] = total[:8]
        back_far[...] = total[8:]

    @pl.when(is_air())
    def _():
        aloft = columns[:80, 3:4]
        lifted = jnp.sum(gather(range(SLOTS)), axis=0, keepdims=True)
        rounded = (y[:, :CELLS] + aloft * lifted).astype(BF16)
        image[...] = rounded
        surface = jnp.sum(aloft * rounded.astype(F32), axis=0, keepdims=True)
        scatter([surface, surface])

    @pl.when(is_sea())
    def _():
        forcing_weight = columns[:40, 4:6]
        fields = (lax.broadcasted_iota(jnp.int32, (16, CELLS), 0) & 4) == 0
        halves = []
        pulled = []
        for half in range(2):
            folded = gather(range(4 * half, 4 * half + 4))
            forcing = [jnp.sum(folded[4 * f : 4 * f + 4], axis=0, keepdims=True) for f in range(2)]
            added = forcing_weight[:, :1] * forcing[0] + forcing_weight[:, 1:] * forcing[1]
            fine = mask[half : half + 1, :] * (y[:40, span(half)] + added)
            rounded = fine.astype(BF16).astype(F32)
            halves.append(rounded)
            first, other = [
                jnp.sum(forcing_weight[:, f : f + 1] * rounded, axis=0, keepdims=True) for f in range(2)
            ]
            pulled.append(jnp.where(fields, first, other))
        image[...] = jnp.concatenate(halves, axis=0).astype(BF16)
        scatter(pulled)


def cotangent_kernel(image, near, far, columns, cotangent):
    @pl.when(is_air())
    def _():
        arrived = near[...] + far[...]
        total = image[...].astype(F32)
        for f in range(2):
            row = jnp.concatenate([arrived[f * 4 + q : f * 4 + q + 1, :] for q in range(4)], axis=1)
            total = total + columns[:80, 1 + f : 2 + f] * row
        cotangent[...] = total.astype(BF16)

    @pl.when(is_sea())
    def _():
        cotangent[...] = image[...]


def spread_rows(target, rows):
    line = lax.broadcasted_iota(jnp.int32, (160, 160), 0)
    place = lane_iota((160, 160))
    order = jnp.where(place == (line & 1) * 80 + (line >> 1), 1.0, 0.0).astype(BF16)
    stacked = jnp.concatenate(rows, axis=0).astype(BF16)
    target[0] = dot(order, stacked).astype(BF16).reshape(80, ROWS, COLS)


def unpack_kernel(packed, image):
    wide = packed[...].astype(F32)
    spread_rows(image, [wide[:, r * COLS : (r + 1) * COLS] for r in range(ROWS)])


def adjoint_main_kernel(
    own, above, below, to_left, to_right, bwd1, bwd2, slope, inner, sides, stack, hidden
):
    def run(channels, width, depth, count):
        padded = depth // 3
        for pair in range(0, count, 2):
            pieces = []
            for a in range(3):
                pieces.append(stack[:padded, (pair + a) * COLS : (pair + a + 2) * COLS])
            back = dot(bwd1[:width, :depth], jnp.concatenate(pieces, axis=0))
            span = slice(pair * COLS, (pair + 2) * COLS)
            back = back * slope[:width, span].astype(F32) * kept(2, count, pair)
            hidden[:width, span] = back.astype(BF16)
        for row, result in enumerate(inner_rows(bwd2, hidden, channels, width, count - 2)):
            inner[:channels, row * COLS : (row + 1) * COLS] = result

    def store(field, place, rows):
        stack[: rows.shape[0], place * COLS : (place + 1) * COLS] = rows

    @pl.when(is_air())
    def _():
        own_sides(to_left, to_right, sides, False)
        air_rows(own, above, below, 1, store)
        run(80, 512, 720, 4)

    @pl.when(is_sea())
    def _():
        own_sides(to_left, to_right, sides, True)
        sea_rows(own, above, below, 1, store)
        run(40, 256, 384, 6)


def adjoint_edge_kernel(
    sides, from_left, from_right, inner, slope, bwd1, bwd2, near, far, product
):
    def run(channels, width, depth, count):
        stack = edge_stack(sides, from_left, from_right, channels == 40)
        edge = halved_dot(bwd1[:width, :depth], stack)
        edge = edge * slope[:width, :].astype(F32)
        edge = jnp.where(edge_kept(count) > 0.0, edge, 0.0)
        rows = outer_rows(bwd2, edge, channels, width, count - 2)
        return [
            inner[:channels, i * COLS : (i + 1) * COLS] + row for i, row in enumerate(rows)
        ]

    @pl.when(is_air())
    def _():
        spread_rows(product, run(80, 512, 720, 4))

    @pl.when(is_sea())
    def _():
        results = run(40, 256, 384, 6)
        arrived = near[...] + far[...]
        channel = lax.broadcasted_iota(jnp.int32, (40, COLS), 0)
        rows = []
        for r in range(ROWS):
            halves = []
            for half in range(2):
                fine = 2 * half + r
                row = jnp.concatenate(
                    [arrived[2 * fine + q : 2 * fine + q + 1, :] for q in range(2)], axis=1
                )
                halves.append(results[fine] + jnp.where(channel == 0, row, 0.0))
            rows.append(jnp.concatenate(halves, axis=0))
        spread_rows(product, rows)


def call(kernel, out_shape, inputs, scratch=(), limit=8, loads=False, idle=0):
    vmem = pl.BlockSpec(memory_space=pltpu.VMEM)
    source = vmem
    if loads:
        source = pl.BlockSpec(memory_space=pltpu.HBM)
        inputs = [pltpu.with_memory_space_constraint(array, pltpu.HBM) for array in inputs]
    for i in range(len(inputs) - idle, len(inputs)):
        inputs[i] = pltpu.with_memory_space_constraint(inputs[i], pltpu.HBM)
    return pl.pallas_call(
        kernel,
        out_shape=tuple(jax.ShapeDtypeStruct(shape, dtype) for shape, dtype in out_shape),
        in_specs=[source] * (len(inputs) - idle) + [pl.BlockSpec(memory_space=pltpu.HBM)] * idle,
        out_specs=tuple(vmem for _ in out_shape),
        scratch_shapes=list(scratch),
        compiler_params=pltpu.CompilerParams(vmem_limit_bytes=limit << 20),
    )(*inputs)


def lat_pair(block):
    count = lax.axis_size("lat")
    above = lax.ppermute(block, "lat", [(i, (i + 1) % count) for i in range(count)])
    below = lax.ppermute(block, "lat", [((i + 1) % count, i) for i in range(count)])
    return above, below


def lon_pair(to_left, to_right):
    count = lax.axis_size("lon")
    from_left = lax.ppermute(to_right, "lon", [(i, (i + 1) % count) for i in range(count)])
    from_right = lax.ppermute(to_left, "lon", [((i + 1) % count, i) for i in range(count)])
    return from_left, from_right


def across(near, far, shift):
    count = lax.axis_size("lon")
    route = []
    for part in range(2):
        for i in range(count):
            route.append((part * count + i, (1 - part) * count + (i + shift) % count))
    same = lax.ppermute(near, "comp", [(0, 1), (1, 0)])
    moved = lax.ppermute(far, ("comp", "lon"), route)
    return same, moved


def shards(
    state,
    direction,
    air_first,
    air_bias,
    air_second,
    air_flux,
    aloft_reaction_to_seawarmth,
    sea_first,
    sea_bias,
    sea_second,
    sea_forcing,
    regrid_index,
    regrid_weight,
    land_mask,
):
    (own,) = call(
        pack_kernel,
        [((160, CELLS), BF16)],
        [state, direction],
        [pltpu.VMEM((2, 80, ROWS, COLS), BF16), pltpu.SemaphoreType.DMA((2,))],
        loads=True,
    )
    above, below = lat_pair(own)
    raw = [
        air_first.transpose(0, 2, 1),
        air_second,
        sea_first.transpose(0, 2, 1),
        sea_second,
        regrid_index,
        regrid_weight,
        land_mask,
        air_bias.reshape(1, 512),
        sea_bias.reshape(1, 256),
        air_flux,
        aloft_reaction_to_seawarmth.reshape(1, 80),
        sea_forcing.T,
    ]
    fwd1, fwd2, bwd1, bwd2, hot, picked, mask, columns = call(
        prepare_kernel,
        [
            ((512, 720), BF16), ((240, 1536), BF16), ((512, 720), BF16), ((240, 1536), BF16),
            ((128, SLOTS * CELLS), BF16), ((16, SLOTS * CELLS), F32),
            ((2, CELLS), F32), ((512, 8), F32),
        ],
        raw,
        [pltpu.VMEM(array.shape, array.dtype) for array in raw] + [pltpu.SemaphoreType.DMA((12,))],
        limit=20,
        loads=True,
    )
    to_left, to_right = call(edge_kernel, [((80, 128), BF16)] * 2, [own, above, below, columns])
    from_left, from_right = lon_pair(to_left, to_right)
    inner, slope, sides = call(
        tangent_main_kernel,
        [((80, 2 * CELLS), F32), ((512, 6 * COLS), BF16), ((2, 80, 128), F32)],
        [own, above, below, to_left, to_right, fwd1, fwd2, columns],
        [pltpu.VMEM((240, 16 * COLS), BF16), pltpu.VMEM((512, 6 * COLS), BF16)],
        limit=16,
    )
    y, edge_slope, payload = call(
        tangent_edge_kernel,
        [((80, 2 * CELLS), F32), ((512, 128), BF16), ((8, 128), F32)],
        [own, sides, from_left, from_right, inner, fwd1, fwd2, columns],
        limit=16,
    )
    near, far = across(payload, payload, -1)
    image, back_near, back_far = call(
        couple_kernel,
        [((80, CELLS), BF16), ((8, 128), F32), ((8, 128), F32)],
        [y, near, far, hot, picked, mask, columns],
    )
    back_near, back_far = across(back_near, back_far, 1)
    (result,) = call(unpack_kernel, [((1, 80, ROWS, COLS), BF16)], [image])
    (cotangent,) = call(
        cotangent_kernel, [((80, CELLS), BF16)],
        [image, back_near, back_far, columns],
    )
    above, below = lat_pair(cotangent)
    to_left, to_right = call(
        edge_kernel, [((80, 128), BF16)] * 2,
        [cotangent, above, below, result],
        idle=1,
    )
    from_left, from_right = lon_pair(to_left, to_right)
    inner, sides = call(
        adjoint_main_kernel,
        [((80, 2 * CELLS), F32), ((2, 80, 128), F32)],
        [cotangent, above, below, to_left, to_right, bwd1, bwd2, slope],
        [pltpu.VMEM((240, 8 * COLS), BF16), pltpu.VMEM((512, 6 * COLS), BF16)],
        limit=16,
    )
    (product,) = call(
        adjoint_edge_kernel,
        [((1, 80, ROWS, COLS), BF16)],
        [
            sides, from_left, from_right, inner, edge_slope, bwd1, bwd2,
            back_near, back_far,
        ],
        limit=16,
    )
    return result, product


def solution(mesh):
    return jax.shard_map(
        shards,
        mesh=mesh,
        in_specs=(
            P("comp", None, "lat", "lon"),
            P("comp", None, "lat", "lon"),
            P(),
            P(),
            P(),
            P(),
            P(),
            P(),
            P(),
            P(),
            P(),
            P("comp", None, "lat", "lon"),
            P("comp", None, "lat", "lon"),
            P(None, "lat", "lon"),
        ),
        out_specs=(P("comp", None, "lat", "lon"), P("comp", None, "lat", "lon")),
        check_vma=False,
    )
```
